256 devices in a mesh: ctx: 64 (over y, z, core), tp: 4 (over x).
Axes of the slice: x: 4, y: 4, z: 8, core: 2. Of those that a mesh axis runs over, the one named last changes fastest.
Arguments:
- outer_gate: bfloat16 [8192, 1024], P('ctx', 'tp'), may hold values from -6 to 6
- inner_gate: bfloat16 [8192, 1024], P('ctx', 'tp'), may hold values from -6 to 6
- values: bfloat16 [8192, 1024], P('ctx', 'tp'), may hold values from -6 to 6
- residues: float32 [16, 1024], P(None, 'tp'), may hold values from -4 to 4
- log_decay: float32 [16, 1024], P(None, 'tp'), may hold values from -16 to -2, as said below
- skip_gain: float32 [1024], P('tp'), may hold values from 0.5 to 1.5
- out_weight: bfloat16 [1024, 8192], P('tp'), may hold values from -0.25 to 0.25
- out_grad: bfloat16 [8192, 8192], P('ctx', 'tp'), may hold values from -4 to 4
Outputs:
- mixed: bfloat16 [8192, 8192], P('ctx', 'tp')
- grad_outer: bfloat16 [8192, 1024], P('ctx', 'tp')
- grad_inner: bfloat16 [8192, 1024], P('ctx', 'tp')
- grad_values: bfloat16 [8192, 1024], P('ctx', 'tp')
- grad_weight: float32 [1024, 8192], P('tp', 'ctx')
- grad_skip: float32 [1024], P('tp')
- grad_residues: float32 [16, 1024], P(None, 'tp')
- grad_decay: float32 [16, 1024], P(None, 'tp')
The draws below stay inside these ranges and needn't reach their ends.
Inputs may be any that keep to these rules, and one draw needn't show every extreme that they name: exp(log_decay) is a decay rate per position between 0.3 / 8192 and 0.12.
All inputs are finite; a program needn't handle non-finite values.
Results may differ from the reference program's by a relative error of at most 0.015.
Values may be sent and summed in bfloat16 or wider, within the bound.
No kernel may reach another device: no remote copies, remote signals or barrier semaphores. Data moves between devices by JAX's collectives and lax.ppermute only.
A program may use at most 128 MiB of HBM per device.

```python
import jax
import jax.numpy as jnp
from jax import lax

D = 8192
C = 1024
MODES = 16
LENGTH = 8192


def draw_log_decay(key, part):
    key_slow, key_fast, key_pick = jax.random.split(key, 3)
    tokens_all = 1.0 * LENGTH
    slow_part = jax.random.uniform(key_slow, (MODES, C), jnp.float32, jnp.log(0.3 / tokens_all), jnp.log(2.0 / tokens_all))
    fast_part = jax.random.uniform(key_fast, (MODES, C), jnp.float32, jnp.log(0.04), jnp.log(0.12))
    slow_share = 0.5
    chosen = jax.random.uniform(key_pick, (MODES, C), jnp.float32) < slow_share
    return jnp.where(chosen, slow_part, fast_part)


def with_spikes(drawn, rng, source, target, blocks, factor):
    owner, partner = [(jnp.arange(drawn.shape[position]) // (drawn.shape[position] // blocks)).reshape([-1 if axis == position else 1 for axis in range(drawn.ndim)]) for position in (source, target)]
    chosen = jax.random.permutation(rng, blocks)[partner]
    strong = (owner == chosen) | (owner == (partner + blocks // 2) % blocks)
    return jnp.where(strong, factor * drawn, drawn)


def level_of(key, shape, pieces, smallest, largest):
    gain, own = 1.0, jax.random.fold_in(key, 6)
    for axis_at, shards_of in pieces:
        steps = jnp.exp(jax.random.uniform(jax.random.fold_in(own, axis_at), (shards_of,), jnp.float32, smallest / len(pieces), largest / len(pieces)))
        gain = gain * jnp.repeat(steps, shape[axis_at] // shards_of).reshape([-1 if axis == axis_at else 1 for axis in range(len(shape))])
    return gain


def normal_values(rng, shape, width, most, shards=(), kind=jnp.bfloat16):
    values = jax.random.normal(rng, shape, jnp.float32) * width
    if len(shards) > 0:
        values = level_of(rng, shape, shards, -0.22, 0.18) * values
    return jnp.clip(values, min=-most, max=most).astype(kind)


def gaussian_with(rng, dims, deviation, reach, cuts, heavy, held_as=jnp.bfloat16):
    values = deviation * jax.random.normal(rng, dims, jnp.float32)
    if cuts:
        values = values * level_of(rng, dims, cuts, -0.22, 0.18)
    return jnp.clip(with_spikes(values, jax.random.fold_in(rng, 3), *heavy), -reach, reach).astype(held_as)


def setup_inputs(seed: int = 0) -> dict:
    keys = jax.random.split(jax.random.key(seed), 9)
    outer_gate = normal_values(keys[0], (LENGTH, C), 1.0, 6.0, ((0, 64), (1, 4)))
    inner_gate = normal_values(keys[1], (LENGTH, C), 1.0, 6.0, ((0, 64), (1, 4)))
    values = normal_values(keys[2], (LENGTH, C), 1.0, 6.0, ((0, 64), (1, 4)))
    residues = normal_values(keys[3], (MODES, C), 0.25, 4.0, ((1, 4),), jnp.float32)
    log_decay = draw_log_decay(jax.random.fold_in(keys[8], 71), 0)
    skip_gain = jnp.clip(0.5 + 1.0 * jax.random.uniform(keys[5], (C,), jnp.float32) ** level_of(keys[5], (C,), ((0, 4),), -0.2, 0.2), 0.5, 1.5)
    out_weight = gaussian_with(keys[6], (C, D), C ** -0.5, 0.25, ((0, 4),), (0, 1, 4, 2.0))
    out_grad = gaussian_with(keys[7], (LENGTH, D), 0.25, 4.0, ((0, 64), (1, 4)), (0, 1, 64, 4.0))
    return dict(outer_gate=outer_gate, inner_gate=inner_gate, values=values, residues=residues, log_decay=log_decay, skip_gain=skip_gain, out_weight=out_weight, out_grad=out_grad)


def mode_rows(residue_row, decay_row, offsets):
    rate_row = jnp.exp(decay_row)
    gain_row = residue_row * jnp.sqrt(-jnp.expm1(-2.0 * rate_row))
    return gain_row[None, :] * jnp.exp(-rate_row[None, :] * offsets[:, None])

def impulse(residues, log_decay, offsets):

    def accumulate(summed, mode_pair):
        return (summed + mode_rows(mode_pair[0], mode_pair[1], offsets), None)
    initial = jnp.zeros((offsets.shape[0], residues.shape[1]), residues.dtype)
    summed, _ = lax.scan(accumulate, initial, (residues, log_decay))
    return summed

def impulse_grads(residues, log_decay, offsets, grad_response):

    def one_mode(carry, mode_pair):

        def rows_of(residue_row, decay_row):
            return mode_rows(residue_row, decay_row, offsets)
        _, pullback = jax.vjp(rows_of, mode_pair[0], mode_pair[1])
        grad_res, grad_dec = pullback(grad_response)
        return (carry, (grad_res, grad_dec))
    _, grads = lax.scan(one_mode, 0, (residues, log_decay))
    return grads

def reference(outer_gate, inner_gate, values, residues, log_decay, skip_gain, out_weight, out_grad):
    outer_f = outer_gate.astype(jnp.float32)
    inner_f = inner_gate.astype(jnp.float32)
    value_f = values.astype(jnp.float32)
    mixed_in = inner_f * value_f
    offsets = jnp.arange(LENGTH).astype(residues.dtype)
    response = impulse(residues, log_decay, offsets)
    padded_len = 2 * LENGTH
    spec_u = jnp.fft.rfft(mixed_in, n=padded_len, axis=0)
    spec_h = jnp.fft.rfft(response, n=padded_len, axis=0)
    conv_out = jnp.fft.irfft(spec_u * spec_h, n=padded_len, axis=0)[:LENGTH]
    gated = conv_out + skip_gain[None, :] * mixed_in
    result = (outer_f * gated).astype(jnp.bfloat16)
    mixed = jnp.dot(result, out_weight, preferred_element_type=jnp.float32).astype(jnp.bfloat16)
    grad_gated = jnp.dot(out_grad, out_weight.T, preferred_element_type=jnp.float32)
    grad_weight = jnp.dot(result.T, out_grad, preferred_element_type=jnp.float32)
    grad_conv = grad_gated * outer_f
    grad_outer = (grad_gated * gated).astype(jnp.bfloat16)
    spec_g = jnp.fft.rfft(grad_conv, n=padded_len, axis=0)
    corr_in = jnp.fft.irfft(spec_g * jnp.conj(spec_h), n=padded_len, axis=0)[:LENGTH]
    grad_mixed = corr_in + skip_gain[None, :] * grad_conv
    grad_inner = (grad_mixed * value_f).astype(jnp.bfloat16)
    grad_values = (grad_mixed * inner_f).astype(jnp.bfloat16)
    grad_skip = lax.optimization_barrier(jnp.sum(grad_conv * mixed_in, axis=0))
    grad_response = jnp.fft.irfft(spec_g * jnp.conj(spec_u), n=padded_len, axis=0)[:LENGTH]
    grad_residues, grad_decay = impulse_grads(residues, log_decay, offsets, grad_response)
    return (mixed, grad_outer, grad_inner, grad_values, grad_weight, grad_skip, grad_residues, grad_decay)
```

```python
import math

import jax
import jax.numpy as jnp
import numpy as np
from jax import lax
from jax.sharding import PartitionSpec as P

F32 = jnp.float32
BF16 = jnp.bfloat16
EXACT = lax.Precision.HIGHEST


def dft_tables(block):
    size = 2 * block
    freqs = np.arange(block + 1)
    rows = np.arange(block)
    angles = 2.0 * np.pi * (freqs[:, None] * rows[None, :] % size) / size
    forward = np.concatenate([np.cos(angles), -np.sin(angles)], axis=0)
    weight = np.where((freqs == 0) | (freqs == block), 1.0, 2.0)[:, None] / size
    inverse = np.concatenate([weight * np.cos(angles), -weight * np.sin(angles)], axis=0).T
    return jnp.asarray(forward, F32), jnp.asarray(inverse, F32)


def spectrum(forward, rows):
    both = jnp.dot(forward, rows, precision=EXACT, preferred_element_type=F32)
    half = both.shape[0] // 2
    return both[:half], both[half:]


def back(inverse, real_part, imag_part):
    return jnp.dot(
        inverse, jnp.concatenate([real_part, imag_part], 0), precision=EXACT, preferred_element_type=F32
    )


def body(outer_gate, inner_gate, values, residues, log_decay, skip_gain, out_weight, out_grad):
    ctx = lax.axis_size("ctx")
    tps = lax.axis_size("tp")
    dev = lax.axis_index("ctx")
    tp = lax.axis_index("tp")
    block, chans = outer_gate.shape
    modes = residues.shape[0]
    feats = out_grad.shape[1]
    ny = tps
    nz = ctx // (2 * ny)
    pairs = ctx // 2
    core = dev % 2
    pair = dev // 2
    yy = dev // (2 * nz)
    width = feats // (2 * nz)

    def swap_core(a):
        return lax.ppermute(a, "ctx", [(i, i ^ 1) for i in range(ctx)])

    def shift_tp(a, k):
        return lax.ppermute(a, "tp", [(i, (i + k) % tps) for i in range(tps)])

    def shift_y(a, k):
        per = 2 * nz
        return lax.ppermute(a, "ctx", [(i, (i // per + k) % ny * per + i % per) for i in range(ctx)])

    def of_pairs(a):
        return lax.all_to_all(
            jnp.broadcast_to(a[None], (pairs, *a.shape)),
            "ctx",
            0,
            0,
            tiled=True,
            axis_index_groups=[[2 * i + j for i in range(pairs)] for j in range(2)],
        )

    og = out_grad.reshape(block, nz, 2, width)
    og_mine = lax.dynamic_index_in_dim(og, core, 2, keepdims=False)
    og_other = lax.dynamic_index_in_dim(og, 1 - core, 2, keepdims=False)
    pg0 = jnp.concatenate([og_mine, swap_core(og_other)], 0).reshape(2 * block, nz * width)
    pgs = [pg0] + [shift_tp(pg0, k) for k in range(1, tps)]

    outer_f = outer_gate.astype(F32)
    inner_f = inner_gate.astype(F32)
    value_f = values.astype(F32)
    u = inner_f * value_f
    rate = jnp.exp(log_decay)
    norm = jnp.sqrt(-jnp.expm1(-2.0 * rate))
    gain = residues * norm
    rows = jnp.arange(block, dtype=F32)[None, :, None]
    rate3 = rate[:, None, :]
    fall = jnp.exp(-rate3 * rows)
    rise = jnp.exp(-rate3 * (block - rows))
    fall_block = jnp.exp(-rate * block)

    lead = rise * u[None]
    st = jnp.sum(lead, 1)
    st_lag = jnp.sum(lead * (block - rows), 1)
    mine = jnp.concatenate([st, st_lag], 0)
    theirs = swap_core(mine)
    first = jnp.where(core == 0, mine, theirs)
    second = jnp.where(core == 0, theirs, mine)
    half = chans // 2

    def my_half(a):
        return lax.dynamic_slice_in_dim(a, core * half, half, a.ndim - 1)

    def both_halves(a):
        other = swap_core(a)
        return jnp.concatenate(
            [jnp.where(core == 0, a, other), jnp.where(core == 0, other, a)], a.ndim - 1
        )

    rate_h = my_half(rate)
    decay_h = jnp.exp(-rate_h * block)
    f_h, s_h = my_half(first), my_half(second)
    total = decay_h * f_h[:modes] + s_h[:modes]
    total_lag = decay_h * (block * f_h[:modes] + f_h[modes:]) + s_h[modes:]
    gathered = of_pairs(jnp.concatenate([total, total_lag], 0).astype(BF16)).astype(F32)
    place = jnp.arange(pairs, dtype=jnp.int32)
    gap = (2 * block) * jnp.maximum(pair - 1 - place, 0).astype(F32)[:, None, None]
    weight = jnp.where(
        (place < pair)[:, None, None], jnp.exp(-rate_h[None] * gap), 0.0
    )
    in_h = jnp.sum(weight * gathered[:, :modes], 0)
    in_lag_h = jnp.sum(weight * (gap * gathered[:, :modes] + gathered[:, modes:]), 0)
    incoming = both_halves(jnp.concatenate([in_h, in_lag_h], 0))
    in_pair, in_pair_lag = incoming[:modes], incoming[modes:]
    x_in = jnp.where(core == 0, in_pair, fall_block * in_pair + first[:modes])
    x_lag = jnp.where(
        core == 0, in_pair_lag, fall_block * (in_pair_lag + block * in_pair) + first[modes:]
    )

    forward, inverse = dft_tables(block)
    response = jnp.sum(gain[:, None, :] * fall, 0)
    h_re, h_im = spectrum(forward, response)
    u_re, u_im = spectrum(forward, u)
    conv_local = back(inverse, h_re * u_re - h_im * u_im, h_re * u_im + h_im * u_re)
    conv_out = conv_local + jnp.sum((gain * x_in)[:, None, :] * fall, 0)
    gated = conv_out + skip_gain[None, :] * u
    result = (outer_f * gated).astype(BF16)

    result_pair = jnp.concatenate([result, swap_core(result)], 0)
    parts = [
        lax.dot_general(result_pair, pg, (((0,), (0,)), ((), ())), preferred_element_type=F32)
        .astype(BF16)
        .reshape(chans, nz, width)
        .swapaxes(0, 1)
        for pg in pgs
    ]
    parts = jnp.stack(parts, 0)

    def part_for(s):
        return lax.dynamic_index_in_dim(parts, (tp - yy - s) % tps, 0, keepdims=False)

    over_y = [part_for(0)] + [shift_y(part_for(s), s) for s in range(1, ny)]
    summed_y = sum(a.astype(F32) for a in over_y).astype(BF16)

    w_blocks = out_weight.reshape(chans, tps, feats)

    def projected(k):
        w_block = lax.dynamic_index_in_dim(w_blocks, (tp + k) % tps, 1, keepdims=False)
        return jnp.dot(result, w_block, preferred_element_type=F32)

    mixed = projected(0)
    for k in range(1, tps):
        mixed = mixed + shift_tp(projected(k).astype(BF16), k).astype(F32)
    mixed = mixed.astype(BF16)

    w_half = lax.dynamic_index_in_dim(
        out_weight.reshape(chans, tps, nz, 2, width), core, 3, keepdims=False
    ).reshape(chans, tps, nz * width)
    grad_pair = 0.0
    for k in range(tps):
        w_block = lax.dynamic_index_in_dim(w_half, (tp - k) % tps, 1, keepdims=False)
        grad_pair = grad_pair + lax.dot_general(
            pgs[k], w_block, (((1,), (1,)), ((), ())), preferred_element_type=F32
        )
    grad_gated = grad_pair[:block] + swap_core(grad_pair[block:])
    gc = grad_gated * outer_f
    grad_outer = (grad_gated * gated).astype(BF16)

    g_re, g_im = spectrum(forward, gc)
    corr_local = back(inverse, h_re * g_re + h_im * g_im, h_re * g_im - h_im * g_re)
    lags = back(inverse, u_re * g_re + u_im * g_im, u_re * g_im - u_im * g_re)
    fg = fall * gc[None]
    g_st = jnp.sum(fg, 1)
    g_lag = jnp.sum(fg * rows, 1)
    fl = fall * lags[None]
    sum_a = g_st * x_in + jnp.sum(fl, 1)
    sum_b = g_lag * x_in + g_st * x_lag + jnp.sum(fl * rows, 1)
    sum_skip = jnp.sum(gc * u, 0, keepdims=True)
    mine_g = jnp.concatenate([g_st, sum_a, sum_b, sum_skip], 0)
    theirs_g = swap_core(mine_g)
    later = jnp.where(core == 0, theirs_g[:modes], mine_g[:modes])
    mine_h, theirs_h = my_half(mine_g), my_half(theirs_g)
    early_h = jnp.where(core == 0, mine_h[:modes], theirs_h[:modes])
    total_g = early_h + decay_h * my_half(later)
    sent = jnp.concatenate([total_g, mine_h[modes:] + theirs_h[modes:]], 0)
    got = of_pairs(sent.astype(BF16)).astype(F32)
    gap_g = (2 * block) * jnp.maximum(place - pair - 1, 0).astype(F32)[:, None, None]
    weight_g = jnp.where((place > pair)[:, None, None], jnp.exp(-rate_h[None] * gap_g), 0.0)
    h_half = jnp.sum(weight_g * got[:, :modes], 0)
    sums_half = jnp.sum(got[:, modes:], 0)
    final = both_halves(jnp.concatenate([h_half, sums_half], 0))
    h_pair = final[:modes]
    h_in = jnp.where(core == 0, later + fall_block * h_pair, h_pair)
    tot_a, tot_b = final[modes : 2 * modes], final[2 * modes : 3 * modes]
    grad_skip = final[3 * modes]
    grad_residues = norm * tot_a
    grad_decay = rate * residues * (jnp.exp(-2.0 * rate) / norm * tot_a - norm * tot_b)
    corr_in = corr_local + jnp.sum((gain * h_in)[:, None, :] * rise, 0)
    grad_mixed = corr_in + skip_gain[None, :] * gc
    grad_inner = (grad_mixed * value_f).astype(BF16)
    grad_values = (grad_mixed * inner_f).astype(BF16)

    over_z = lax.all_to_all(
        summed_y,
        "ctx",
        0,
        0,
        tiled=True,
        axis_index_groups=[
            [i * 2 * nz + j * 2 + k for j in range(nz)] for i in range(ny) for k in range(2)
        ],
    )
    grad_weight = jnp.sum(over_z.astype(F32), 0)
    return (
        mixed,
        grad_outer,
        grad_inner,
        grad_values,
        grad_weight,
        grad_skip,
        grad_residues,
        grad_decay,
    )


def solution(mesh):
    placed = (
        P("ctx", "tp"),
        P("ctx", "tp"),
        P("ctx", "tp"),
        P(None, "tp"),
        P(None, "tp"),
        P("tp"),
        P("tp", None),
        P("ctx", "tp"),
    )
    return jax.shard_map(
        body,
        mesh=mesh,
        in_specs=placed,
        out_specs=(
            P("ctx", "tp"),
            P("ctx", "tp"),
            P("ctx", "tp"),
            P("ctx", "tp"),
            P("tp", "ctx"),
            P("tp"),
            P(None, "tp"),
            P(None, "tp"),
        ),
        check_vma=False,
    )
```

```python
import jax
import jax.numpy as jnp
import numpy as np
from jax import lax
from jax.sharding import PartitionSpec as P

F32 = jnp.float32
BF16 = jnp.bfloat16
EXACT = lax.Precision.HIGHEST


def dft_tables(block):
    size = 2 * block
    freqs = np.arange(block + 1)
    rows = np.arange(block)
    angles = 2.0 * np.pi * (freqs[:, None] * rows[None, :] % size) / size
    forward = np.concatenate([np.cos(angles), -np.sin(angles)], axis=0)
    weight = np.where((freqs == 0) | (freqs == block), 1.0, 2.0)[:, None] / size
    inverse = np.concatenate([weight * np.cos(angles), -weight * np.sin(angles)], axis=0).T
    return jnp.asarray(forward, F32), jnp.asarray(inverse, F32)


def spectrum(forward, rows):
    both = jnp.dot(forward, rows, precision=EXACT, preferred_element_type=F32)
    half = both.shape[0] // 2
    return both[:half], both[half:]


def back(inverse, real_part, imag_part):
    return jnp.dot(
        inverse, jnp.concatenate([real_part, imag_part], 0), precision=EXACT, preferred_element_type=F32
    )


def body(outer_gate, inner_gate, values, residues, log_decay, skip_gain, out_weight, out_grad):
    ctx = lax.axis_size("ctx")
    tps = lax.axis_size("tp")
    dev = lax.axis_index("ctx")
    tp = lax.axis_index("tp")
    block, chans = outer_gate.shape
    modes = residues.shape[0]
    feats = out_grad.shape[1]
    ny = tps
    nz = ctx // (2 * ny)
    pairs = ctx // 2
    core = dev % 2
    pair = dev // 2
    yy = dev // (2 * nz)
    width = feats // (2 * nz)

    def swap_core(a):
        return lax.ppermute(a, "ctx", [(i, i ^ 1) for i in range(ctx)])

    def shift_tp(a, k):
        return lax.ppermute(a, "tp", [(i, (i + k) % tps) for i in range(tps)])

    def shift_y(a, k):
        per = 2 * nz
        return lax.ppermute(a, "ctx", [(i, (i // per + k) % ny * per + i % per) for i in range(ctx)])

    def of_pairs(a):
        copies = jnp.broadcast_to(a[None], (pairs, *a.shape))
        groups = [[2 * i + j for i in range(pairs)] for j in range(2)]
        return lax.all_to_all(copies, "ctx", 0, 0, tiled=True, axis_index_groups=groups)

    og = out_grad.reshape(block, nz, 2, width)
    og_mine = lax.dynamic_index_in_dim(og, core, 2, keepdims=False)
    og_other = lax.dynamic_index_in_dim(og, 1 - core, 2, keepdims=False)
    pg0 = jnp.concatenate([og_mine, swap_core(og_other)], 0).reshape(2 * block, nz * width)
    pgs = [pg0] + [shift_tp(pg0, k) for k in range(1, tps)]

    u = inner_gate.astype(F32) * values.astype(F32)
    rate = jnp.exp(log_decay)
    rows = jnp.arange(block, dtype=F32)[None, :, None]
    rate3 = rate[:, None, :]
    rise = jnp.exp(-rate3 * (block - rows))
    fall_block = jnp.exp(-rate * block)

    lead = rise * u[None]
    st = jnp.sum(lead, 1)
    st_lag = jnp.sum(lead * (block - rows), 1)
    mine = jnp.concatenate([st, st_lag], 0)
    theirs = swap_core(mine)
    first = jnp.where(core == 0, mine, theirs)
    second = jnp.where(core == 0, theirs, mine)
    half = chans // 2

    def my_half(a):
        return lax.dynamic_slice_in_dim(a, core * half, half, a.ndim - 1)

    def both_halves(a):
        other = swap_core(a)
        return jnp.concatenate(
            [jnp.where(core == 0, a, other), jnp.where(core == 0, other, a)], a.ndim - 1
        )

    rate_h = my_half(rate)
    decay_h = jnp.exp(-rate_h * block)
    f_h, s_h = my_half(first), my_half(second)
    total = decay_h * f_h[:modes] + s_h[:modes]
    total_lag = decay_h * (block * f_h[:modes] + f_h[modes:]) + s_h[modes:]
    to_send = jnp.concatenate([total, total_lag], 0).astype(BF16)
    gathered = of_pairs(to_send).astype(F32)
    place = jnp.arange(pairs, dtype=jnp.int32)
    gap = (2 * block) * jnp.maximum(pair - 1 - place, 0).astype(F32)[:, None, None]
    weight = jnp.where(
        (place < pair)[:, None, None], jnp.exp(-rate_h[None] * gap), 0.0
    )
    in_h = jnp.sum(weight * gathered[:, :modes], 0)
    in_lag_h = jnp.sum(weight * (gap * gathered[:, :modes] + gathered[:, modes:]), 0)
    incoming = both_halves(jnp.concatenate([in_h, in_lag_h], 0))
    in_pair, in_pair_lag = incoming[:modes], incoming[modes:]
    x_in = jnp.where(core == 0, in_pair, fall_block * in_pair + first[:modes])
    x_lag = jnp.where(
        core == 0, in_pair_lag, fall_block * (in_pair_lag + block * in_pair) + first[modes:]
    )

    outer_gate, inner_gate, values, residues, log_decay, x_in, x_lag = lax.optimization_barrier(
        (outer_gate, inner_gate, values, residues, log_decay, x_in, x_lag)
    )
    rate = jnp.exp(log_decay)
    gain = residues * jnp.sqrt(-jnp.expm1(-2.0 * rate))
    fall = jnp.exp(-rate[:, None, :] * rows)
    outer_f = outer_gate.astype(F32)
    u = inner_gate.astype(F32) * values.astype(F32)

    forward, inverse = dft_tables(block)
    response = jnp.sum(gain[:, None, :] * fall, 0)
    h_re, h_im = spectrum(forward, response)
    u_re, u_im = spectrum(forward, u)
    conv_local = back(inverse, h_re * u_re - h_im * u_im, h_re * u_im + h_im * u_re)
    conv_out = conv_local + jnp.sum((gain * x_in)[:, None, :] * fall, 0)
    gated = conv_out + skip_gain[None, :] * u
    result = (outer_f * gated).astype(BF16)

    result_pair = jnp.concatenate([result, swap_core(result)], 0)
    parts = [
        lax.dot_general(result_pair, pg, (((0,), (0,)), ((), ())), preferred_element_type=F32)
        .astype(BF16)
        .reshape(chans, nz, width)
        .swapaxes(0, 1)
        for pg in pgs
    ]
    parts = jnp.stack(parts, 0)

    def part_for(s):
        return lax.dynamic_index_in_dim(parts, (tp - yy - s) % tps, 0, keepdims=False)

    y_parts = [part_for(s) for s in range(ny)]
    over_y = [y_parts[0]] + [shift_y(y_parts[s], s) for s in range(1, ny)]
    summed_y = sum(a.astype(F32) for a in over_y).astype(BF16)

    w_blocks = out_weight.reshape(chans, tps, feats)

    def projected(k):
        w_block = lax.dynamic_index_in_dim(w_blocks, (tp + k) % tps, 1, keepdims=False)
        return jnp.dot(result, w_block, preferred_element_type=F32)

    mixed = projected(0)
    for k in range(1, tps):
        piece = projected(k).astype(BF16)
        piece = shift_tp(piece, k)
        mixed = mixed + piece.astype(F32)
    mixed = mixed.astype(BF16)

    w_half = lax.dynamic_index_in_dim(
        out_weight.reshape(chans, tps, nz, 2, width), core, 3, keepdims=False
    ).reshape(chans, tps, nz * width)
    grad_pair = 0.0
    for k in range(tps):
        w_block = lax.dynamic_index_in_dim(w_half, (tp - k) % tps, 1, keepdims=False)
        grad_pair = grad_pair + lax.dot_general(
            pgs[k], w_block, (((1,), (1,)), ((), ())), preferred_element_type=F32
        )
    grad_gated = grad_pair[:block] + swap_core(grad_pair[block:])
    outer_gate, inner_gate, values, residues, log_decay, grad_gated = lax.optimization_barrier(
        (outer_gate, inner_gate, values, residues, log_decay, grad_gated)
    )
    outer_f = outer_gate.astype(F32)
    inner_f = inner_gate.astype(F32)
    value_f = values.astype(F32)
    u = inner_f * value_f
    rate = jnp.exp(log_decay)
    norm = jnp.sqrt(-jnp.expm1(-2.0 * rate))
    gain = residues * norm
    fall = jnp.exp(-rate[:, None, :] * rows)
    rise = jnp.exp(-rate[:, None, :] * (block - rows))
    fall_block = jnp.exp(-rate * block)
    gc = grad_gated * outer_f
    grad_outer = (grad_gated * gated).astype(BF16)

    g_re, g_im = spectrum(forward, gc)
    corr_local = back(inverse, h_re * g_re + h_im * g_im, h_re * g_im - h_im * g_re)
    lags = back(inverse, u_re * g_re + u_im * g_im, u_re * g_im - u_im * g_re)
    fg = fall * gc[None]
    g_st = jnp.sum(fg, 1)
    g_lag = jnp.sum(fg * rows, 1)
    fl = fall * lags[None]
    sum_a = g_st * x_in + jnp.sum(fl, 1)
    sum_b = g_lag * x_in + g_st * x_lag + jnp.sum(fl * rows, 1)
    sum_skip = jnp.sum(gc * u, 0, keepdims=True)
    mine_g = jnp.concatenate([g_st, sum_a, sum_b, sum_skip], 0)
    theirs_g = swap_core(mine_g)
    later = jnp.where(core == 0, theirs_g[:modes], mine_g[:modes])
    mine_h, theirs_h = my_half(mine_g), my_half(theirs_g)
    early_h = jnp.where(core == 0, mine_h[:modes], theirs_h[:modes])
    total_g = early_h + decay_h * my_half(later)
    sent = jnp.concatenate([total_g, mine_h[modes:] + theirs_h[modes:]], 0).astype(BF16)
    got = of_pairs(sent).astype(F32)
    gap_g = (2 * block) * jnp.maximum(place - pair - 1, 0).astype(F32)[:, None, None]
    weight_g = jnp.where((place > pair)[:, None, None], jnp.exp(-rate_h[None] * gap_g), 0.0)
    h_half = jnp.sum(weight_g * got[:, :modes], 0)
    sums_half = jnp.sum(got[:, modes:], 0)
    final = both_halves(jnp.concatenate([h_half, sums_half], 0))
    h_pair = final[:modes]
    h_in = jnp.where(core == 0, later + fall_block * h_pair, h_pair)
    tot_a, tot_b = final[modes : 2 * modes], final[2 * modes : 3 * modes]
    grad_skip = final[3 * modes]
    grad_residues = norm * tot_a
    grad_decay = rate * residues * (jnp.exp(-2.0 * rate) / norm * tot_a - norm * tot_b)
    corr_in = corr_local + jnp.sum((gain * h_in)[:, None, :] * rise, 0)
    grad_mixed = corr_in + skip_gain[None, :] * gc
    grad_inner = (grad_mixed * value_f).astype(BF16)
    grad_values = (grad_mixed * inner_f).astype(BF16)

    z_groups = [[i * 2 * nz + j * 2 + k for j in range(nz)] for i in range(ny) for k in range(2)]
    over_z = lax.all_to_all(summed_y, "ctx", 0, 0, tiled=True, axis_index_groups=z_groups)
    grad_weight = jnp.sum(over_z.astype(F32), 0)
    return (
        mixed,
        grad_outer,
        grad_inner,
        grad_values,
        grad_weight,
        grad_skip,
        grad_residues,
        grad_decay,
    )


def solution(mesh):
    placed = (
        P("ctx", "tp"),
        P("ctx", "tp"),
        P("ctx", "tp"),
        P(None, "tp"),
        P(None, "tp"),
        P("tp"),
        P("tp", None),
        P("ctx", "tp"),
    )

    return jax.shard_map(
        body,
        mesh=mesh,
        in_specs=placed,
        out_specs=(
            P("ctx", "tp"),
            P("ctx", "tp"),
            P("ctx", "tp"),
            P("ctx", "tp"),
            P("tp", "ctx"),
            P("tp"),
            P(None, "tp"),
            P(None, "tp"),
        ),
        check_vma=False,
    )
```

```python
import jax
import jax.numpy as jnp
import numpy as np
from jax import lax
from jax.experimental import pallas as pl
from jax.experimental.layout import Layout, with_layout_constraint
from jax.experimental.pallas import tpu as pltpu
from jax.sharding import PartitionSpec as P

F32 = jnp.float32
BF16 = jnp.bfloat16
EXACT = lax.Precision.HIGHEST


def dft_tables(block):
    size = 2 * block
    freqs = np.arange(block + 1)
    rows = np.arange(block)
    angles = 2.0 * np.pi * (freqs[:, None] * rows[None, :] % size) / size
    forward = np.concatenate([np.cos(angles), -np.sin(angles)], axis=0)
    weight = np.where((freqs == 0) | (freqs == block), 1.0, 2.0)[:, None] / size
    inverse = np.concatenate([weight * np.cos(angles), -weight * np.sin(angles)], axis=0).T
    return jnp.asarray(forward, F32), jnp.asarray(inverse, F32)


def spectrum(forward, rows):
    both = jnp.dot(forward, rows, precision=EXACT, preferred_element_type=F32)
    half = both.shape[0] // 2
    return both[:half], both[half:]


def back(inverse, real_part, imag_part):
    return jnp.dot(
        inverse, jnp.concatenate([real_part, imag_part], 0), precision=EXACT, preferred_element_type=F32
    )


def row_major(a):
    return with_layout_constraint(a, Layout(major_to_minor=tuple(range(a.ndim))))


def in_vmem(count):
    return [pl.BlockSpec(memory_space=pltpu.VMEM)] * count


def given_half(turns, rows, width):
    count = rows.shape[1] // (2 * width)

    def kernel(turns_ref, rows_ref, out_ref):
        other = 1 - turns_ref[0]
        for i in range(count):
            at = pl.multiple_of((2 * i + other) * width, width)
            out_ref[:, i * width : (i + 1) * width] = rows_ref[:, pl.ds(at, width)]

    return pl.pallas_call(
        kernel,
        out_shape=jax.ShapeDtypeStruct((rows.shape[0], count * width), rows.dtype),
        in_specs=[pl.BlockSpec(memory_space=pltpu.SMEM)] + in_vmem(1),
        out_specs=in_vmem(1)[0],
    )(turns, rows)


def weight_parts(turns, result, result_other, blocks, taken, width):
    count = len(blocks)
    tokens, chans = result.shape
    tiles = blocks[0].shape[1] // (2 * width)

    def kernel(turns_ref, *refs):
        mine_ref, other_ref = refs[:2]
        block_refs, taken_refs = refs[2 : 2 + count], refs[2 + count : 2 + 2 * count]
        out_refs, all_ref = refs[2 + 2 * count : -1], refs[-1]
        core = turns_ref[0]
        for k in range(count):
            for i in range(tiles):
                at = pl.multiple_of((2 * i + core) * width, width)
                lanes = slice(i * width, (i + 1) * width)
                all_ref[k, :tokens, lanes] = block_refs[k][:, pl.ds(at, width)]
            all_ref[k, tokens:, :] = taken_refs[k][...]
        left = jnp.concatenate([mine_ref[...], other_ref[...]], 0).T
        for s in range(count):
            part = jnp.dot(
                left, all_ref[(turns_ref[1] - s + count) % count], preferred_element_type=F32
            ).astype(BF16)
            for i in range(tiles):
                out_refs[s][i] = part[:, i * width : (i + 1) * width]

    return pl.pallas_call(
        kernel,
        out_shape=[jax.ShapeDtypeStruct((tiles, chans, width), BF16)] * count,
        in_specs=[pl.BlockSpec(memory_space=pltpu.SMEM)] + in_vmem(2 + 2 * count),
        out_specs=in_vmem(count),
        scratch_shapes=[pltpu.VMEM((count, 2 * tokens, tiles * width), BF16)],
    )(turns, result, result_other, *blocks, *taken)


def body(outer_gate, inner_gate, values, residues, log_decay, skip_gain, out_weight, out_grad):
    ctx = lax.axis_size("ctx")
    tps = lax.axis_size("tp")
    dev = lax.axis_index("ctx")
    tp = lax.axis_index("tp")
    block, chans = outer_gate.shape
    first_weight = row_major(out_weight)
    modes = residues.shape[0]
    feats = out_grad.shape[1]
    ny = tps
    nz = ctx // (2 * ny)
    pairs = ctx // 2
    core = dev % 2
    pair = dev // 2
    yy = dev // (2 * nz)
    width = feats // (2 * nz)

    def swap_core(a):
        return lax.ppermute(a, "ctx", [(i, i ^ 1) for i in range(ctx)])

    def shift_tp(a, k):
        return lax.ppermute(a, "tp", [(i, (i + k) % tps) for i in range(tps)])

    def shift_y(a, k):
        per = 2 * nz
        return lax.ppermute(a, "ctx", [(i, (i // per + k) % ny * per + i % per) for i in range(ctx)])

    def of_pairs(a):
        copies = jnp.broadcast_to(a[None], (pairs, *a.shape))
        groups = [[2 * i + j for i in range(pairs)] for j in range(2)]
        return lax.all_to_all(copies, "ctx", 0, 0, tiled=True, axis_index_groups=groups)

    og = [out_grad] + [row_major(shift_tp(out_grad, k)) for k in range(1, tps)]

    u = inner_gate.astype(F32) * values.astype(F32)
    rate = jnp.exp(log_decay)
    rows = jnp.arange(block, dtype=F32)[None, :, None]
    rate3 = rate[:, None, :]
    rise = jnp.exp(-rate3 * (block - rows))
    fall_block = jnp.exp(-rate * block)

    lead = rise * u[None]
    st = jnp.sum(lead, 1)
    st_lag = jnp.sum(lead * (block - rows), 1)
    mine = jnp.concatenate([st, st_lag], 0)
    theirs = swap_core(mine)
    first = jnp.where(core == 0, mine, theirs)
    second = jnp.where(core == 0, theirs, mine)
    half = chans // 2

    def my_half(a):
        return lax.dynamic_slice_in_dim(a, core * half, half, a.ndim - 1)

    def both_halves(a):
        other = swap_core(a)
        return jnp.concatenate(
            [jnp.where(core == 0, a, other), jnp.where(core == 0, other, a)], a.ndim - 1
        )

    rate_h = my_half(rate)
    decay_h = jnp.exp(-rate_h * block)
    f_h, s_h = my_half(first), my_half(second)
    total = decay_h * f_h[:modes] + s_h[:modes]
    total_lag = decay_h * (block * f_h[:modes] + f_h[modes:]) + s_h[modes:]
    to_send = jnp.concatenate([total, total_lag], 0).astype(BF16)
    gathered = of_pairs(to_send).astype(F32)
    place = jnp.arange(pairs, dtype=jnp.int32)
    gap = (2 * block) * jnp.maximum(pair - 1 - place, 0).astype(F32)[:, None, None]
    weight = jnp.where(
        (place < pair)[:, None, None], jnp.exp(-rate_h[None] * gap), 0.0
    )
    in_h = jnp.sum(weight * gathered[:, :modes], 0)
    in_lag_h = jnp.sum(weight * (gap * gathered[:, :modes] + gathered[:, modes:]), 0)
    incoming = both_halves(jnp.concatenate([in_h, in_lag_h], 0))
    in_pair, in_pair_lag = incoming[:modes], incoming[modes:]
    x_in = jnp.where(core == 0, in_pair, fall_block * in_pair + first[:modes])
    x_lag = jnp.where(
        core == 0, in_pair_lag, fall_block * (in_pair_lag + block * in_pair) + first[modes:]
    )

    outer_gate, inner_gate, values, residues, log_decay, x_in, x_lag = lax.optimization_barrier(
        (outer_gate, inner_gate, values, residues, log_decay, x_in, x_lag)
    )
    rate = jnp.exp(log_decay)
    gain = residues * jnp.sqrt(-jnp.expm1(-2.0 * rate))
    fall = jnp.exp(-rate[:, None, :] * rows)
    outer_f = outer_gate.astype(F32)
    u = inner_gate.astype(F32) * values.astype(F32)

    forward, inverse = dft_tables(block)
    response = jnp.sum(gain[:, None, :] * fall, 0)
    h_re, h_im = spectrum(forward, response)
    u_re, u_im = spectrum(forward, u)
    conv_local = back(inverse, h_re * u_re - h_im * u_im, h_re * u_im + h_im * u_re)
    conv_out = conv_local + jnp.sum((gain * x_in)[:, None, :] * fall, 0)
    gated = conv_out + skip_gain[None, :] * u
    result = row_major((outer_f * gated).astype(BF16))

    turns = jnp.stack([core, (tp - yy) % tps]).astype(jnp.int32)
    given = [given_half(turns, a, width) for a in og]
    taken = [swap_core(a) for a in given]
    result_other = swap_core(result)
    y_parts = weight_parts(turns, result, result_other, og, taken, width)
    over_y = [y_parts[0]] + [shift_y(y_parts[s], s) for s in range(1, ny)]
    summed_y = sum(a.astype(F32) for a in over_y).astype(BF16)

    late = lax.optimization_barrier((result, gated, out_weight, *y_parts))
    result, gated, out_weight = late[:3]

    def projected(k):
        w_block = lax.dynamic_slice_in_dim(out_weight, (tp + k) % tps * feats, feats, 1)
        return jnp.dot(result, w_block, preferred_element_type=F32)

    mixed = projected(0)
    for k in range(1, tps):
        piece = projected(k).astype(BF16)
        piece = shift_tp(piece, k)
        mixed = mixed + piece.astype(F32)
    mixed = mixed.astype(BF16)

    grad_gated = 0.0
    for k in range(tps):
        w_block = lax.dynamic_slice_in_dim(first_weight, (tp - k) % tps * feats, feats, 1)
        grad_gated = grad_gated + lax.dot_general(
            og[k], w_block, (((1,), (1,)), ((), ())), preferred_element_type=F32
        )
    late = lax.optimization_barrier(
        (outer_gate, inner_gate, values, residues, log_decay, grad_gated, *y_parts)
    )
    outer_gate, inner_gate, values, residues, log_decay, grad_gated = late[:6]
    outer_f = outer_gate.astype(F32)
    inner_f = inner_gate.astype(F32)
    value_f = values.astype(F32)
    u = inner_f * value_f
    rate = jnp.exp(log_decay)
    norm = jnp.sqrt(-jnp.expm1(-2.0 * rate))
    gain = residues * norm
    fall = jnp.exp(-rate[:, None, :] * rows)
    rise = jnp.exp(-rate[:, None, :] * (block - rows))
    fall_block = jnp.exp(-rate * block)
    gc = grad_gated * outer_f
    grad_outer = (grad_gated * gated).astype(BF16)

    g_re, g_im = spectrum(forward, gc)
    corr_local = back(inverse, h_re * g_re + h_im * g_im, h_re * g_im - h_im * g_re)
    lags = back(inverse, u_re * g_re + u_im * g_im, u_re * g_im - u_im * g_re)
    fg = fall * gc[None]
    g_st = jnp.sum(fg, 1)
    g_lag = jnp.sum(fg * rows, 1)
    fl = fall * lags[None]
    sum_a = g_st * x_in + jnp.sum(fl, 1)
    sum_b = g_lag * x_in + g_st * x_lag + jnp.sum(fl * rows, 1)
    sum_skip = jnp.sum(gc * u, 0, keepdims=True)
    mine_g = jnp.concatenate([g_st, sum_a, sum_b, sum_skip], 0)
    theirs_g = swap_core(mine_g)
    later = jnp.where(core == 0, theirs_g[:modes], mine_g[:modes])
    mine_h, theirs_h = my_half(mine_g), my_half(theirs_g)
    early_h = jnp.where(core == 0, mine_h[:modes], theirs_h[:modes])
    total_g = early_h + decay_h * my_half(later)
    sent = jnp.concatenate([total_g, mine_h[modes:] + theirs_h[modes:]], 0).astype(BF16)
    got = of_pairs(sent).astype(F32)
    gap_g = (2 * block) * jnp.maximum(place - pair - 1, 0).astype(F32)[:, None, None]
    weight_g = jnp.where((place > pair)[:, None, None], jnp.exp(-rate_h[None] * gap_g), 0.0)
    h_half = jnp.sum(weight_g * got[:, :modes], 0)
    sums_half = jnp.sum(got[:, modes:], 0)
    final = both_halves(jnp.concatenate([h_half, sums_half], 0))
    h_pair = final[:modes]
    h_in = jnp.where(core == 0, later + fall_block * h_pair, h_pair)
    tot_a, tot_b = final[modes : 2 * modes], final[2 * modes : 3 * modes]
    grad_skip = final[3 * modes]
    grad_residues = norm * tot_a
    grad_decay = rate * residues * (jnp.exp(-2.0 * rate) / norm * tot_a - norm * tot_b)
    corr_in = corr_local + jnp.sum((gain * h_in)[:, None, :] * rise, 0)
    grad_mixed = corr_in + skip_gain[None, :] * gc
    grad_inner = (grad_mixed * value_f).astype(BF16)
    grad_values = (grad_mixed * inner_f).astype(BF16)

    z_groups = [[i * 2 * nz + j * 2 + k for j in range(nz)] for i in range(ny) for k in range(2)]
    over_z = lax.all_to_all(summed_y, "ctx", 0, 0, tiled=True, axis_index_groups=z_groups)
    grad_weight = jnp.sum(over_z.astype(F32), 0)
    return (
        mixed,
        grad_outer,
        grad_inner,
        grad_values,
        grad_weight,
        grad_skip,
        grad_residues,
        grad_decay,
    )


def solution(mesh):
    placed = (
        P("ctx", "tp"),
        P("ctx", "tp"),
        P("ctx", "tp"),
        P(None, "tp"),
        P(None, "tp"),
        P("tp"),
        P("tp", None),
        P("ctx", "tp"),
    )

    return jax.shard_map(
        body,
        mesh=mesh,
        in_specs=placed,
        out_specs=(
            P("ctx", "tp"),
            P("ctx", "tp"),
            P("ctx", "tp"),
            P("ctx", "tp"),
            P("tp", "ctx"),
            P("tp"),
            P(None, "tp"),
            P(None, "tp"),
        ),
        check_vma=False,
    )
```

```python
import jax
import jax.numpy as jnp
import numpy as np
from jax import lax
from jax.experimental import pallas as pl
from jax.experimental.layout import Layout, with_layout_constraint
from jax.experimental.pallas import tpu as pltpu
from jax.sharding import PartitionSpec as P

F32 = jnp.float32
BF16 = jnp.bfloat16
EXACT = lax.Precision.HIGHEST


def dft_tables(block):
    size = 2 * block
    freqs = np.arange(block + 1)
    rows = np.arange(block)
    angles = 2.0 * np.pi * (freqs[:, None] * rows[None, :] % size) / size
    forward = np.concatenate([np.cos(angles), -np.sin(angles)], axis=0)
    weight = np.where((freqs == 0) | (freqs == block), 1.0, 2.0)[:, None] / size
    inverse = np.concatenate([weight * np.cos(angles), -weight * np.sin(angles)], axis=0).T
    return jnp.asarray(forward, F32), jnp.asarray(inverse, F32)


def spectrum(forward, rows):
    both = jnp.dot(forward, rows, precision=EXACT, preferred_element_type=F32)
    half = both.shape[0] // 2
    return both[:half], both[half:]


def back(inverse, real_part, imag_part):
    return jnp.dot(
        inverse, jnp.concatenate([real_part, imag_part], 0), precision=EXACT, preferred_element_type=F32
    )


def row_major(a):
    return with_layout_constraint(a, Layout(major_to_minor=tuple(range(a.ndim))))


def in_vmem(count):
    return [pl.BlockSpec(memory_space=pltpu.VMEM)] * count


def weight_parts(turns, result, result_other, blocks, taken, width):
    count = len(blocks)
    tokens, chans = result.shape
    tiles = blocks[0].shape[1] // (2 * width)

    def kernel(turns_ref, *refs):
        mine_ref, other_ref = refs[:2]
        block_refs, taken_refs = refs[2 : 2 + count], refs[2 + count : 2 + 2 * count]
        out_refs, all_ref = refs[2 + 2 * count : -1], refs[-1]
        core = turns_ref[0]
        for k in range(count):
            for i in range(tiles):
                at = pl.multiple_of((2 * i + core) * width, width)
                lanes = slice(i * width, (i + 1) * width)
                all_ref[k, :tokens, lanes] = block_refs[k][:, pl.ds(at, width)]
                all_ref[k, tokens:, lanes] = taken_refs[k][:, pl.ds(at, width)]
        left = jnp.concatenate([mine_ref[...], other_ref[...]], 0).T
        for s in range(count):
            part = jnp.dot(
                left, all_ref[(turns_ref[1] - s + count) % count], preferred_element_type=F32
            ).astype(BF16)
            for i in range(tiles):
                out_refs[s][i] = part[:, i * width : (i + 1) * width]

    return pl.pallas_call(
        kernel,
        out_shape=[jax.ShapeDtypeStruct((tiles, chans, width), BF16)] * count,
        in_specs=[pl.BlockSpec(memory_space=pltpu.SMEM)] + in_vmem(2 + 2 * count),
        out_specs=in_vmem(count),
        scratch_shapes=[pltpu.VMEM((count, 2 * tokens, tiles * width), BF16)],
    )(turns, result, result_other, *blocks, *taken)


def body(outer_gate, inner_gate, values, residues, log_decay, skip_gain, out_weight, out_grad):
    ctx = lax.axis_size("ctx")
    tps = lax.axis_size("tp")
    dev = lax.axis_index("ctx")
    tp = lax.axis_index("tp")
    block, chans = outer_gate.shape
    modes = residues.shape[0]
    feats = out_grad.shape[1]
    ny = tps
    nz = ctx // (2 * ny)
    core = dev % 2
    zz = dev // 2 % nz
    yy = dev // (2 * nz)
    width = feats // (2 * nz)

    def swap_core(a):
        return lax.ppermute(a, "ctx", [(i, i ^ 1) for i in range(ctx)])

    def shift_tp(a, k):
        return lax.ppermute(a, "tp", [(i, (i + k) % tps) for i in range(tps)])

    def shift_y(a, k):
        per = 2 * nz
        return lax.ppermute(a, "ctx", [(i, (i // per + k) % ny * per + i % per) for i in range(ctx)])

    z_groups = [[i * 2 * nz + j * 2 + k for j in range(nz)] for i in range(ny) for k in range(2)]

    def of_plane(a):
        copies = jnp.broadcast_to(a[None], (nz, *a.shape))
        return lax.all_to_all(copies, "ctx", 0, 0, tiled=True, axis_index_groups=z_groups)

    og = [out_grad] + [row_major(shift_tp(out_grad, k)) for k in range(1, tps)]

    u = inner_gate.astype(F32) * values.astype(F32)
    rate = jnp.exp(log_decay)
    rows = jnp.arange(block, dtype=F32)[None, :, None]
    rate3 = rate[:, None, :]
    rise = jnp.exp(-rate3 * (block - rows))
    fall_block = jnp.exp(-rate * block)

    lead = rise * u[None]
    st = jnp.sum(lead, 1)
    st_lag = jnp.sum(lead * (block - rows), 1)
    mine = jnp.concatenate([st, st_lag], 0)
    theirs = swap_core(mine)
    first = jnp.where(core == 0, mine, theirs)
    second = jnp.where(core == 0, theirs, mine)
    half = chans // 2

    def my_half(a):
        return lax.dynamic_slice_in_dim(a, core * half, half, a.ndim - 1)

    def both_halves(a):
        other = swap_core(a)
        return jnp.concatenate(
            [jnp.where(core == 0, a, other), jnp.where(core == 0, other, a)], a.ndim - 1
        )

    rate_h = my_half(rate)
    decay_h = jnp.exp(-rate_h * block)
    f_h, s_h = my_half(first), my_half(second)
    total = decay_h * f_h[:modes] + s_h[:modes]
    total_lag = decay_h * (block * f_h[:modes] + f_h[modes:]) + s_h[modes:]
    to_send = jnp.concatenate([total, total_lag], 0).astype(BF16)
    gathered = of_plane(to_send).astype(F32)
    place = jnp.arange(nz, dtype=jnp.int32)
    per_pair = 2 * block
    per_plane = per_pair * nz

    def weights(which, gap):
        gap = jnp.where(which, gap, 0).astype(F32)[:, None, None] * per_pair
        return jnp.where(which[:, None, None], jnp.exp(-rate_h[None] * gap), 0.0), gap

    def carried(w, gap):
        base = gathered[:, :modes]
        return jnp.sum(w * base, 0), jnp.sum(w * (gap * base + gathered[:, modes:]), 0)

    plane, plane_lag = carried(*weights(place >= 0, nz - 1 - place))
    plane_all = jnp.concatenate([plane, plane_lag], 0)
    in_h, in_lag_h = carried(*weights(place < zz, zz - 1 - place))
    y_in, y_in_lag = 0.0, 0.0
    for k in range(1, ny):
        per = 2 * nz
        came = lax.ppermute(
            plane_all, "ctx", [(i, i + k * per) for i in range(ctx) if i + k * per < ctx]
        )
        gap = float(per_plane * (k - 1))
        w = jnp.exp(-rate_h * gap)
        y_in = y_in + w * came[:modes]
        y_in_lag = y_in_lag + w * (gap * came[:modes] + came[modes:])
    gap = (per_pair * zz).astype(F32)
    w = jnp.exp(-rate_h * gap)
    in_h = in_h + w * y_in
    in_lag_h = in_lag_h + w * (gap * y_in + y_in_lag)
    incoming = both_halves(jnp.concatenate([in_h, in_lag_h], 0))
    in_pair, in_pair_lag = incoming[:modes], incoming[modes:]
    x_in = jnp.where(core == 0, in_pair, fall_block * in_pair + first[:modes])
    x_lag = jnp.where(
        core == 0, in_pair_lag, fall_block * (in_pair_lag + block * in_pair) + first[modes:]
    )

    outer_gate, inner_gate, values, residues, log_decay, x_in, x_lag = lax.optimization_barrier(
        (outer_gate, inner_gate, values, residues, log_decay, x_in, x_lag)
    )
    rate = jnp.exp(log_decay)
    gain = residues * jnp.sqrt(-jnp.expm1(-2.0 * rate))
    fall = jnp.exp(-rate[:, None, :] * rows)
    outer_f = outer_gate.astype(F32)
    u = inner_gate.astype(F32) * values.astype(F32)

    forward, inverse = dft_tables(block)
    response = jnp.sum(gain[:, None, :] * fall, 0)
    h_re, h_im = spectrum(forward, response)
    u_re, u_im = spectrum(forward, u)
    conv_local = back(inverse, h_re * u_re - h_im * u_im, h_re * u_im + h_im * u_re)
    conv_out = conv_local + jnp.sum((gain * x_in)[:, None, :] * fall, 0)
    gated = conv_out + skip_gain[None, :] * u
    result = row_major((outer_f * gated).astype(BF16))

    turns = jnp.stack([core, (tp - yy) % tps]).astype(jnp.int32)
    taken = [row_major(swap_core(a)) for a in og]
    result_other = swap_core(result)
    y_parts = weight_parts(turns, result, result_other, og, taken, width)
    over_y = [y_parts[0]] + [shift_y(y_parts[s], s) for s in range(1, ny)]
    summed_y = sum(a.astype(F32) for a in over_y).astype(BF16)

    late = lax.optimization_barrier((result, gated, out_weight, *y_parts))
    result, gated, out_weight = late[:3]

    def projected(k):
        w_block = lax.dynamic_slice_in_dim(out_weight, (tp + k) % tps * feats, feats, 1)
        return jnp.dot(result, w_block, preferred_element_type=F32)

    mixed = projected(0)
    for k in range(1, tps):
        piece = projected(k).astype(BF16)
        piece = shift_tp(piece, k)
        mixed = mixed + piece.astype(F32)
    mixed = mixed.astype(BF16)

    grad_gated = 0.0
    for k in range(tps):
        w_block = lax.dynamic_slice_in_dim(out_weight, (tp - k) % tps * feats, feats, 1)
        grad_gated = grad_gated + lax.dot_general(
            og[k], w_block, (((1,), (1,)), ((), ())), preferred_element_type=F32
        )
    late = lax.optimization_barrier(
        (outer_gate, inner_gate, values, residues, log_decay, grad_gated, *y_parts)
    )
    outer_gate, inner_gate, values, residues, log_decay, grad_gated = late[:6]
    outer_f = outer_gate.astype(F32)
    inner_f = inner_gate.astype(F32)
    value_f = values.astype(F32)
    u = inner_f * value_f
    rate = jnp.exp(log_decay)
    norm = jnp.sqrt(-jnp.expm1(-2.0 * rate))
    gain = residues * norm
    fall = jnp.exp(-rate[:, None, :] * rows)
    rise = jnp.exp(-rate[:, None, :] * (block - rows))
    fall_block = jnp.exp(-rate * block)
    gc = grad_gated * outer_f
    grad_outer = (grad_gated * gated).astype(BF16)

    g_re, g_im = spectrum(forward, gc)
    corr_local = back(inverse, h_re * g_re + h_im * g_im, h_re * g_im - h_im * g_re)
    lags = back(inverse, u_re * g_re + u_im * g_im, u_re * g_im - u_im * g_re)
    fg = fall * gc[None]
    g_st = jnp.sum(fg, 1)
    g_lag = jnp.sum(fg * rows, 1)
    fl = fall * lags[None]
    sum_a = g_st * x_in + jnp.sum(fl, 1)
    sum_b = g_lag * x_in + g_st * x_lag + jnp.sum(fl * rows, 1)
    sum_skip = jnp.sum(gc * u, 0, keepdims=True)
    mine_g = jnp.concatenate([g_st, sum_a, sum_b, sum_skip], 0)
    theirs_g = swap_core(mine_g)
    later = jnp.where(core == 0, theirs_g[:modes], mine_g[:modes])
    mine_h, theirs_h = my_half(mine_g), my_half(theirs_g)
    early_h = jnp.where(core == 0, mine_h[:modes], theirs_h[:modes])
    total_g = early_h + decay_h * my_half(later)
    sent = jnp.concatenate([total_g, mine_h[modes:] + theirs_h[modes:]], 0).astype(BF16)
    got = of_plane(sent).astype(F32)
    plane_h = jnp.sum(weights(place >= 0, place)[0] * got[:, :modes], 0)
    plane_sums = jnp.sum(got[:, modes:], 0)
    plane_g = jnp.concatenate([plane_h, plane_sums], 0)
    h_half = jnp.sum(weights(place > zz, place - zz - 1)[0] * got[:, :modes], 0)
    y_h, sums_half = 0.0, plane_sums
    for k in range(1, ny):
        came = shift_y(plane_g, -k)
        w = jnp.exp(-rate_h * float(per_plane * (k - 1)))
        y_h = y_h + jnp.where(yy + k < ny, w * came[:modes], 0.0)
        sums_half = sums_half + came[modes:]
    h_half = h_half + jnp.exp(-rate_h * (per_pair * (nz - 1 - zz)).astype(F32)) * y_h
    final = both_halves(jnp.concatenate([h_half, sums_half], 0))
    h_pair = final[:modes]
    h_in = jnp.where(core == 0, later + fall_block * h_pair, h_pair)
    tot_a, tot_b = final[modes : 2 * modes], final[2 * modes : 3 * modes]
    grad_skip = final[3 * modes]
    grad_residues = norm * tot_a
    grad_decay = rate * residues * (jnp.exp(-2.0 * rate) / norm * tot_a - norm * tot_b)
    corr_in = corr_local + jnp.sum((gain * h_in)[:, None, :] * rise, 0)
    grad_mixed = corr_in + skip_gain[None, :] * gc
    grad_inner = (grad_mixed * value_f).astype(BF16)
    grad_values = (grad_mixed * inner_f).astype(BF16)

    over_z = lax.all_to_all(summed_y, "ctx", 0, 0, tiled=True, axis_index_groups=z_groups)
    grad_weight = jnp.sum(over_z.astype(F32), 0)
    return (
        mixed,
        grad_outer,
        grad_inner,
        grad_values,
        grad_weight,
        grad_skip,
        grad_residues,
        grad_decay,
    )


def solution(mesh):
    placed = (
        P("ctx", "tp"),
        P("ctx", "tp"),
        P("ctx", "tp"),
        P(None, "tp"),
        P(None, "tp"),
        P("tp"),
        P("tp", None),
        P("ctx", "tp"),
    )

    return jax.shard_map(
        body,
        mesh=mesh,
        in_specs=placed,
        out_specs=(
            P("ctx", "tp"),
            P("ctx", "tp"),
            P("ctx", "tp"),
            P("ctx", "tp"),
            P("tp", "ctx"),
            P("tp"),
            P(None, "tp"),
            P(None, "tp"),
        ),
        check_vma=False,
    )
```

```python
import jax
import jax.numpy as jnp
import numpy as np
from jax import lax
from jax.experimental import pallas as pl
from jax.experimental.layout import Layout, with_layout_constraint
from jax.experimental.pallas import tpu as pltpu
from jax.sharding import PartitionSpec as P

F32 = jnp.float32
BF16 = jnp.bfloat16
EXACT = lax.Precision.HIGHEST


def dft_tables(block):
    size = 2 * block
    freqs = np.arange(block + 1)
    rows = np.arange(block)
    angles = 2.0 * np.pi * (freqs[:, None] * rows[None, :] % size) / size
    forward = np.concatenate([np.cos(angles), -np.sin(angles)], axis=0)
    weight = np.where((freqs == 0) | (freqs == block), 1.0, 2.0)[:, None] / size
    inverse = np.concatenate([weight * np.cos(angles), -weight * np.sin(angles)], axis=0).T
    return jnp.asarray(forward, F32), jnp.asarray(inverse, F32)


def spectrum(forward, rows):
    both = jnp.dot(forward, rows, precision=EXACT, preferred_element_type=F32)
    half = both.shape[0] // 2
    return both[:half], both[half:]


def back(inverse, real_part, imag_part):
    return jnp.dot(
        inverse, jnp.concatenate([real_part, imag_part], 0), precision=EXACT, preferred_element_type=F32
    )


def row_major(a):
    return with_layout_constraint(a, Layout(major_to_minor=tuple(range(a.ndim))))


def in_vmem(count):
    return [pl.BlockSpec(memory_space=pltpu.VMEM)] * count


def weight_parts(turns, result, result_other, blocks, taken, width):
    count = len(blocks)
    tokens, chans = result.shape
    tiles = blocks[0].shape[1] // (2 * width)

    def kernel(turns_ref, *refs):
        mine_ref, other_ref = refs[:2]
        block_refs, taken_refs = refs[2 : 2 + count], refs[2 + count : 2 + 2 * count]
        out_refs, all_ref = refs[2 + 2 * count : -1], refs[-1]
        core = turns_ref[0]
        for k in range(count):
            for i in range(tiles):
                at = pl.multiple_of((2 * i + core) * width, width)
                lanes = slice(i * width, (i + 1) * width)
                all_ref[k, :tokens, lanes] = block_refs[k][:, pl.ds(at, width)]
                all_ref[k, tokens:, lanes] = taken_refs[k][:, pl.ds(at, width)]
        left = jnp.concatenate([mine_ref[...], other_ref[...]], 0).T
        for s in range(count):
            part = jnp.dot(
                left, all_ref[(turns_ref[1] - s + count) % count], preferred_element_type=F32
            ).astype(BF16)
            for i in range(tiles):
                out_refs[s][i] = part[:, i * width : (i + 1) * width]

    return pl.pallas_call(
        kernel,
        out_shape=[jax.ShapeDtypeStruct((tiles, chans, width), BF16)] * count,
        in_specs=[pl.BlockSpec(memory_space=pltpu.SMEM)] + in_vmem(2 + 2 * count),
        out_specs=in_vmem(count),
        scratch_shapes=[pltpu.VMEM((count, 2 * tokens, tiles * width), BF16)],
    )(turns, result, result_other, *blocks, *taken)


def body(outer_gate, inner_gate, values, residues, log_decay, skip_gain, out_weight, out_grad):
    ctx = lax.axis_size("ctx")
    tps = lax.axis_size("tp")
    dev = lax.axis_index("ctx")
    tp = lax.axis_index("tp")
    block, chans = outer_gate.shape
    modes = residues.shape[0]
    feats = out_grad.shape[1]
    ny = tps
    nz = ctx // (2 * ny)
    core = dev % 2
    pair = dev // 2
    zz = pair % nz
    pairs = ctx // 2
    yy = dev // (2 * nz)
    width = feats // (2 * nz)

    def swap_core(a):
        return lax.ppermute(a, "ctx", [(i, i ^ 1) for i in range(ctx)])

    def shift_tp(a, k):
        return lax.ppermute(a, "tp", [(i, (i + k) % tps) for i in range(tps)])

    def shift_y(a, k):
        per = 2 * nz
        return lax.ppermute(a, "ctx", [(i, (i // per + k) % ny * per + i % per) for i in range(ctx)])

    z_groups = [[i * 2 * nz + j * 2 + k for j in range(nz)] for i in range(ny) for k in range(2)]

    def of_plane(a):
        copies = jnp.broadcast_to(a[None], (nz, *a.shape))
        return lax.all_to_all(copies, "ctx", 0, 0, tiled=True, axis_index_groups=z_groups)

    def of_pairs(a):
        copies = jnp.broadcast_to(a[None], (pairs, *a.shape))
        groups = [[2 * i + j for i in range(pairs)] for j in range(2)]
        return lax.all_to_all(copies, "ctx", 0, 0, tiled=True, axis_index_groups=groups)

    og = [out_grad] + [row_major(shift_tp(out_grad, k)) for k in range(1, tps)]

    u = inner_gate.astype(F32) * values.astype(F32)
    rate = jnp.exp(log_decay)
    rows = jnp.arange(block, dtype=F32)[None, :, None]
    rate3 = rate[:, None, :]
    rise = jnp.exp(-rate3 * (block - rows))
    fall_block = jnp.exp(-rate * block)

    lead = rise * u[None]
    st = jnp.sum(lead, 1)
    st_lag = jnp.sum(lead * (block - rows), 1)
    mine = jnp.concatenate([st, st_lag], 0)
    theirs = swap_core(mine)
    first = jnp.where(core == 0, mine, theirs)
    second = jnp.where(core == 0, theirs, mine)
    half = chans // 2

    def my_half(a):
        return lax.dynamic_slice_in_dim(a, core * half, half, a.ndim - 1)

    def both_halves(a):
        other = swap_core(a)
        return jnp.concatenate(
            [jnp.where(core == 0, a, other), jnp.where(core == 0, other, a)], a.ndim - 1
        )

    rate_h = my_half(rate)
    decay_h = jnp.exp(-rate_h * block)
    f_h, s_h = my_half(first), my_half(second)
    total = decay_h * f_h[:modes] + s_h[:modes]
    total_lag = decay_h * (block * f_h[:modes] + f_h[modes:]) + s_h[modes:]
    to_send = jnp.concatenate([total, total_lag], 0).astype(BF16)
    gathered = of_pairs(to_send).astype(F32)
    place = jnp.arange(nz, dtype=jnp.int32)
    every = jnp.arange(pairs, dtype=jnp.int32)
    per_pair = 2 * block
    per_plane = per_pair * nz

    def weights(which, gap):
        gap = jnp.where(which, gap, 0).astype(F32)[:, None, None] * per_pair
        return jnp.where(which[:, None, None], jnp.exp(-rate_h[None] * gap), 0.0), gap

    w, gap = weights(every < pair, pair - 1 - every)
    base = gathered[:, :modes]
    in_h = jnp.sum(w * base, 0)
    in_lag_h = jnp.sum(w * (gap * base + gathered[:, modes:]), 0)
    incoming = both_halves(jnp.concatenate([in_h, in_lag_h], 0))
    in_pair, in_pair_lag = incoming[:modes], incoming[modes:]
    x_in = jnp.where(core == 0, in_pair, fall_block * in_pair + first[:modes])
    x_lag = jnp.where(
        core == 0, in_pair_lag, fall_block * (in_pair_lag + block * in_pair) + first[modes:]
    )

    outer_gate, inner_gate, values, residues, log_decay, x_in, x_lag = lax.optimization_barrier(
        (outer_gate, inner_gate, values, residues, log_decay, x_in, x_lag)
    )
    rate = jnp.exp(log_decay)
    gain = residues * jnp.sqrt(-jnp.expm1(-2.0 * rate))
    fall = jnp.exp(-rate[:, None, :] * rows)
    outer_f = outer_gate.astype(F32)
    u = inner_gate.astype(F32) * values.astype(F32)

    forward, inverse = dft_tables(block)
    response = jnp.sum(gain[:, None, :] * fall, 0)
    h_re, h_im = spectrum(forward, response)
    u_re, u_im = spectrum(forward, u)
    conv_local = back(inverse, h_re * u_re - h_im * u_im, h_re * u_im + h_im * u_re)
    conv_out = conv_local + jnp.sum((gain * x_in)[:, None, :] * fall, 0)
    gated = conv_out + skip_gain[None, :] * u
    result = row_major((outer_f * gated).astype(BF16))

    turns = jnp.stack([core, (tp - yy) % tps]).astype(jnp.int32)
    taken = [row_major(swap_core(a)) for a in og]
    result_other = swap_core(result)
    y_parts = weight_parts(turns, result, result_other, og, taken, width)
    over_y = [y_parts[0]] + [shift_y(y_parts[s], s) for s in range(1, ny)]
    summed_y = sum(a.astype(F32) for a in over_y).astype(BF16)

    late = lax.optimization_barrier((result, gated, out_weight, *y_parts))
    result, gated, out_weight = late[:3]

    def projected(k):
        w_block = lax.dynamic_slice_in_dim(out_weight, (tp + k) % tps * feats, feats, 1)
        return jnp.dot(result, w_block, preferred_element_type=F32).astype(BF16)

    mixed = projected(0).astype(F32)
    for k in range(1, tps):
        piece = projected(k)
        piece = shift_tp(piece, k)
        mixed = mixed + piece.astype(F32)
    mixed = mixed.astype(BF16)

    grad_gated = 0.0
    for k in range(tps):
        w_block = lax.dynamic_slice_in_dim(out_weight, (tp - k) % tps * feats, feats, 1)
        grad_gated = grad_gated + lax.dot_general(
            og[k], w_block, (((1,), (1,)), ((), ())), preferred_element_type=F32
        )
    late = lax.optimization_barrier(
        (outer_gate, inner_gate, values, residues, log_decay, grad_gated, *y_parts)
    )
    outer_gate, inner_gate, values, residues, log_decay, grad_gated = late[:6]
    outer_f = outer_gate.astype(F32)
    inner_f = inner_gate.astype(F32)
    value_f = values.astype(F32)
    u = inner_f * value_f
    rate = jnp.exp(log_decay)
    norm = jnp.sqrt(-jnp.expm1(-2.0 * rate))
    gain = residues * norm
    fall = jnp.exp(-rate[:, None, :] * rows)
    rise = jnp.exp(-rate[:, None, :] * (block - rows))
    fall_block = jnp.exp(-rate * block)
    gc = grad_gated * outer_f
    grad_outer = (grad_gated * gated).astype(BF16)

    g_re, g_im = spectrum(forward, gc)
    corr_local = back(inverse, h_re * g_re + h_im * g_im, h_re * g_im - h_im * g_re)
    lags = back(inverse, u_re * g_re + u_im * g_im, u_re * g_im - u_im * g_re)
    fg = fall * gc[None]
    g_st = jnp.sum(fg, 1)
    g_lag = jnp.sum(fg * rows, 1)
    fl = fall * lags[None]
    sum_a = g_st * x_in + jnp.sum(fl, 1)
    sum_b = g_lag * x_in + g_st * x_lag + jnp.sum(fl * rows, 1)
    sum_skip = jnp.sum(gc * u, 0, keepdims=True)
    mine_g = jnp.concatenate([g_st, sum_a, sum_b, sum_skip], 0)
    theirs_g = swap_core(mine_g)
    later = jnp.where(core == 0, theirs_g[:modes], mine_g[:modes])
    mine_h, theirs_h = my_half(mine_g), my_half(theirs_g)
    early_h = jnp.where(core == 0, mine_h[:modes], theirs_h[:modes])
    total_g = early_h + decay_h * my_half(later)
    sent = jnp.concatenate([total_g, mine_h[modes:] + theirs_h[modes:]], 0).astype(BF16)
    got = of_plane(sent).astype(F32)
    plane_h = jnp.sum(weights(place >= 0, place)[0] * got[:, :modes], 0)
    plane_sums = jnp.sum(got[:, modes:], 0)
    plane_g = jnp.concatenate([plane_h, plane_sums], 0)
    h_half = jnp.sum(weights(place > zz, place - zz - 1)[0] * got[:, :modes], 0)
    y_h, sums_half = 0.0, plane_sums
    for k in range(1, ny):
        came = shift_y(plane_g, -k)
        w = jnp.exp(-rate_h * float(per_plane * (k - 1)))
        y_h = y_h + jnp.where(yy + k < ny, w * came[:modes], 0.0)
        sums_half = sums_half + came[modes:]
    h_half = h_half + jnp.exp(-rate_h * (per_pair * (nz - 1 - zz)).astype(F32)) * y_h
    final = both_halves(jnp.concatenate([h_half, sums_half], 0))
    h_pair = final[:modes]
    h_in = jnp.where(core == 0, later + fall_block * h_pair, h_pair)
    tot_a, tot_b = final[modes : 2 * modes], final[2 * modes : 3 * modes]
    grad_skip = final[3 * modes]
    grad_residues = norm * tot_a
    grad_decay = rate * residues * (jnp.exp(-2.0 * rate) / norm * tot_a - norm * tot_b)
    corr_in = corr_local + jnp.sum((gain * h_in)[:, None, :] * rise, 0)
    grad_mixed = corr_in + skip_gain[None, :] * gc
    grad_inner = (grad_mixed * value_f).astype(BF16)
    grad_values = (grad_mixed * inner_f).astype(BF16)

    over_z = lax.all_to_all(summed_y, "ctx", 0, 0, tiled=True, axis_index_groups=z_groups)
    grad_weight = jnp.sum(over_z.astype(F32), 0)
    return (
        mixed,
        grad_outer,
        grad_inner,
        grad_values,
        grad_weight,
        grad_skip,
        grad_residues,
        grad_decay,
    )


def solution(mesh):
    placed = (
        P("ctx", "tp"),
        P("ctx", "tp"),
        P("ctx", "tp"),
        P(None, "tp"),
        P(None, "tp"),
        P("tp"),
        P("tp", None),
        P("ctx", "tp"),
    )

    return jax.shard_map(
        body,
        mesh=mesh,
        in_specs=placed,
        out_specs=(
            P("ctx", "tp"),
            P("ctx", "tp"),
            P("ctx", "tp"),
            P("ctx", "tp"),
            P("tp", "ctx"),
            P("tp"),
            P(None, "tp"),
            P(None, "tp"),
        ),
        check_vma=False,
    )
```

```python
import jax
import jax.numpy as jnp
import numpy as np
from jax import lax
from jax.experimental import pallas as pl
from jax.experimental.layout import Layout, with_layout_constraint
from jax.experimental.pallas import tpu as pltpu
from jax.sharding import PartitionSpec as P

F32 = jnp.float32
BF16 = jnp.bfloat16
EXACT = lax.Precision.HIGHEST


def dft_tables(block):
    size = 2 * block
    freqs = np.arange(block + 1)
    rows = np.arange(block)
    angles = 2.0 * np.pi * (freqs[:, None] * rows[None, :] % size) / size
    forward = np.concatenate([np.cos(angles), -np.sin(angles)], axis=0)
    weight = np.where((freqs == 0) | (freqs == block), 1.0, 2.0)[:, None] / size
    inverse = np.concatenate([weight * np.cos(angles), -weight * np.sin(angles)], axis=0).T
    return jnp.asarray(forward, F32), jnp.asarray(inverse, F32)


def spectrum(forward, rows):
    both = jnp.dot(forward, rows, precision=EXACT, preferred_element_type=F32)
    half = both.shape[0] // 2
    return both[:half], both[half:]


def back(inverse, real_part, imag_part):
    return jnp.dot(
        inverse, jnp.concatenate([real_part, imag_part], 0), precision=EXACT, preferred_element_type=F32
    )


def row_major(a):
    return with_layout_constraint(a, Layout(major_to_minor=tuple(range(a.ndim))))


def in_vmem(count):
    return [pl.BlockSpec(memory_space=pltpu.VMEM)] * count


def weight_parts(turns, result, result_other, blocks, taken, width):
    count = len(blocks)
    tokens, chans = result.shape
    tiles = blocks[0].shape[1] // (2 * width)

    def kernel(turns_ref, *refs):
        mine_ref, other_ref = refs[:2]
        block_refs, taken_refs = refs[2 : 2 + count], refs[2 + count : 2 + 2 * count]
        out_refs = refs[2 + 2 * count : 2 + 3 * count]
        all_ref, part_ref, in_sems, out_sems = refs[2 + 3 * count :]
        core = turns_ref[0]
        for k in range(count):
            for i in range(tiles):
                at = pl.multiple_of((2 * i + core) * width, width)
                lanes = pl.ds(i * width, width)
                for half, source in enumerate((block_refs[k], taken_refs[k])):
                    pltpu.make_async_copy(
                        source.at[:, pl.ds(at, width)],
                        all_ref.at[k, pl.ds(half * tokens, tokens), lanes],
                        in_sems.at[k],
                    ).start()
        left = jnp.concatenate([mine_ref[...], other_ref[...]], 0).T
        for k in range(count):
            pltpu.make_async_copy(all_ref.at[k], all_ref.at[k], in_sems.at[k]).wait()
        for s in range(count):
            part = jnp.dot(
                left, all_ref[(turns_ref[1] - s + count) % count], preferred_element_type=F32
            ).astype(BF16)
            for i in range(tiles):
                part_ref[s, i] = part[:, i * width : (i + 1) * width]
            pltpu.make_async_copy(part_ref.at[s], out_refs[s], out_sems.at[s]).start()
        for s in range(count):
            pltpu.make_async_copy(part_ref.at[s], out_refs[s], out_sems.at[s]).wait()

    return pl.pallas_call(
        kernel,
        out_shape=[jax.ShapeDtypeStruct((tiles, chans, width), BF16)] * count,
        in_specs=[pl.BlockSpec(memory_space=pltpu.SMEM)]
        + in_vmem(2)
        + [pl.BlockSpec(memory_space=pl.ANY)] * (2 * count),
        out_specs=[pl.BlockSpec(memory_space=pl.ANY)] * count,
        scratch_shapes=[
            pltpu.VMEM((count, 2 * tokens, tiles * width), BF16),
            pltpu.VMEM((count, tiles, chans, width), BF16),
            pltpu.SemaphoreType.DMA((count,)),
            pltpu.SemaphoreType.DMA((count,)),
        ],
    )(turns, result, result_other, *blocks, *taken)


def projections(turns, result, blocks, weight):
    count = len(blocks)
    tokens, feats = blocks[0].shape
    chans = result.shape[1]

    def kernel(turns_ref, result_ref, *refs):
        block_refs, weight_ref = refs[:count], refs[count]
        grad_ref, piece_refs = refs[count + 1], refs[count + 2 :]
        for j in range(count):

            @pl.when(pl.program_id(0) == j)
            def _():
                w = weight_ref[...]
                piece_refs[j][...] = jnp.dot(
                    result_ref[...], w, preferred_element_type=F32
                ).astype(BF16)
                term = lax.dot_general(
                    block_refs[-j % count][...],
                    w,
                    (((1,), (1,)), ((), ())),
                    preferred_element_type=F32,
                )
                grad_ref[...] = term if j == 0 else grad_ref[...] + term

    def whole(shape):
        return pl.BlockSpec(shape, lambda j, turns_ref: (0, 0))

    return pl.pallas_call(
        kernel,
        out_shape=[jax.ShapeDtypeStruct((tokens, chans), F32)]
        + [jax.ShapeDtypeStruct((tokens, feats), BF16)] * count,
        grid_spec=pltpu.PrefetchScalarGridSpec(
            num_scalar_prefetch=1,
            grid=(count,),
            in_specs=[whole((tokens, chans))]
            + [whole((tokens, feats))] * count
            + [pl.BlockSpec((chans, feats), lambda j, turns_ref: (0, (turns_ref[2] + j) % count))],
            out_specs=[whole((tokens, chans))] + [whole((tokens, feats))] * count,
        ),
    )(turns, result, *blocks, weight)


def body(outer_gate, inner_gate, values, residues, log_decay, skip_gain, out_weight, out_grad):
    ctx = lax.axis_size("ctx")
    tps = lax.axis_size("tp")
    dev = lax.axis_index("ctx")
    tp = lax.axis_index("tp")
    block, chans = outer_gate.shape
    modes = residues.shape[0]
    feats = out_grad.shape[1]
    ny = tps
    nz = ctx // (2 * ny)
    core = dev % 2
    pair = dev // 2
    zz = pair % nz
    pairs = ctx // 2
    yy = dev // (2 * nz)
    width = feats // (2 * nz)

    def swap_core(a):
        return lax.ppermute(a, "ctx", [(i, i ^ 1) for i in range(ctx)])

    def shift_tp(a, k):
        return lax.ppermute(a, "tp", [(i, (i + k) % tps) for i in range(tps)])

    def shift_y(a, k):
        per = 2 * nz
        return lax.ppermute(a, "ctx", [(i, (i // per + k) % ny * per + i % per) for i in range(ctx)])

    z_groups = [[i * 2 * nz + j * 2 + k for j in range(nz)] for i in range(ny) for k in range(2)]

    def of_plane(a):
        copies = jnp.broadcast_to(a[None], (nz, *a.shape))
        return lax.all_to_all(copies, "ctx", 0, 0, tiled=True, axis_index_groups=z_groups)

    def of_pairs(a):
        copies = jnp.broadcast_to(a[None], (pairs, *a.shape))
        groups = [[2 * i + j for i in range(pairs)] for j in range(2)]
        return lax.all_to_all(copies, "ctx", 0, 0, tiled=True, axis_index_groups=groups)

    og = [out_grad] + [row_major(shift_tp(out_grad, k)) for k in range(1, tps)]

    u = inner_gate.astype(F32) * values.astype(F32)
    rate = jnp.exp(log_decay)
    rows = jnp.arange(block, dtype=F32)[None, :, None]
    rate3 = rate[:, None, :]
    rise = jnp.exp(-rate3 * (block - rows))
    fall_block = jnp.exp(-rate * block)

    lead = rise * u[None]
    st = jnp.sum(lead, 1)
    st_lag = jnp.sum(lead * (block - rows), 1)
    mine = jnp.concatenate([st, st_lag], 0)
    theirs = swap_core(mine)
    first = jnp.where(core == 0, mine, theirs)
    second = jnp.where(core == 0, theirs, mine)
    half = chans // 2

    def my_half(a):
        return lax.dynamic_slice_in_dim(a, core * half, half, a.ndim - 1)

    def both_halves(a):
        other = swap_core(a)
        return jnp.concatenate(
            [jnp.where(core == 0, a, other), jnp.where(core == 0, other, a)], a.ndim - 1
        )

    rate_h = my_half(rate)
    decay_h = jnp.exp(-rate_h * block)
    f_h, s_h = my_half(first), my_half(second)
    total = decay_h * f_h[:modes] + s_h[:modes]
    total_lag = decay_h * (block * f_h[:modes] + f_h[modes:]) + s_h[modes:]
    to_send = jnp.concatenate([total, total_lag], 0).astype(BF16)
    gathered = of_pairs(to_send).astype(F32)
    place = jnp.arange(nz, dtype=jnp.int32)
    every = jnp.arange(pairs, dtype=jnp.int32)
    per_pair = 2 * block
    per_plane = per_pair * nz

    def weights(which, gap):
        gap = jnp.where(which, gap, 0).astype(F32)[:, None, None] * per_pair
        return jnp.where(which[:, None, None], jnp.exp(-rate_h[None] * gap), 0.0), gap

    w, gap = weights(every < pair, pair - 1 - every)
    base = gathered[:, :modes]
    in_h = jnp.sum(w * base, 0)
    in_lag_h = jnp.sum(w * (gap * base + gathered[:, modes:]), 0)
    incoming = both_halves(jnp.concatenate([in_h, in_lag_h], 0))
    in_pair, in_pair_lag = incoming[:modes], incoming[modes:]
    x_in = jnp.where(core == 0, in_pair, fall_block * in_pair + first[:modes])
    x_lag = jnp.where(
        core == 0, in_pair_lag, fall_block * (in_pair_lag + block * in_pair) + first[modes:]
    )

    outer_gate, inner_gate, values, residues, log_decay, x_in, x_lag = lax.optimization_barrier(
        (outer_gate, inner_gate, values, residues, log_decay, x_in, x_lag)
    )
    rate = jnp.exp(log_decay)
    gain = residues * jnp.sqrt(-jnp.expm1(-2.0 * rate))
    fall = jnp.exp(-rate[:, None, :] * rows)
    outer_f = outer_gate.astype(F32)
    u = inner_gate.astype(F32) * values.astype(F32)

    forward, inverse = dft_tables(block)
    response = jnp.sum(gain[:, None, :] * fall, 0)
    h_re, h_im = spectrum(forward, response)
    u_re, u_im = spectrum(forward, u)
    conv_local = back(inverse, h_re * u_re - h_im * u_im, h_re * u_im + h_im * u_re)
    conv_out = conv_local + jnp.sum((gain * x_in)[:, None, :] * fall, 0)
    gated = conv_out + skip_gain[None, :] * u
    result = row_major((outer_f * gated).astype(BF16))

    turns = jnp.stack([core, (tp - yy) % tps, tp]).astype(jnp.int32)
    taken = [row_major(swap_core(a)) for a in og]
    result_other = swap_core(result)
    y_parts = weight_parts(turns, result, result_other, og, taken, width)
    over_y = [y_parts[0]] + [shift_y(y_parts[s], s) for s in range(1, ny)]
    summed_y = sum(a.astype(F32) for a in over_y).astype(BF16)

    late = lax.optimization_barrier((result, gated, *y_parts))
    result, gated = late[:2]
    grad_gated, *pieces = projections(turns, result, og, out_weight)
    mixed = pieces[0].astype(F32)
    for k in range(1, tps):
        piece = shift_tp(pieces[k], k)
        mixed = mixed + piece.astype(F32)
    mixed = mixed.astype(BF16)

    late = lax.optimization_barrier(
        (outer_gate, inner_gate, values, residues, log_decay, grad_gated, *y_parts)
    )
    outer_gate, inner_gate, values, residues, log_decay, grad_gated = late[:6]
    outer_f = outer_gate.astype(F32)
    inner_f = inner_gate.astype(F32)
    value_f = values.astype(F32)
    u = inner_f * value_f
    rate = jnp.exp(log_decay)
    norm = jnp.sqrt(-jnp.expm1(-2.0 * rate))
    gain = residues * norm
    fall = jnp.exp(-rate[:, None, :] * rows)
    rise = jnp.exp(-rate[:, None, :] * (block - rows))
    fall_block = jnp.exp(-rate * block)
    gc = grad_gated * outer_f
    grad_outer = (grad_gated * gated).astype(BF16)

    g_re, g_im = spectrum(forward, gc)
    corr_local = back(inverse, h_re * g_re + h_im * g_im, h_re * g_im - h_im * g_re)
    lags = back(inverse, u_re * g_re + u_im * g_im, u_re * g_im - u_im * g_re)
    fg = fall * gc[None]
    g_st = jnp.sum(fg, 1)
    g_lag = jnp.sum(fg * rows, 1)
    fl = fall * lags[None]
    sum_a = g_st * x_in + jnp.sum(fl, 1)
    sum_b = g_lag * x_in + g_st * x_lag + jnp.sum(fl * rows, 1)
    sum_skip = jnp.sum(gc * u, 0, keepdims=True)
    mine_g = jnp.concatenate([g_st, sum_a, sum_b, sum_skip], 0)
    theirs_g = swap_core(mine_g)
    later = jnp.where(core == 0, theirs_g[:modes], mine_g[:modes])
    mine_h, theirs_h = my_half(mine_g), my_half(theirs_g)
    early_h = jnp.where(core == 0, mine_h[:modes], theirs_h[:modes])
    total_g = early_h + decay_h * my_half(later)
    sent = jnp.concatenate([total_g, mine_h[modes:] + theirs_h[modes:]], 0).astype(BF16)
    got = of_plane(sent).astype(F32)
    plane_h = jnp.sum(weights(place >= 0, place)[0] * got[:, :modes], 0)
    plane_sums = jnp.sum(got[:, modes:], 0)
    plane_g = jnp.concatenate([plane_h, plane_sums], 0)
    h_half = jnp.sum(weights(place > zz, place - zz - 1)[0] * got[:, :modes], 0)
    y_h, sums_half = 0.0, plane_sums
    for k in range(1, ny):
        came = shift_y(plane_g, -k)
        w = jnp.exp(-rate_h * float(per_plane * (k - 1)))
        y_h = y_h + jnp.where(yy + k < ny, w * came[:modes], 0.0)
        sums_half = sums_half + came[modes:]
    h_half = h_half + jnp.exp(-rate_h * (per_pair * (nz - 1 - zz)).astype(F32)) * y_h
    final = both_halves(jnp.concatenate([h_half, sums_half], 0))
    h_pair = final[:modes]
    h_in = jnp.where(core == 0, later + fall_block * h_pair, h_pair)
    tot_a, tot_b = final[modes : 2 * modes], final[2 * modes : 3 * modes]
    grad_skip = final[3 * modes]
    grad_residues = norm * tot_a
    grad_decay = rate * residues * (jnp.exp(-2.0 * rate) / norm * tot_a - norm * tot_b)
    corr_in = corr_local + jnp.sum((gain * h_in)[:, None, :] * rise, 0)
    grad_mixed = corr_in + skip_gain[None, :] * gc
    grad_inner = (grad_mixed * value_f).astype(BF16)
    grad_values = (grad_mixed * inner_f).astype(BF16)

    over_z = lax.all_to_all(summed_y, "ctx", 0, 0, tiled=True, axis_index_groups=z_groups)
    grad_weight = jnp.sum(over_z.astype(F32), 0)
    return (
        mixed,
        grad_outer,
        grad_inner,
        grad_values,
        grad_weight,
        grad_skip,
        grad_residues,
        grad_decay,
    )


def solution(mesh):
    placed = (
        P("ctx", "tp"),
        P("ctx", "tp"),
        P("ctx", "tp"),
        P(None, "tp"),
        P(None, "tp"),
        P("tp"),
        P("tp", None),
        P("ctx", "tp"),
    )

    return jax.shard_map(
        body,
        mesh=mesh,
        in_specs=placed,
        out_specs=(
            P("ctx", "tp"),
            P("ctx", "tp"),
            P("ctx", "tp"),
            P("ctx", "tp"),
            P("tp", "ctx"),
            P("tp"),
            P(None, "tp"),
            P(None, "tp"),
        ),
        check_vma=False,
    )
```

```python
import jax
import jax.numpy as jnp
import numpy as np
from jax import lax
from jax.experimental import pallas as pl
from jax.experimental.layout import Layout, with_layout_constraint
from jax.experimental.pallas import tpu as pltpu
from jax.sharding import PartitionSpec as P

F32 = jnp.float32
BF16 = jnp.bfloat16
EXACT = lax.Precision.HIGHEST


def dft_tables(block):
    size = 2 * block
    freqs = np.arange(block + 1)
    rows = np.arange(block)
    angles = 2.0 * np.pi * (freqs[:, None] * rows[None, :] % size) / size
    forward = np.concatenate([np.cos(angles), -np.sin(angles)], axis=0)
    weight = np.where((freqs == 0) | (freqs == block), 1.0, 2.0)[:, None] / size
    inverse = np.concatenate([weight * np.cos(angles), -weight * np.sin(angles)], axis=0).T
    return jnp.asarray(forward, F32), jnp.asarray(inverse, F32)


def spectrum(forward, rows):
    both = jnp.dot(forward, rows, precision=EXACT, preferred_element_type=F32)
    half = both.shape[0] // 2
    return both[:half], both[half:]


def back(inverse, real_part, imag_part):
    return jnp.dot(
        inverse, jnp.concatenate([real_part, imag_part], 0), precision=EXACT, preferred_element_type=F32
    )


def row_major(a):
    return with_layout_constraint(a, Layout(major_to_minor=tuple(range(a.ndim))))


def in_vmem(count):
    return [pl.BlockSpec(memory_space=pltpu.VMEM)] * count


def weight_parts(turns, result, result_other, blocks, taken, width):
    count = len(blocks)
    tokens, chans = result.shape
    tiles = blocks[0].shape[1] // (2 * width)

    def kernel(turns_ref, *refs):
        mine_ref, other_ref = refs[:2]
        block_refs, taken_refs = refs[2 : 2 + count], refs[2 + count : 2 + 2 * count]
        out_refs = refs[2 + 2 * count : 2 + 3 * count]
        all_ref, part_ref, in_sems, out_sems = refs[2 + 3 * count :]
        core = turns_ref[0]
        for k in range(count):
            for i in range(tiles):
                at = pl.multiple_of((2 * i + core) * width, width)
                lanes = pl.ds(i * width, width)
                for half, source in enumerate((block_refs[k], taken_refs[k])):
                    pltpu.make_async_copy(
                        source.at[:, pl.ds(at, width)],
                        all_ref.at[k, pl.ds(half * tokens, tokens), lanes],
                        in_sems.at[k],
                    ).start()
        left = jnp.concatenate([mine_ref[...], other_ref[...]], 0).T
        for k in range(count):
            pltpu.make_async_copy(all_ref.at[k], all_ref.at[k], in_sems.at[k]).wait()
        for s in range(count):
            part = jnp.dot(
                left, all_ref[(turns_ref[1] - s + count) % count], preferred_element_type=F32
            ).astype(BF16)
            for i in range(tiles):
                part_ref[s, i] = part[:, i * width : (i + 1) * width]
            pltpu.make_async_copy(part_ref.at[s], out_refs[s], out_sems.at[s]).start()
        for s in range(count):
            pltpu.make_async_copy(part_ref.at[s], out_refs[s], out_sems.at[s]).wait()

    return pl.pallas_call(
        kernel,
        out_shape=[jax.ShapeDtypeStruct((tiles, chans, width), BF16)] * count,
        in_specs=[pl.BlockSpec(memory_space=pltpu.SMEM)]
        + in_vmem(2)
        + [pl.BlockSpec(memory_space=pl.ANY)] * (2 * count),
        out_specs=[pl.BlockSpec(memory_space=pl.ANY)] * count,
        scratch_shapes=[
            pltpu.VMEM((count, 2 * tokens, tiles * width), BF16),
            pltpu.VMEM((count, tiles, chans, width), BF16),
            pltpu.SemaphoreType.DMA((count,)),
            pltpu.SemaphoreType.DMA((count,)),
        ],
        compiler_params=pltpu.CompilerParams(vmem_limit_bytes=12 * 2**20),
    )(turns, result, result_other, *blocks, *taken)


def projections(turns, result, blocks, weight):
    count = len(blocks)
    tokens, feats = blocks[0].shape
    chans = result.shape[1]

    def kernel(turns_ref, result_ref, *refs):
        block_refs, weight_ref = refs[:count], refs[count]
        grad_ref, piece_refs = refs[count + 1], refs[count + 2 :]
        grad = None
        for j in range(count):
            at = pl.multiple_of((turns_ref[2] + j) % count * feats, feats)
            w = weight_ref[:, pl.ds(at, feats)]
            piece_refs[j][...] = jnp.dot(result_ref[...], w, preferred_element_type=F32).astype(
                BF16
            )
            term = lax.dot_general(
                block_refs[-j % count][...],
                w,
                (((1,), (1,)), ((), ())),
                preferred_element_type=F32,
            )
            grad = term if j == 0 else grad + term
        grad_ref[...] = grad

    return pl.pallas_call(
        kernel,
        out_shape=[jax.ShapeDtypeStruct((tokens, chans), F32)]
        + [jax.ShapeDtypeStruct((tokens, feats), BF16)] * count,
        in_specs=[pl.BlockSpec(memory_space=pltpu.SMEM)] + in_vmem(2 + count),
        out_specs=in_vmem(1 + count),
        compiler_params=pltpu.CompilerParams(vmem_limit_bytes=24 * 2**20),
    )(turns, result, *blocks, weight)


def body(outer_gate, inner_gate, values, residues, log_decay, skip_gain, out_weight, out_grad):
    ctx = lax.axis_size("ctx")
    tps = lax.axis_size("tp")
    dev = lax.axis_index("ctx")
    tp = lax.axis_index("tp")
    block, chans = outer_gate.shape
    modes = residues.shape[0]
    feats = out_grad.shape[1]
    ny = tps
    nz = ctx // (2 * ny)
    core = dev % 2
    pair = dev // 2
    zz = pair % nz
    pairs = ctx // 2
    yy = dev // (2 * nz)
    width = feats // (2 * nz)

    def swap_core(a):
        return lax.ppermute(a, "ctx", [(i, i ^ 1) for i in range(ctx)])

    def shift_tp(a, k):
        return lax.ppermute(a, "tp", [(i, (i + k) % tps) for i in range(tps)])

    def shift_y(a, k):
        per = 2 * nz
        return lax.ppermute(a, "ctx", [(i, (i // per + k) % ny * per + i % per) for i in range(ctx)])

    z_groups = [[i * 2 * nz + j * 2 + k for j in range(nz)] for i in range(ny) for k in range(2)]

    def of_plane(a):
        copies = jnp.broadcast_to(a[None], (nz, *a.shape))
        return lax.all_to_all(copies, "ctx", 0, 0, tiled=True, axis_index_groups=z_groups)

    def of_pairs(a):
        copies = jnp.broadcast_to(a[None], (pairs, *a.shape))
        groups = [[2 * i + j for i in range(pairs)] for j in range(2)]
        return lax.all_to_all(copies, "ctx", 0, 0, tiled=True, axis_index_groups=groups)

    og = [out_grad] + [row_major(shift_tp(out_grad, k)) for k in range(1, tps)]

    u = inner_gate.astype(F32) * values.astype(F32)
    rate = jnp.exp(log_decay)
    rows = jnp.arange(block, dtype=F32)[None, :, None]
    rate3 = rate[:, None, :]
    rise = jnp.exp(-rate3 * (block - rows))
    fall_block = jnp.exp(-rate * block)

    lead = rise * u[None]
    st = jnp.sum(lead, 1)
    st_lag = jnp.sum(lead * (block - rows), 1)
    mine = jnp.concatenate([st, st_lag], 0)
    theirs = swap_core(mine)
    first = jnp.where(core == 0, mine, theirs)
    second = jnp.where(core == 0, theirs, mine)
    half = chans // 2

    def my_half(a):
        return lax.dynamic_slice_in_dim(a, core * half, half, a.ndim - 1)

    def both_halves(a):
        other = swap_core(a)
        return jnp.concatenate(
            [jnp.where(core == 0, a, other), jnp.where(core == 0, other, a)], a.ndim - 1
        )

    rate_h = my_half(rate)
    decay_h = jnp.exp(-rate_h * block)
    f_h, s_h = my_half(first), my_half(second)
    total = decay_h * f_h[:modes] + s_h[:modes]
    total_lag = decay_h * (block * f_h[:modes] + f_h[modes:]) + s_h[modes:]
    to_send = jnp.concatenate([total, total_lag], 0).astype(BF16)
    gathered = of_pairs(to_send).astype(F32)
    place = jnp.arange(nz, dtype=jnp.int32)
    every = jnp.arange(pairs, dtype=jnp.int32)
    per_pair = 2 * block
    per_plane = per_pair * nz

    def weights(which, gap):
        gap = jnp.where(which, gap, 0).astype(F32)[:, None, None] * per_pair
        return jnp.where(which[:, None, None], jnp.exp(-rate_h[None] * gap), 0.0), gap

    w, gap = weights(every < pair, pair - 1 - every)
    base = gathered[:, :modes]
    in_h = jnp.sum(w * base, 0)
    in_lag_h = jnp.sum(w * (gap * base + gathered[:, modes:]), 0)
    incoming = both_halves(jnp.concatenate([in_h, in_lag_h], 0))
    in_pair, in_pair_lag = incoming[:modes], incoming[modes:]
    x_in = jnp.where(core == 0, in_pair, fall_block * in_pair + first[:modes])
    x_lag = jnp.where(
        core == 0, in_pair_lag, fall_block * (in_pair_lag + block * in_pair) + first[modes:]
    )

    outer_gate, inner_gate, values, residues, log_decay, x_in, x_lag = lax.optimization_barrier(
        (outer_gate, inner_gate, values, residues, log_decay, x_in, x_lag)
    )
    rate = jnp.exp(log_decay)
    gain = residues * jnp.sqrt(-jnp.expm1(-2.0 * rate))
    fall = jnp.exp(-rate[:, None, :] * rows)
    outer_f = outer_gate.astype(F32)
    u = inner_gate.astype(F32) * values.astype(F32)

    forward, inverse = dft_tables(block)
    response = jnp.sum(gain[:, None, :] * fall, 0)
    h_re, h_im = spectrum(forward, response)
    u_re, u_im = spectrum(forward, u)
    conv_local = back(inverse, h_re * u_re - h_im * u_im, h_re * u_im + h_im * u_re)
    conv_out = conv_local + jnp.sum((gain * x_in)[:, None, :] * fall, 0)
    gated = conv_out + skip_gain[None, :] * u
    result = row_major((outer_f * gated).astype(BF16))

    turns = jnp.stack([core, (tp - yy) % tps, tp]).astype(jnp.int32)
    taken = [row_major(swap_core(a)) for a in og]
    result_other = swap_core(result)
    y_parts = weight_parts(turns, result, result_other, og, taken, width)
    over_y = [y_parts[0]] + [shift_y(y_parts[s], s) for s in range(1, ny)]
    summed_y = sum(a.astype(F32) for a in over_y).astype(BF16)

    late = lax.optimization_barrier((result, gated, *y_parts))
    result, gated = late[:2]
    grad_gated, *pieces = projections(turns, result, og, out_weight)
    mixed = pieces[0].astype(F32)
    for k in range(1, tps):
        piece = shift_tp(pieces[k], k)
        mixed = mixed + piece.astype(F32)
    mixed = mixed.astype(BF16)

    late = lax.optimization_barrier(
        (outer_gate, inner_gate, values, residues, log_decay, grad_gated, *y_parts)
    )
    outer_gate, inner_gate, values, residues, log_decay, grad_gated = late[:6]
    outer_f = outer_gate.astype(F32)
    inner_f = inner_gate.astype(F32)
    value_f = values.astype(F32)
    u = inner_f * value_f
    rate = jnp.exp(log_decay)
    norm = jnp.sqrt(-jnp.expm1(-2.0 * rate))
    gain = residues * norm
    fall = jnp.exp(-rate[:, None, :] * rows)
    rise = jnp.exp(-rate[:, None, :] * (block - rows))
    fall_block = jnp.exp(-rate * block)
    gc = grad_gated * outer_f
    grad_outer = (grad_gated * gated).astype(BF16)

    g_re, g_im = spectrum(forward, gc)
    corr_local = back(inverse, h_re * g_re + h_im * g_im, h_re * g_im - h_im * g_re)
    lags = back(inverse, u_re * g_re + u_im * g_im, u_re * g_im - u_im * g_re)
    fg = fall * gc[None]
    g_st = jnp.sum(fg, 1)
    g_lag = jnp.sum(fg * rows, 1)
    fl = fall * lags[None]
    sum_a = g_st * x_in + jnp.sum(fl, 1)
    sum_b = g_lag * x_in + g_st * x_lag + jnp.sum(fl * rows, 1)
    sum_skip = jnp.sum(gc * u, 0, keepdims=True)
    mine_g = jnp.concatenate([g_st, sum_a, sum_b, sum_skip], 0)
    theirs_g = swap_core(mine_g)
    later = jnp.where(core == 0, theirs_g[:modes], mine_g[:modes])
    mine_h, theirs_h = my_half(mine_g), my_half(theirs_g)
    early_h = jnp.where(core == 0, mine_h[:modes], theirs_h[:modes])
    total_g = early_h + decay_h * my_half(later)
    sent = jnp.concatenate([total_g, mine_h[modes:] + theirs_h[modes:]], 0).astype(BF16)
    got = of_plane(sent).astype(F32)
    plane_h = jnp.sum(weights(place >= 0, place)[0] * got[:, :modes], 0)
    plane_sums = jnp.sum(got[:, modes:], 0)
    plane_g = jnp.concatenate([plane_h, plane_sums], 0)
    h_half = jnp.sum(weights(place > zz, place - zz - 1)[0] * got[:, :modes], 0)
    y_h, sums_half = 0.0, plane_sums
    for k in range(1, ny):
        came = shift_y(plane_g, -k)
        w = jnp.exp(-rate_h * float(per_plane * (k - 1)))
        y_h = y_h + jnp.where(yy + k < ny, w * came[:modes], 0.0)
        sums_half = sums_half + came[modes:]
    h_half = h_half + jnp.exp(-rate_h * (per_pair * (nz - 1 - zz)).astype(F32)) * y_h
    final = both_halves(jnp.concatenate([h_half, sums_half], 0))
    h_pair = final[:modes]
    h_in = jnp.where(core == 0, later + fall_block * h_pair, h_pair)
    tot_a, tot_b = final[modes : 2 * modes], final[2 * modes : 3 * modes]
    grad_skip = final[3 * modes]
    grad_residues = norm * tot_a
    grad_decay = rate * residues * (jnp.exp(-2.0 * rate) / norm * tot_a - norm * tot_b)
    corr_in = corr_local + jnp.sum((gain * h_in)[:, None, :] * rise, 0)
    grad_mixed = corr_in + skip_gain[None, :] * gc
    grad_inner = (grad_mixed * value_f).astype(BF16)
    grad_values = (grad_mixed * inner_f).astype(BF16)

    over_z = lax.all_to_all(summed_y, "ctx", 0, 0, tiled=True, axis_index_groups=z_groups)
    grad_weight = jnp.sum(over_z.astype(F32), 0)
    return (
        mixed,
        grad_outer,
        grad_inner,
        grad_values,
        grad_weight,
        grad_skip,
        grad_residues,
        grad_decay,
    )


def solution(mesh):
    placed = (
        P("ctx", "tp"),
        P("ctx", "tp"),
        P("ctx", "tp"),
        P(None, "tp"),
        P(None, "tp"),
        P("tp"),
        P("tp", None),
        P("ctx", "tp"),
    )

    return jax.shard_map(
        body,
        mesh=mesh,
        in_specs=placed,
        out_specs=(
            P("ctx", "tp"),
            P("ctx", "tp"),
            P("ctx", "tp"),
            P("ctx", "tp"),
            P("tp", "ctx"),
            P("tp"),
            P(None, "tp"),
            P(None, "tp"),
        ),
        check_vma=False,
    )
```

```python
import jax
import jax.numpy as jnp
import numpy as np
from jax import lax
from jax.experimental import pallas as pl
from jax.experimental.layout import Layout, with_layout_constraint
from jax.experimental.pallas import tpu as pltpu
from jax.sharding import PartitionSpec as P

F32 = jnp.float32
BF16 = jnp.bfloat16
EXACT = lax.Precision.HIGHEST


def dft_tables(block):
    size = 2 * block
    freqs = np.arange(block + 1)
    rows = np.arange(block)
    angles = 2.0 * np.pi * (freqs[:, None] * rows[None, :] % size) / size
    forward = np.concatenate([np.cos(angles), -np.sin(angles)], axis=0)
    weight = np.where((freqs == 0) | (freqs == block), 1.0, 2.0)[:, None] / size
    inverse = np.concatenate([weight * np.cos(angles), -weight * np.sin(angles)], axis=0).T
    return jnp.asarray(forward, F32), jnp.asarray(inverse, F32)


def spectrum(forward, rows):
    both = jnp.dot(forward, rows, precision=EXACT, preferred_element_type=F32)
    half = both.shape[0] // 2
    return both[:half], both[half:]


def back(inverse, real_part, imag_part):
    return jnp.dot(
        inverse, jnp.concatenate([real_part, imag_part], 0), precision=EXACT, preferred_element_type=F32
    )


def row_major(a):
    return with_layout_constraint(a, Layout(major_to_minor=tuple(range(a.ndim))))


def in_vmem(count):
    return [pl.BlockSpec(memory_space=pltpu.VMEM)] * count


def weight_parts(turns, result, result_other, blocks, taken, width):
    count = len(blocks)
    tokens, chans = result.shape
    tiles = blocks[0].shape[1] // (2 * width)

    def kernel(turns_ref, *refs):
        mine_ref, other_ref = refs[:2]
        block_refs, taken_refs = refs[2 : 2 + count], refs[2 + count : 2 + 2 * count]
        out_refs = refs[2 + 2 * count : 2 + 3 * count]
        all_ref, part_ref, in_sems, out_sems = refs[2 + 3 * count :]
        core = turns_ref[0]
        for k in range(count):
            for i in range(tiles):
                at = pl.multiple_of((2 * i + core) * width, width)
                lanes = pl.ds(i * width, width)
                for half, source in enumerate((block_refs[k], taken_refs[k])):
                    pltpu.make_async_copy(
                        source.at[:, pl.ds(at, width)],
                        all_ref.at[k, pl.ds(half * tokens, tokens), lanes],
                        in_sems.at[k],
                    ).start()
        left = jnp.concatenate([mine_ref[...], other_ref[...]], 0).T
        for k in range(count):
            pltpu.make_async_copy(all_ref.at[k], all_ref.at[k], in_sems.at[k]).wait()
        for s in range(count):
            part = jnp.dot(
                left, all_ref[(turns_ref[1] - s + count) % count], preferred_element_type=F32
            ).astype(BF16)
            for i in range(tiles):
                part_ref[s, i] = part[:, i * width : (i + 1) * width]
            pltpu.make_async_copy(part_ref.at[s], out_refs[s], out_sems.at[s]).start()
        for s in range(count):
            pltpu.make_async_copy(part_ref.at[s], out_refs[s], out_sems.at[s]).wait()

    return pl.pallas_call(
        kernel,
        out_shape=[jax.ShapeDtypeStruct((tiles, chans, width), BF16)] * count,
        in_specs=[pl.BlockSpec(memory_space=pltpu.SMEM)]
        + in_vmem(2)
        + [pl.BlockSpec(memory_space=pl.ANY)] * (2 * count),
        out_specs=[pl.BlockSpec(memory_space=pl.ANY)] * count,
        scratch_shapes=[
            pltpu.VMEM((count, 2 * tokens, tiles * width), BF16),
            pltpu.VMEM((count, tiles, chans, width), BF16),
            pltpu.SemaphoreType.DMA((count,)),
            pltpu.SemaphoreType.DMA((count,)),
        ],
        compiler_params=pltpu.CompilerParams(vmem_limit_bytes=12 * 2**20),
    )(turns, result, result_other, *blocks, *taken)


def gated_gradient(turns, blocks, weight):
    count = len(blocks)
    tokens, feats = blocks[0].shape
    chans = weight.shape[0]

    def kernel(turns_ref, *refs):
        weight_ref, grad_ref = refs[count:]
        grad = None
        for k in range(count):
            at = pl.multiple_of((turns_ref[2] - k + count) % count * feats, feats)
            term = lax.dot_general(
                refs[k][...],
                weight_ref[:, pl.ds(at, feats)],
                (((1,), (1,)), ((), ())),
                preferred_element_type=F32,
            )
            grad = term if k == 0 else grad + term
        grad_ref[...] = grad

    return pl.pallas_call(
        kernel,
        out_shape=jax.ShapeDtypeStruct((tokens, chans), F32),
        in_specs=[pl.BlockSpec(memory_space=pltpu.SMEM)] + in_vmem(1 + count),
        out_specs=in_vmem(1)[0],
        compiler_params=pltpu.CompilerParams(vmem_limit_bytes=16 * 2**20),
    )(turns, *blocks, weight)


def output_pieces(turns, result, weight, count):
    tokens = result.shape[0]
    feats = weight.shape[1] // count

    def kernel(turns_ref, result_ref, weight_ref, *piece_refs):
        for k in range(count):
            at = pl.multiple_of((turns_ref[2] + k) % count * feats, feats)
            piece_refs[k][...] = jnp.dot(
                result_ref[...], weight_ref[:, pl.ds(at, feats)], preferred_element_type=F32
            ).astype(BF16)

    return pl.pallas_call(
        kernel,
        out_shape=[jax.ShapeDtypeStruct((tokens, feats), BF16)] * count,
        in_specs=[pl.BlockSpec(memory_space=pltpu.SMEM)] + in_vmem(2),
        out_specs=in_vmem(count),
        compiler_params=pltpu.CompilerParams(vmem_limit_bytes=16 * 2**20),
    )(turns, result, weight)


def body(outer_gate, inner_gate, values, residues, log_decay, skip_gain, out_weight, out_grad):
    ctx = lax.axis_size("ctx")
    tps = lax.axis_size("tp")
    dev = lax.axis_index("ctx")
    tp = lax.axis_index("tp")
    block, chans = outer_gate.shape
    modes = residues.shape[0]
    feats = out_grad.shape[1]
    ny = tps
    nz = ctx // (2 * ny)
    core = dev % 2
    pair = dev // 2
    pairs = ctx // 2
    yy = dev // (2 * nz)
    width = feats // (2 * nz)

    def swap_core(a):
        return lax.ppermute(a, "ctx", [(i, i ^ 1) for i in range(ctx)])

    def shift_tp(a, k):
        return lax.ppermute(a, "tp", [(i, (i + k) % tps) for i in range(tps)])

    def shift_y(a, k):
        per = 2 * nz
        return lax.ppermute(a, "ctx", [(i, (i // per + k) % ny * per + i % per) for i in range(ctx)])

    z_groups = [[i * 2 * nz + j * 2 + k for j in range(nz)] for i in range(ny) for k in range(2)]

    def of_pairs(a):
        copies = jnp.broadcast_to(a[None], (pairs, *a.shape))
        groups = [[2 * i + j for i in range(pairs)] for j in range(2)]
        return lax.all_to_all(copies, "ctx", 0, 0, tiled=True, axis_index_groups=groups)

    og = [out_grad] + [row_major(shift_tp(out_grad, k)) for k in range(1, tps)]

    u = inner_gate.astype(F32) * values.astype(F32)
    rate = jnp.exp(log_decay)
    rows = jnp.arange(block, dtype=F32)[None, :, None]
    rate3 = rate[:, None, :]
    rise = jnp.exp(-rate3 * (block - rows))
    fall_block = jnp.exp(-rate * block)

    lead = rise * u[None]
    st = jnp.sum(lead, 1)
    st_lag = jnp.sum(lead * (block - rows), 1)
    mine = jnp.concatenate([st, st_lag], 0)
    theirs = swap_core(mine)
    first = jnp.where(core == 0, mine, theirs)
    second = jnp.where(core == 0, theirs, mine)
    half = chans // 2

    def my_half(a):
        return lax.dynamic_slice_in_dim(a, core * half, half, a.ndim - 1)

    def both_halves(a):
        other = swap_core(a)
        return jnp.concatenate(
            [jnp.where(core == 0, a, other), jnp.where(core == 0, other, a)], a.ndim - 1
        )

    rate_h = my_half(rate)
    decay_h = jnp.exp(-rate_h * block)
    f_h, s_h = my_half(first), my_half(second)
    total = decay_h * f_h[:modes] + s_h[:modes]
    total_lag = decay_h * (block * f_h[:modes] + f_h[modes:]) + s_h[modes:]
    to_send = jnp.concatenate([total, total_lag], 0).astype(BF16)
    gathered = of_pairs(to_send).astype(F32)
    every = jnp.arange(pairs, dtype=jnp.int32)
    per_pair = 2 * block

    def weights(which, gap):
        gap = jnp.where(which, gap, 0).astype(F32)[:, None, None] * per_pair
        return jnp.where(which[:, None, None], jnp.exp(-rate_h[None] * gap), 0.0), gap

    w, gap = weights(every < pair, pair - 1 - every)
    base = gathered[:, :modes]
    in_h = jnp.sum(w * base, 0)
    in_lag_h = jnp.sum(w * (gap * base + gathered[:, modes:]), 0)
    incoming = both_halves(jnp.concatenate([in_h, in_lag_h], 0))
    in_pair, in_pair_lag = incoming[:modes], incoming[modes:]
    x_in = jnp.where(core == 0, in_pair, fall_block * in_pair + first[:modes])
    x_lag = jnp.where(
        core == 0, in_pair_lag, fall_block * (in_pair_lag + block * in_pair) + first[modes:]
    )

    outer_gate, inner_gate, values, residues, log_decay, x_in, x_lag = lax.optimization_barrier(
        (outer_gate, inner_gate, values, residues, log_decay, x_in, x_lag)
    )
    rate = jnp.exp(log_decay)
    gain = residues * jnp.sqrt(-jnp.expm1(-2.0 * rate))
    fall = jnp.exp(-rate[:, None, :] * rows)
    outer_f = outer_gate.astype(F32)
    u = inner_gate.astype(F32) * values.astype(F32)

    forward, inverse = dft_tables(block)
    response = jnp.sum(gain[:, None, :] * fall, 0)
    h_re, h_im = spectrum(forward, response)
    u_re, u_im = spectrum(forward, u)
    conv_local = back(inverse, h_re * u_re - h_im * u_im, h_re * u_im + h_im * u_re)
    conv_out = conv_local + jnp.sum((gain * x_in)[:, None, :] * fall, 0)
    gated = conv_out + skip_gain[None, :] * u
    result = row_major((outer_f * gated).astype(BF16))

    turns = jnp.stack([core, (tp - yy) % tps, tp]).astype(jnp.int32)
    taken = [row_major(swap_core(out_grad))]
    taken = taken + [row_major(swap_core(a)) for a in og[1:]]
    result_other = swap_core(result)
    y_parts = weight_parts(turns, result, result_other, og, taken, width)
    over_y = [y_parts[0]] + [shift_y(y_parts[s], s) for s in range(1, ny)]
    summed_y = sum(a.astype(F32) for a in over_y).astype(BF16)

    late = lax.optimization_barrier((result, gated, *y_parts))
    result, gated = late[:2]
    grad_gated = gated_gradient(turns, og, out_weight)
    pieces = output_pieces(turns, result, out_weight, tps)
    mixed = pieces[0].astype(F32)
    for k in range(1, tps):
        piece = shift_tp(pieces[k], k)
        mixed = mixed + piece.astype(F32)
    mixed = mixed.astype(BF16)

    late = lax.optimization_barrier(
        (outer_gate, inner_gate, values, residues, log_decay, grad_gated, *y_parts)
    )
    outer_gate, inner_gate, values, residues, log_decay, grad_gated = late[:6]
    outer_f = outer_gate.astype(F32)
    inner_f = inner_gate.astype(F32)
    value_f = values.astype(F32)
    u = inner_f * value_f
    rate = jnp.exp(log_decay)
    norm = jnp.sqrt(-jnp.expm1(-2.0 * rate))
    gain = residues * norm
    fall = jnp.exp(-rate[:, None, :] * rows)
    rise = jnp.exp(-rate[:, None, :] * (block - rows))
    fall_block = jnp.exp(-rate * block)
    gc = grad_gated * outer_f
    grad_outer = (grad_gated * gated).astype(BF16)

    g_re, g_im = spectrum(forward, gc)
    corr_local = back(inverse, h_re * g_re + h_im * g_im, h_re * g_im - h_im * g_re)
    lags = back(inverse, u_re * g_re + u_im * g_im, u_re * g_im - u_im * g_re)
    fg = fall * gc[None]
    g_st = jnp.sum(fg, 1)
    g_lag = jnp.sum(fg * rows, 1)
    fl = fall * lags[None]
    sum_a = g_st * x_in + jnp.sum(fl, 1)
    sum_b = g_lag * x_in + g_st * x_lag + jnp.sum(fl * rows, 1)
    sum_skip = jnp.sum(gc * u, 0, keepdims=True)
    mine_g = jnp.concatenate([g_st, sum_a, sum_b, sum_skip], 0)
    theirs_g = swap_core(mine_g)
    later = jnp.where(core == 0, theirs_g[:modes], mine_g[:modes])
    mine_h, theirs_h = my_half(mine_g), my_half(theirs_g)
    early_h = jnp.where(core == 0, mine_h[:modes], theirs_h[:modes])
    total_g = early_h + decay_h * my_half(later)
    sent = jnp.concatenate([total_g, mine_h[modes:] + theirs_h[modes:]], 0).astype(BF16)
    got = of_pairs(sent)
    got = got.astype(F32)
    w = weights(every > pair, every - pair - 1)[0]
    h_half = jnp.sum(w * got[:, :modes], 0)
    sums_half = jnp.sum(got[:, modes:], 0)
    final = both_halves(jnp.concatenate([h_half, sums_half], 0))
    h_pair = final[:modes]
    h_in = jnp.where(core == 0, later + fall_block * h_pair, h_pair)
    tot_a, tot_b = final[modes : 2 * modes], final[2 * modes : 3 * modes]
    grad_skip = final[3 * modes]
    grad_residues = norm * tot_a
    grad_decay = rate * residues * (jnp.exp(-2.0 * rate) / norm * tot_a - norm * tot_b)
    corr_in = corr_local + jnp.sum((gain * h_in)[:, None, :] * rise, 0)
    grad_mixed = corr_in + skip_gain[None, :] * gc
    grad_inner = (grad_mixed * value_f).astype(BF16)
    grad_values = (grad_mixed * inner_f).astype(BF16)

    over_z = lax.all_to_all(summed_y, "ctx", 0, 0, tiled=True, axis_index_groups=z_groups)
    grad_weight = jnp.sum(over_z.astype(F32), 0)
    return (
        mixed,
        grad_outer,
        grad_inner,
        grad_values,
        grad_weight,
        grad_skip,
        grad_residues,
        grad_decay,
    )


def solution(mesh):
    placed = (
        P("ctx", "tp"),
        P("ctx", "tp"),
        P("ctx", "tp"),
        P(None, "tp"),
        P(None, "tp"),
        P("tp"),
        P("tp", None),
        P("ctx", "tp"),
    )

    return jax.shard_map(
        body,
        mesh=mesh,
        in_specs=placed,
        out_specs=(
            P("ctx", "tp"),
            P("ctx", "tp"),
            P("ctx", "tp"),
            P("ctx", "tp"),
            P("tp", "ctx"),
            P("tp"),
            P(None, "tp"),
            P(None, "tp"),
        ),
        check_vma=False,
    )
```

```python
import jax
import jax.numpy as jnp
import numpy as np
from jax import lax
from jax.experimental import pallas as pl
from jax.experimental.layout import Layout, with_layout_constraint
from jax.experimental.pallas import tpu as pltpu
from jax.sharding import PartitionSpec as P

F32 = jnp.float32
BF16 = jnp.bfloat16
EXACT = lax.Precision.HIGHEST


def dft_tables(block):
    size = 2 * block
    freqs = np.arange(block + 1)
    rows = np.arange(block)
    angles = 2.0 * np.pi * (freqs[:, None] * rows[None, :] % size) / size
    forward = np.concatenate([np.cos(angles), -np.sin(angles)], axis=0)
    weight = np.where((freqs == 0) | (freqs == block), 1.0, 2.0)[:, None] / size
    inverse = np.concatenate([weight * np.cos(angles), -weight * np.sin(angles)], axis=0).T
    return jnp.asarray(forward, F32), jnp.asarray(inverse, F32)


def spectrum(forward, rows):
    both = jnp.dot(forward, rows, precision=EXACT, preferred_element_type=F32)
    half = both.shape[0] // 2
    return both[:half], both[half:]


def back(inverse, real_part, imag_part):
    return jnp.dot(
        inverse, jnp.concatenate([real_part, imag_part], 0), precision=EXACT, preferred_element_type=F32
    )


def row_major(a):
    return with_layout_constraint(a, Layout(major_to_minor=tuple(range(a.ndim))))


def in_vmem(count):
    return [pl.BlockSpec(memory_space=pltpu.VMEM)] * count


def weight_parts(turns, result, result_other, blocks, taken, width):
    count = len(blocks)
    tokens, chans = result.shape
    tiles = blocks[0].shape[1] // (2 * width)

    def kernel(turns_ref, *refs):
        mine_ref, other_ref = refs[:2]
        block_refs, taken_refs = refs[2 : 2 + count], refs[2 + count : 2 + 2 * count]
        out_refs = refs[2 + 2 * count : 2 + 3 * count]
        all_ref, part_ref, in_sems, out_sems = refs[2 + 3 * count :]
        core = turns_ref[0]
        for k in range(count):
            for i in range(tiles):
                at = pl.multiple_of((2 * i + core) * width, width)
                lanes = pl.ds(i * width, width)
                for half, source in enumerate((block_refs[k], taken_refs[k])):
                    pltpu.make_async_copy(
                        source.at[:, pl.ds(at, width)],
                        all_ref.at[k, pl.ds(half * tokens, tokens), lanes],
                        in_sems.at[k],
                    ).start()
        left = jnp.concatenate([mine_ref[...], other_ref[...]], 0).T
        for k in range(count):
            pltpu.make_async_copy(all_ref.at[k], all_ref.at[k], in_sems.at[k]).wait()
        for s in range(count):
            part = jnp.dot(
                left, all_ref[(turns_ref[1] - s + count) % count], preferred_element_type=F32
            ).astype(BF16)
            for i in range(tiles):
                part_ref[s, i] = part[:, i * width : (i + 1) * width]
            pltpu.make_async_copy(part_ref.at[s], out_refs[s], out_sems.at[s]).start()
        for s in range(count):
            pltpu.make_async_copy(part_ref.at[s], out_refs[s], out_sems.at[s]).wait()

    return pl.pallas_call(
        kernel,
        out_shape=[jax.ShapeDtypeStruct((tiles, chans, width), BF16)] * count,
        in_specs=[pl.BlockSpec(memory_space=pltpu.SMEM)]
        + in_vmem(2)
        + [pl.BlockSpec(memory_space=pl.ANY)] * (2 * count),
        out_specs=[pl.BlockSpec(memory_space=pl.ANY)] * count,
        scratch_shapes=[
            pltpu.VMEM((count, 2 * tokens, tiles * width), BF16),
            pltpu.VMEM((count, tiles, chans, width), BF16),
            pltpu.SemaphoreType.DMA((count,)),
            pltpu.SemaphoreType.DMA((count,)),
        ],
        compiler_params=pltpu.CompilerParams(vmem_limit_bytes=6 * 2**20),
    )(turns, result, result_other, *blocks, *taken)


def projections(turns, result, blocks, weight):
    count = len(blocks)
    tokens, feats = blocks[0].shape
    chans = result.shape[1]

    def kernel(turns_ref, result_ref, *refs):
        block_refs, weight_ref = refs[:count], refs[count]
        grad_ref, piece_refs = refs[count + 1], refs[count + 2 :]
        grad = None
        for j in range(count):
            at = pl.multiple_of((turns_ref[2] + j) % count * feats, feats)
            w = weight_ref[:, pl.ds(at, feats)]
            piece_refs[j][...] = jnp.dot(result_ref[...], w, preferred_element_type=F32).astype(
                BF16
            )
            term = lax.dot_general(
                block_refs[-j % count][...],
                w,
                (((1,), (1,)), ((), ())),
                preferred_element_type=F32,
            )
            grad = term if j == 0 else grad + term
        grad_ref[...] = grad

    return pl.pallas_call(
        kernel,
        out_shape=[jax.ShapeDtypeStruct((tokens, chans), F32)]
        + [jax.ShapeDtypeStruct((tokens, feats), BF16)] * count,
        in_specs=[pl.BlockSpec(memory_space=pltpu.SMEM)] + in_vmem(2 + count),
        out_specs=in_vmem(1 + count),
        compiler_params=pltpu.CompilerParams(vmem_limit_bytes=6 * 2**20),
    )(turns, result, *blocks, weight)


def body(outer_gate, inner_gate, values, residues, log_decay, skip_gain, out_weight, out_grad):
    ctx = lax.axis_size("ctx")
    tps = lax.axis_size("tp")
    dev = lax.axis_index("ctx")
    tp = lax.axis_index("tp")
    block, chans = outer_gate.shape
    modes = residues.shape[0]
    feats = out_grad.shape[1]
    ny = tps
    nz = ctx // (2 * ny)
    core = dev % 2
    pair = dev // 2
    zz = pair % nz
    pairs = ctx // 2
    yy = dev // (2 * nz)
    width = feats // (2 * nz)

    def swap_core(a):
        return lax.ppermute(a, "ctx", [(i, i ^ 1) for i in range(ctx)])

    def shift_tp(a, k):
        return lax.ppermute(a, "tp", [(i, (i + k) % tps) for i in range(tps)])

    def shift_y(a, k):
        per = 2 * nz
        return lax.ppermute(a, "ctx", [(i, (i // per + k) % ny * per + i % per) for i in range(ctx)])

    z_groups = [[i * 2 * nz + j * 2 + k for j in range(nz)] for i in range(ny) for k in range(2)]

    def of_plane(a):
        copies = jnp.broadcast_to(a[None], (nz, *a.shape))
        return lax.all_to_all(copies, "ctx", 0, 0, tiled=True, axis_index_groups=z_groups)

    def of_pairs(a):
        copies = jnp.broadcast_to(a[None], (pairs, *a.shape))
        groups = [[2 * i + j for i in range(pairs)] for j in range(2)]
        return lax.all_to_all(copies, "ctx", 0, 0, tiled=True, axis_index_groups=groups)

    og = [out_grad] + [row_major(shift_tp(out_grad, k)) for k in range(1, tps)]

    u = inner_gate.astype(F32) * values.astype(F32)
    rate = jnp.exp(log_decay)
    rows = jnp.arange(block, dtype=F32)[None, :, None]
    rate3 = rate[:, None, :]
    rise = jnp.exp(-rate3 * (block - rows))
    fall_block = jnp.exp(-rate * block)

    lead = rise * u[None]
    st = jnp.sum(lead, 1)
    st_lag = jnp.sum(lead * (block - rows), 1)
    mine = jnp.concatenate([st, st_lag], 0)
    theirs = swap_core(mine)
    first = jnp.where(core == 0, mine, theirs)
    second = jnp.where(core == 0, theirs, mine)
    half = chans // 2

    def my_half(a):
        return lax.dynamic_slice_in_dim(a, core * half, half, a.ndim - 1)

    def both_halves(a):
        other = swap_core(a)
        return jnp.concatenate(
            [jnp.where(core == 0, a, other), jnp.where(core == 0, other, a)], a.ndim - 1
        )

    rate_h = my_half(rate)
    decay_h = jnp.exp(-rate_h * block)
    f_h, s_h = my_half(first), my_half(second)
    total = decay_h * f_h[:modes] + s_h[:modes]
    total_lag = decay_h * (block * f_h[:modes] + f_h[modes:]) + s_h[modes:]
    to_send = jnp.concatenate([total, total_lag], 0).astype(BF16)
    gathered = of_pairs(to_send).astype(F32)
    place = jnp.arange(nz, dtype=jnp.int32)
    every = jnp.arange(pairs, dtype=jnp.int32)
    per_pair = 2 * block
    per_plane = per_pair * nz

    def weights(which, gap):
        gap = jnp.where(which, gap, 0).astype(F32)[:, None, None] * per_pair
        return jnp.where(which[:, None, None], jnp.exp(-rate_h[None] * gap), 0.0), gap

    w, gap = weights(every < pair, pair - 1 - every)
    base = gathered[:, :modes]
    in_h = jnp.sum(w * base, 0)
    in_lag_h = jnp.sum(w * (gap * base + gathered[:, modes:]), 0)
    incoming = both_halves(jnp.concatenate([in_h, in_lag_h], 0))
    in_pair, in_pair_lag = incoming[:modes], incoming[modes:]
    x_in = jnp.where(core == 0, in_pair, fall_block * in_pair + first[:modes])
    x_lag = jnp.where(
        core == 0, in_pair_lag, fall_block * (in_pair_lag + block * in_pair) + first[modes:]
    )

    outer_gate, inner_gate, values, residues, log_decay, x_in, x_lag = lax.optimization_barrier(
        (outer_gate, inner_gate, values, residues, log_decay, x_in, x_lag)
    )
    rate = jnp.exp(log_decay)
    gain = residues * jnp.sqrt(-jnp.expm1(-2.0 * rate))
    fall = jnp.exp(-rate[:, None, :] * rows)
    outer_f = outer_gate.astype(F32)
    u = inner_gate.astype(F32) * values.astype(F32)

    forward, inverse = dft_tables(block)
    response = jnp.sum(gain[:, None, :] * fall, 0)
    h_re, h_im = spectrum(forward, response)
    u_re, u_im = spectrum(forward, u)
    conv_local = back(inverse, h_re * u_re - h_im * u_im, h_re * u_im + h_im * u_re)
    conv_out = conv_local + jnp.sum((gain * x_in)[:, None, :] * fall, 0)
    gated = conv_out + skip_gain[None, :] * u
    result = row_major((outer_f * gated).astype(BF16))

    turns = jnp.stack([core, (tp - yy) % tps, tp]).astype(jnp.int32)
    taken = [row_major(swap_core(a)) for a in og]
    result_other = swap_core(result)
    y_parts = weight_parts(turns, result, result_other, og, taken, width)
    over_y = [y_parts[0]] + [shift_y(y_parts[s], s) for s in range(1, ny)]
    summed_y = sum(a.astype(F32) for a in over_y).astype(BF16)

    late = lax.optimization_barrier((result, gated, *y_parts))
    result, gated = late[:2]
    grad_gated, *pieces = projections(turns, result, og, out_weight)
    mixed = pieces[0].astype(F32)
    for k in range(1, tps):
        piece = shift_tp(pieces[k], k)
        mixed = mixed + piece.astype(F32)
    mixed = mixed.astype(BF16)

    late = lax.optimization_barrier(
        (outer_gate, inner_gate, values, residues, log_decay, grad_gated, *y_parts)
    )
    outer_gate, inner_gate, values, residues, log_decay, grad_gated = late[:6]
    outer_f = outer_gate.astype(F32)
    inner_f = inner_gate.astype(F32)
    value_f = values.astype(F32)
    u = inner_f * value_f
    rate = jnp.exp(log_decay)
    norm = jnp.sqrt(-jnp.expm1(-2.0 * rate))
    gain = residues * norm
    fall = jnp.exp(-rate[:, None, :] * rows)
    rise = jnp.exp(-rate[:, None, :] * (block - rows))
    fall_block = jnp.exp(-rate * block)
    gc = grad_gated * outer_f
    grad_outer = (grad_gated * gated).astype(BF16)

    g_re, g_im = spectrum(forward, gc)
    corr_local = back(inverse, h_re * g_re + h_im * g_im, h_re * g_im - h_im * g_re)
    lags = back(inverse, u_re * g_re + u_im * g_im, u_re * g_im - u_im * g_re)
    fg = fall * gc[None]
    g_st = jnp.sum(fg, 1)
    g_lag = jnp.sum(fg * rows, 1)
    fl = fall * lags[None]
    sum_a = g_st * x_in + jnp.sum(fl, 1)
    sum_b = g_lag * x_in + g_st * x_lag + jnp.sum(fl * rows, 1)
    sum_skip = jnp.sum(gc * u, 0, keepdims=True)
    mine_g = jnp.concatenate([g_st, sum_a, sum_b, sum_skip], 0)
    theirs_g = swap_core(mine_g)
    later = jnp.where(core == 0, theirs_g[:modes], mine_g[:modes])
    mine_h, theirs_h = my_half(mine_g), my_half(theirs_g)
    early_h = jnp.where(core == 0, mine_h[:modes], theirs_h[:modes])
    total_g = early_h + decay_h * my_half(later)
    sent = jnp.concatenate([total_g, mine_h[modes:] + theirs_h[modes:]], 0).astype(BF16)
    got = of_plane(sent)
    got = got.astype(F32)
    plane_h = jnp.sum(weights(place >= 0, place)[0] * got[:, :modes], 0)
    plane_sums = jnp.sum(got[:, modes:], 0)
    plane_g = jnp.concatenate([plane_h, plane_sums], 0)
    h_half = jnp.sum(weights(place > zz, place - zz - 1)[0] * got[:, :modes], 0)
    y_h, sums_half = 0.0, plane_sums
    for k in range(1, ny):
        came = shift_y(plane_g, -k)
        w = jnp.exp(-rate_h * float(per_plane * (k - 1)))
        y_h = y_h + jnp.where(yy + k < ny, w * came[:modes], 0.0)
        sums_half = sums_half + came[modes:]
    h_half = h_half + jnp.exp(-rate_h * (per_pair * (nz - 1 - zz)).astype(F32)) * y_h
    final = both_halves(jnp.concatenate([h_half, sums_half], 0))
    h_pair = final[:modes]
    h_in = jnp.where(core == 0, later + fall_block * h_pair, h_pair)
    tot_a, tot_b = final[modes : 2 * modes], final[2 * modes : 3 * modes]
    grad_skip = final[3 * modes]
    grad_residues = norm * tot_a
    grad_decay = rate * residues * (jnp.exp(-2.0 * rate) / norm * tot_a - norm * tot_b)
    corr_in = corr_local + jnp.sum((gain * h_in)[:, None, :] * rise, 0)
    grad_mixed = corr_in + skip_gain[None, :] * gc
    grad_inner = (grad_mixed * value_f).astype(BF16)
    grad_values = (grad_mixed * inner_f).astype(BF16)

    over_z = lax.all_to_all(summed_y, "ctx", 0, 0, tiled=True, axis_index_groups=z_groups)
    grad_weight = jnp.sum(over_z.astype(F32), 0)
    return (
        mixed,
        grad_outer,
        grad_inner,
        grad_values,
        grad_weight,
        grad_skip,
        grad_residues,
        grad_decay,
    )


def solution(mesh):
    placed = (
        P("ctx", "tp"),
        P("ctx", "tp"),
        P("ctx", "tp"),
        P(None, "tp"),
        P(None, "tp"),
        P("tp"),
        P("tp", None),
        P("ctx", "tp"),
    )

    return jax.shard_map(
        body,
        mesh=mesh,
        in_specs=placed,
        out_specs=(
            P("ctx", "tp"),
            P("ctx", "tp"),
            P("ctx", "tp"),
            P("ctx", "tp"),
            P("tp", "ctx"),
            P("tp"),
            P(None, "tp"),
            P(None, "tp"),
        ),
        check_vma=False,
    )
```

```python
import jax
import jax.numpy as jnp
import numpy as np
from jax import lax
from jax.experimental import pallas as pl
from jax.experimental.layout import Layout, with_layout_constraint
from jax.experimental.pallas import tpu as pltpu
from jax.sharding import PartitionSpec as P

F32 = jnp.float32
BF16 = jnp.bfloat16
EXACT = lax.Precision.HIGHEST


def dft_tables(block):
    size = 2 * block
    freqs = np.arange(block + 1)
    rows = np.arange(block)
    angles = 2.0 * np.pi * (freqs[:, None] * rows[None, :] % size) / size
    forward = np.concatenate([np.cos(angles), -np.sin(angles)], axis=0)
    weight = np.where((freqs == 0) | (freqs == block), 1.0, 2.0)[:, None] / size
    inverse = np.concatenate([weight * np.cos(angles), -weight * np.sin(angles)], axis=0).T
    return jnp.asarray(forward, F32), jnp.asarray(inverse, F32)


def spectrum(forward, rows):
    both = jnp.dot(forward, rows, precision=EXACT, preferred_element_type=F32)
    half = both.shape[0] // 2
    return both[:half], both[half:]


def back(inverse, real_part, imag_part):
    return jnp.dot(
        inverse, jnp.concatenate([real_part, imag_part], 0), precision=EXACT, preferred_element_type=F32
    )


def row_major(a):
    return with_layout_constraint(a, Layout(major_to_minor=tuple(range(a.ndim))))


def in_vmem(count):
    return [pl.BlockSpec(memory_space=pltpu.VMEM)] * count


def weight_parts(turns, result, result_other, blocks, taken, width):
    count = len(blocks)
    tokens, chans = result.shape
    tiles = blocks[0].shape[1] // (2 * width)

    def kernel(turns_ref, *refs):
        mine_ref, other_ref = refs[:2]
        block_refs, taken_refs = refs[2 : 2 + count], refs[2 + count : 2 + 2 * count]
        out_refs = refs[2 + 2 * count : 2 + 3 * count]
        all_ref, part_ref, in_sems, out_sems = refs[2 + 3 * count :]
        core = turns_ref[0]
        for k in range(count):
            for i in range(tiles):
                at = pl.multiple_of((2 * i + core) * width, width)
                lanes = pl.ds(i * width, width)
                for half, source in enumerate((block_refs[k], taken_refs[k])):
                    pltpu.make_async_copy(
                        source.at[:, pl.ds(at, width)],
                        all_ref.at[k, pl.ds(half * tokens, tokens), lanes],
                        in_sems.at[k],
                    ).start()
        left = jnp.concatenate([mine_ref[...], other_ref[...]], 0).T
        for k in range(count):
            pltpu.make_async_copy(all_ref.at[k], all_ref.at[k], in_sems.at[k]).wait()
        for s in range(count):
            part = jnp.dot(
                left, all_ref[(turns_ref[1] - s + count) % count], preferred_element_type=F32
            ).astype(BF16)
            for i in range(tiles):
                part_ref[s, i] = part[:, i * width : (i + 1) * width]
            pltpu.make_async_copy(part_ref.at[s], out_refs[s], out_sems.at[s]).start()
        for s in range(count):
            pltpu.make_async_copy(part_ref.at[s], out_refs[s], out_sems.at[s]).wait()

    return pl.pallas_call(
        kernel,
        out_shape=[jax.ShapeDtypeStruct((tiles, chans, width), BF16)] * count,
        in_specs=[pl.BlockSpec(memory_space=pltpu.SMEM)]
        + in_vmem(2)
        + [pl.BlockSpec(memory_space=pl.ANY)] * (2 * count),
        out_specs=[pl.BlockSpec(memory_space=pl.ANY)] * count,
        scratch_shapes=[
            pltpu.VMEM((count, 2 * tokens, tiles * width), BF16),
            pltpu.VMEM((count, tiles, chans, width), BF16),
            pltpu.SemaphoreType.DMA((count,)),
            pltpu.SemaphoreType.DMA((count,)),
        ],
        compiler_params=pltpu.CompilerParams(vmem_limit_bytes=6 * 2**20),
    )(turns, result, result_other, *blocks, *taken)


def projections(turns, result, blocks, weight):
    count = len(blocks)
    tokens, feats = blocks[0].shape
    chans = result.shape[1]

    def kernel(turns_ref, result_ref, *refs):
        block_refs, weight_ref = refs[:count], refs[count]
        grad_ref, piece_refs = refs[count + 1], refs[count + 2 :]
        grad = None
        for j in range(count):
            at = pl.multiple_of((turns_ref[2] + j) % count * feats, feats)
            w = weight_ref[:, pl.ds(at, feats)]
            piece_refs[j][...] = jnp.dot(result_ref[...], w, preferred_element_type=F32).astype(
                BF16
            )
            term = lax.dot_general(
                block_refs[-j % count][...],
                w,
                (((1,), (1,)), ((), ())),
                preferred_element_type=F32,
            )
            grad = term if j == 0 else grad + term
        grad_ref[...] = grad

    return pl.pallas_call(
        kernel,
        out_shape=[jax.ShapeDtypeStruct((tokens, chans), F32)]
        + [jax.ShapeDtypeStruct((tokens, feats), BF16)] * count,
        in_specs=[pl.BlockSpec(memory_space=pltpu.SMEM)] + in_vmem(2 + count),
        out_specs=in_vmem(1 + count),
        compiler_params=pltpu.CompilerParams(vmem_limit_bytes=6 * 2**20),
    )(turns, result, *blocks, weight)


def body(outer_gate, inner_gate, values, residues, log_decay, skip_gain, out_weight, out_grad):
    ctx = lax.axis_size("ctx")
    tps = lax.axis_size("tp")
    dev = lax.axis_index("ctx")
    tp = lax.axis_index("tp")
    block, chans = outer_gate.shape
    modes = residues.shape[0]
    feats = out_grad.shape[1]
    ny = tps
    nz = ctx // (2 * ny)
    core = dev % 2
    pair = dev // 2
    pairs = ctx // 2
    yy = dev // (2 * nz)
    width = feats // (2 * nz)

    def swap_core(a):
        return lax.ppermute(a, "ctx", [(i, i ^ 1) for i in range(ctx)])

    def shift_tp(a, k):
        return lax.ppermute(a, "tp", [(i, (i + k) % tps) for i in range(tps)])

    def shift_y(a, k):
        per = 2 * nz
        return lax.ppermute(a, "ctx", [(i, (i // per + k) % ny * per + i % per) for i in range(ctx)])

    z_groups = [[i * 2 * nz + j * 2 + k for j in range(nz)] for i in range(ny) for k in range(2)]

    per = 2 * nz

    def of_plane(a):
        copies = jnp.broadcast_to(a[None], (per, *a.shape))
        groups = [[i * per + j for j in range(per)] for i in range(ny)]
        return lax.all_to_all(copies, "ctx", 0, 0, tiled=True, axis_index_groups=groups)

    def of_pairs(a):
        copies = jnp.broadcast_to(a[None], (pairs, *a.shape))
        groups = [[2 * i + j for i in range(pairs)] for j in range(2)]
        return lax.all_to_all(copies, "ctx", 0, 0, tiled=True, axis_index_groups=groups)

    og = [out_grad] + [row_major(shift_tp(out_grad, k)) for k in range(1, tps)]

    u = inner_gate.astype(F32) * values.astype(F32)
    rate = jnp.exp(log_decay)
    rows = jnp.arange(block, dtype=F32)[None, :, None]
    rate3 = rate[:, None, :]
    rise = jnp.exp(-rate3 * (block - rows))
    fall_block = jnp.exp(-rate * block)

    lead = rise * u[None]
    st = jnp.sum(lead, 1)
    st_lag = jnp.sum(lead * (block - rows), 1)
    mine = jnp.concatenate([st, st_lag], 0)
    theirs = swap_core(mine)
    first = jnp.where(core == 0, mine, theirs)
    second = jnp.where(core == 0, theirs, mine)
    half = chans // 2

    def my_half(a):
        return lax.dynamic_slice_in_dim(a, core * half, half, a.ndim - 1)

    def both_halves(a):
        other = swap_core(a)
        return jnp.concatenate(
            [jnp.where(core == 0, a, other), jnp.where(core == 0, other, a)], a.ndim - 1
        )

    rate_h = my_half(rate)
    decay_h = jnp.exp(-rate_h * block)
    f_h, s_h = my_half(first), my_half(second)
    total = decay_h * f_h[:modes] + s_h[:modes]
    total_lag = decay_h * (block * f_h[:modes] + f_h[modes:]) + s_h[modes:]
    to_send = jnp.concatenate([total, total_lag], 0).astype(BF16)
    gathered = of_pairs(to_send).astype(F32)
    every = jnp.arange(pairs, dtype=jnp.int32)
    per_pair = 2 * block

    def weights(which, gap):
        gap = jnp.where(which, gap, 0).astype(F32)[:, None, None] * per_pair
        return jnp.where(which[:, None, None], jnp.exp(-rate_h[None] * gap), 0.0), gap

    w, gap = weights(every < pair, pair - 1 - every)
    base = gathered[:, :modes]
    in_h = jnp.sum(w * base, 0)
    in_lag_h = jnp.sum(w * (gap * base + gathered[:, modes:]), 0)
    incoming = both_halves(jnp.concatenate([in_h, in_lag_h], 0))
    in_pair, in_pair_lag = incoming[:modes], incoming[modes:]
    x_in = jnp.where(core == 0, in_pair, fall_block * in_pair + first[:modes])
    x_lag = jnp.where(
        core == 0, in_pair_lag, fall_block * (in_pair_lag + block * in_pair) + first[modes:]
    )

    outer_gate, inner_gate, values, residues, log_decay, x_in, x_lag = lax.optimization_barrier(
        (outer_gate, inner_gate, values, residues, log_decay, x_in, x_lag)
    )
    rate = jnp.exp(log_decay)
    gain = residues * jnp.sqrt(-jnp.expm1(-2.0 * rate))
    fall = jnp.exp(-rate[:, None, :] * rows)
    outer_f = outer_gate.astype(F32)
    u = inner_gate.astype(F32) * values.astype(F32)

    forward, inverse = dft_tables(block)
    response = jnp.sum(gain[:, None, :] * fall, 0)
    h_re, h_im = spectrum(forward, response)
    u_re, u_im = spectrum(forward, u)
    conv_local = back(inverse, h_re * u_re - h_im * u_im, h_re * u_im + h_im * u_re)
    conv_out = conv_local + jnp.sum((gain * x_in)[:, None, :] * fall, 0)
    gated = conv_out + skip_gain[None, :] * u
    result = row_major((outer_f * gated).astype(BF16))

    turns = jnp.stack([core, (tp - yy) % tps, tp]).astype(jnp.int32)
    taken = [row_major(swap_core(a)) for a in og]
    result_other = swap_core(result)
    y_parts = weight_parts(turns, result, result_other, og, taken, width)
    over_y = [y_parts[0]] + [shift_y(y_parts[s], s) for s in range(1, ny)]
    summed_y = sum(a.astype(F32) for a in over_y).astype(BF16)

    late = lax.optimization_barrier((result, gated, *y_parts))
    result, gated = late[:2]
    grad_gated, *pieces = projections(turns, result, og, out_weight)
    mixed = pieces[0].astype(F32)
    for k in range(1, tps):
        piece = shift_tp(pieces[k], k)
        mixed = mixed + piece.astype(F32)
    mixed = mixed.astype(BF16)

    late = lax.optimization_barrier(
        (outer_gate, inner_gate, values, residues, log_decay, grad_gated, *y_parts)
    )
    outer_gate, inner_gate, values, residues, log_decay, grad_gated = late[:6]
    outer_f = outer_gate.astype(F32)
    inner_f = inner_gate.astype(F32)
    value_f = values.astype(F32)
    u = inner_f * value_f
    rate = jnp.exp(log_decay)
    norm = jnp.sqrt(-jnp.expm1(-2.0 * rate))
    gain = residues * norm
    fall = jnp.exp(-rate[:, None, :] * rows)
    rise = jnp.exp(-rate[:, None, :] * (block - rows))
    gc = grad_gated * outer_f
    grad_outer = (grad_gated * gated).astype(BF16)

    g_re, g_im = spectrum(forward, gc)
    corr_local = back(inverse, h_re * g_re + h_im * g_im, h_re * g_im - h_im * g_re)
    lags = back(inverse, u_re * g_re + u_im * g_im, u_re * g_im - u_im * g_re)
    fg = fall * gc[None]
    g_st = jnp.sum(fg, 1)
    g_lag = jnp.sum(fg * rows, 1)
    fl = fall * lags[None]
    sum_a = g_st * x_in + jnp.sum(fl, 1)
    sum_b = g_lag * x_in + g_st * x_lag + jnp.sum(fl * rows, 1)
    sum_skip = jnp.sum(gc * u, 0, keepdims=True)
    sent = jnp.concatenate([g_st, sum_a, sum_b, sum_skip], 0).astype(BF16)
    got = of_plane(sent)
    slot = dev % per
    slots = jnp.arange(per, dtype=jnp.int32)

    def falls(which, steps):
        steps = jnp.where(which, steps, 0).astype(F32)[:, None, None] * block
        return jnp.where(which[:, None, None], jnp.exp(-rate[None] * steps), 0.0)

    got = got.astype(F32)
    h_in = jnp.sum(falls(slots > slot, slots - slot - 1) * got[:, :modes], 0)
    plane_h = jnp.sum(falls(slots >= 0, slots) * got[:, :modes], 0)
    sums = jnp.sum(got[:, modes:], 0)
    plane_g = jnp.concatenate([plane_h, sums], 0)
    y_h = 0.0
    for k in range(1, ny):
        came = shift_y(plane_g, -k)
        w = jnp.exp(-rate * float(block * per * (k - 1)))
        y_h = y_h + jnp.where(yy + k < ny, w * came[:modes], 0.0)
        sums = sums + came[modes:]
    h_in = h_in + jnp.exp(-rate * (block * (per - 1 - slot)).astype(F32)) * y_h
    tot_a, tot_b, grad_skip = sums[:modes], sums[modes : 2 * modes], sums[2 * modes]
    grad_residues = norm * tot_a
    grad_decay = rate * residues * (jnp.exp(-2.0 * rate) / norm * tot_a - norm * tot_b)
    corr_in = corr_local + jnp.sum((gain * h_in)[:, None, :] * rise, 0)
    grad_mixed = corr_in + skip_gain[None, :] * gc
    grad_inner = (grad_mixed * value_f).astype(BF16)
    grad_values = (grad_mixed * inner_f).astype(BF16)

    over_z = lax.all_to_all(summed_y, "ctx", 0, 0, tiled=True, axis_index_groups=z_groups)
    grad_weight = jnp.sum(over_z.astype(F32), 0)
    return (
        mixed,
        grad_outer,
        grad_inner,
        grad_values,
        grad_weight,
        grad_skip,
        grad_residues,
        grad_decay,
    )


def solution(mesh):
    placed = (
        P("ctx", "tp"),
        P("ctx", "tp"),
        P("ctx", "tp"),
        P(None, "tp"),
        P(None, "tp"),
        P("tp"),
        P("tp", None),
        P("ctx", "tp"),
    )

    return jax.shard_map(
        body,
        mesh=mesh,
        in_specs=placed,
        out_specs=(
            P("ctx", "tp"),
            P("ctx", "tp"),
            P("ctx", "tp"),
            P("ctx", "tp"),
            P("tp", "ctx"),
            P("tp"),
            P(None, "tp"),
            P(None, "tp"),
        ),
        check_vma=False,
    )
```

```python
import jax
import jax.numpy as jnp
import numpy as np
from jax import lax
from jax.experimental import pallas as pl
from jax.experimental.layout import Layout, with_layout_constraint
from jax.experimental.pallas import tpu as pltpu
from jax.sharding import PartitionSpec as P

F32 = jnp.float32
BF16 = jnp.bfloat16
FINE = lax.Precision.HIGH


def dft_tables(block):
    size = 2 * block
    freqs = np.arange(block + 1)
    rows = np.arange(block)
    angles = 2.0 * np.pi * (freqs[:, None] * rows[None, :] % size) / size
    forward = np.concatenate([np.cos(angles), -np.sin(angles)], axis=0)
    weight = np.where((freqs == 0) | (freqs == block), 1.0, 2.0)[:, None] / size
    inverse = np.concatenate([weight * np.cos(angles), -weight * np.sin(angles)], axis=0).T
    return jnp.asarray(forward, F32), jnp.asarray(inverse, F32)


def spectrum(forward, rows):
    both = jnp.dot(forward, rows, precision=FINE, preferred_element_type=F32)
    half = both.shape[0] // 2
    return both[:half], both[half:]


def back(inverse, real_part, imag_part):
    return jnp.dot(
        inverse, jnp.concatenate([real_part, imag_part], 0), precision=FINE, preferred_element_type=F32
    )


def row_major(a):
    return with_layout_constraint(a, Layout(major_to_minor=tuple(range(a.ndim))))


def in_vmem(count):
    return [pl.BlockSpec(memory_space=pltpu.VMEM)] * count


def weight_parts(turns, result, result_other, blocks, taken, width):
    count = len(blocks)
    tokens, chans = result.shape
    tiles = blocks[0].shape[1] // (2 * width)

    def kernel(turns_ref, *refs):
        mine_ref, other_ref = refs[:2]
        block_refs, taken_refs = refs[2 : 2 + count], refs[2 + count : 2 + 2 * count]
        out_refs = refs[2 + 2 * count : 2 + 3 * count]
        all_ref, part_ref, in_sems, out_sems = refs[2 + 3 * count :]
        core = turns_ref[0]
        for k in range(count):
            for i in range(tiles):
                at = pl.multiple_of((2 * i + core) * width, width)
                lanes = pl.ds(i * width, width)
                for half, source in enumerate((block_refs[k], taken_refs[k])):
                    pltpu.make_async_copy(
                        source.at[:, pl.ds(at, width)],
                        all_ref.at[k, pl.ds(half * tokens, tokens), lanes],
                        in_sems.at[k],
                    ).start()
        left = jnp.concatenate([mine_ref[...], other_ref[...]], 0).T
        for k in range(count):
            pltpu.make_async_copy(all_ref.at[k], all_ref.at[k], in_sems.at[k]).wait()
        for s in range(count):
            part = jnp.dot(
                left, all_ref[(turns_ref[1] - s + count) % count], preferred_element_type=F32
            ).astype(BF16)
            for i in range(tiles):
                part_ref[s, i] = part[:, i * width : (i + 1) * width]
            pltpu.make_async_copy(part_ref.at[s], out_refs[s], out_sems.at[s]).start()
        for s in range(count):
            pltpu.make_async_copy(part_ref.at[s], out_refs[s], out_sems.at[s]).wait()

    return pl.pallas_call(
        kernel,
        out_shape=[jax.ShapeDtypeStruct((tiles, chans, width), BF16)] * count,
        in_specs=[pl.BlockSpec(memory_space=pltpu.SMEM)]
        + in_vmem(2)
        + [pl.BlockSpec(memory_space=pl.ANY)] * (2 * count),
        out_specs=[pl.BlockSpec(memory_space=pl.ANY)] * count,
        scratch_shapes=[
            pltpu.VMEM((count, 2 * tokens, tiles * width), BF16),
            pltpu.VMEM((count, tiles, chans, width), BF16),
            pltpu.SemaphoreType.DMA((count,)),
            pltpu.SemaphoreType.DMA((count,)),
        ],
        compiler_params=pltpu.CompilerParams(vmem_limit_bytes=6 * 2**20),
    )(turns, result, result_other, *blocks, *taken)


def projections(turns, result, blocks, weight):
    count = len(blocks)
    tokens, feats = blocks[0].shape
    chans = result.shape[1]

    def kernel(turns_ref, result_ref, *refs):
        block_refs, weight_ref = refs[:count], refs[count]
        grad_ref, piece_refs = refs[count + 1], refs[count + 2 :]
        grad = None
        for j in range(count):
            at = pl.multiple_of((turns_ref[2] + j) % count * feats, feats)
            w = weight_ref[:, pl.ds(at, feats)]
            piece_refs[j][...] = jnp.dot(result_ref[...], w, preferred_element_type=F32).astype(
                BF16
            )
            term = lax.dot_general(
                block_refs[-j % count][...],
                w,
                (((1,), (1,)), ((), ())),
                preferred_element_type=F32,
            )
            grad = term if j == 0 else grad + term
        grad_ref[...] = grad

    return pl.pallas_call(
        kernel,
        out_shape=[jax.ShapeDtypeStruct((tokens, chans), F32)]
        + [jax.ShapeDtypeStruct((tokens, feats), BF16)] * count,
        in_specs=[pl.BlockSpec(memory_space=pltpu.SMEM)] + in_vmem(2 + count),
        out_specs=in_vmem(1 + count),
        compiler_params=pltpu.CompilerParams(vmem_limit_bytes=6 * 2**20),
    )(turns, result, *blocks, weight)


def body(outer_gate, inner_gate, values, residues, log_decay, skip_gain, out_weight, out_grad):
    ctx = lax.axis_size("ctx")
    tps = lax.axis_size("tp")
    dev = lax.axis_index("ctx")
    tp = lax.axis_index("tp")
    block, chans = outer_gate.shape
    modes = residues.shape[0]
    feats = out_grad.shape[1]
    ny = tps
    nz = ctx // (2 * ny)
    core = dev % 2
    pair = dev // 2
    zz = pair % nz
    pairs = ctx // 2
    yy = dev // (2 * nz)
    width = feats // (2 * nz)

    def swap_core(a):
        return lax.ppermute(a, "ctx", [(i, i ^ 1) for i in range(ctx)])

    def shift_tp(a, k):
        return lax.ppermute(a, "tp", [(i, (i + k) % tps) for i in range(tps)])

    def shift_y(a, k):
        per = 2 * nz
        return lax.ppermute(a, "ctx", [(i, (i // per + k) % ny * per + i % per) for i in range(ctx)])

    z_groups = [[i * 2 * nz + j * 2 + k for j in range(nz)] for i in range(ny) for k in range(2)]

    def of_plane(a):
        copies = jnp.broadcast_to(a[None], (nz, *a.shape))
        return lax.all_to_all(copies, "ctx", 0, 0, tiled=True, axis_index_groups=z_groups)

    def of_pairs(a):
        copies = jnp.broadcast_to(a[None], (pairs, *a.shape))
        groups = [[2 * i + j for i in range(pairs)] for j in range(2)]
        return lax.all_to_all(copies, "ctx", 0, 0, tiled=True, axis_index_groups=groups)

    og = [out_grad] + [row_major(shift_tp(out_grad, k)) for k in range(1, tps)]

    u = inner_gate.astype(F32) * values.astype(F32)
    rate = jnp.exp(log_decay)
    rows = jnp.arange(block, dtype=F32)[None, :, None]
    rate3 = rate[:, None, :]
    rise = jnp.exp(-rate3 * (block - rows))
    fall_block = jnp.exp(-rate * block)

    lead = rise * u[None]
    st = jnp.sum(lead, 1)
    st_lag = jnp.sum(lead * (block - rows), 1)
    mine = jnp.concatenate([st, st_lag], 0)
    theirs = swap_core(mine)
    first = jnp.where(core == 0, mine, theirs)
    second = jnp.where(core == 0, theirs, mine)
    half = chans // 2

    def my_half(a):
        return lax.dynamic_slice_in_dim(a, core * half, half, a.ndim - 1)

    def both_halves(a):
        other = swap_core(a)
        return jnp.concatenate(
            [jnp.where(core == 0, a, other), jnp.where(core == 0, other, a)], a.ndim - 1
        )

    rate_h = my_half(rate)
    decay_h = jnp.exp(-rate_h * block)
    f_h, s_h = my_half(first), my_half(second)
    total = decay_h * f_h[:modes] + s_h[:modes]
    total_lag = decay_h * (block * f_h[:modes] + f_h[modes:]) + s_h[modes:]
    to_send = jnp.concatenate([total, total_lag], 0).astype(BF16)
    gathered = of_pairs(to_send).astype(F32)
    place = jnp.arange(nz, dtype=jnp.int32)
    every = jnp.arange(pairs, dtype=jnp.int32)
    per_pair = 2 * block
    per_plane = per_pair * nz

    def weights(which, gap):
        gap = jnp.where(which, gap, 0).astype(F32)[:, None, None] * per_pair
        return jnp.where(which[:, None, None], jnp.exp(-rate_h[None] * gap), 0.0), gap

    w, gap = weights(every < pair, pair - 1 - every)
    base = gathered[:, :modes]
    in_h = jnp.sum(w * base, 0)
    in_lag_h = jnp.sum(w * (gap * base + gathered[:, modes:]), 0)
    incoming = both_halves(jnp.concatenate([in_h, in_lag_h], 0))
    in_pair, in_pair_lag = incoming[:modes], incoming[modes:]
    x_in = jnp.where(core == 0, in_pair, fall_block * in_pair + first[:modes])
    x_lag = jnp.where(
        core == 0, in_pair_lag, fall_block * (in_pair_lag + block * in_pair) + first[modes:]
    )

    outer_gate, inner_gate, values, residues, log_decay, x_in, x_lag = lax.optimization_barrier(
        (outer_gate, inner_gate, values, residues, log_decay, x_in, x_lag)
    )
    rate = jnp.exp(log_decay)
    gain = residues * jnp.sqrt(-jnp.expm1(-2.0 * rate))
    fall = jnp.exp(-rate[:, None, :] * rows)
    outer_f = outer_gate.astype(F32)
    u = inner_gate.astype(F32) * values.astype(F32)

    forward, inverse = dft_tables(block)
    response = jnp.sum(gain[:, None, :] * fall, 0)
    h_re, h_im = spectrum(forward, response)
    u_re, u_im = spectrum(forward, u)
    conv_local = back(inverse, h_re * u_re - h_im * u_im, h_re * u_im + h_im * u_re)
    conv_out = conv_local + jnp.sum((gain * x_in)[:, None, :] * fall, 0)
    gated = conv_out + skip_gain[None, :] * u
    result = row_major((outer_f * gated).astype(BF16))

    turns = jnp.stack([core, (tp - yy) % tps, tp]).astype(jnp.int32)
    taken = [row_major(swap_core(a)) for a in og]
    result_other = swap_core(result)
    y_parts = weight_parts(turns, result, result_other, og, taken, width)
    over_y = [y_parts[0]] + [shift_y(y_parts[s], s) for s in range(1, ny)]
    summed_y = sum(a.astype(F32) for a in over_y).astype(BF16)

    late = lax.optimization_barrier((result, gated, *y_parts))
    result, gated = late[:2]
    grad_gated, *pieces = projections(turns, result, og, out_weight)
    mixed = pieces[0].astype(F32)
    for k in range(1, tps):
        piece = shift_tp(pieces[k], k)
        mixed = mixed + piece.astype(F32)
    mixed = mixed.astype(BF16)

    late = lax.optimization_barrier(
        (outer_gate, inner_gate, values, residues, log_decay, grad_gated, *y_parts)
    )
    outer_gate, inner_gate, values, residues, log_decay, grad_gated = late[:6]
    outer_f = outer_gate.astype(F32)
    inner_f = inner_gate.astype(F32)
    value_f = values.astype(F32)
    u = inner_f * value_f
    rate = jnp.exp(log_decay)
    norm = jnp.sqrt(-jnp.expm1(-2.0 * rate))
    gain = residues * norm
    fall = jnp.exp(-rate[:, None, :] * rows)
    rise = jnp.exp(-rate[:, None, :] * (block - rows))
    fall_block = jnp.exp(-rate * block)
    gc = grad_gated * outer_f
    grad_outer = (grad_gated * gated).astype(BF16)

    g_re, g_im = spectrum(forward, gc)
    corr_local = back(inverse, h_re * g_re + h_im * g_im, h_re * g_im - h_im * g_re)
    lags = back(inverse, u_re * g_re + u_im * g_im, u_re * g_im - u_im * g_re)
    fg = fall * gc[None]
    g_st = jnp.sum(fg, 1)
    g_lag = jnp.sum(fg * rows, 1)
    fl = fall * lags[None]
    sum_a = g_st * x_in + jnp.sum(fl, 1)
    sum_b = g_lag * x_in + g_st * x_lag + jnp.sum(fl * rows, 1)
    sum_skip = jnp.sum(gc * u, 0, keepdims=True)
    mine_g = jnp.concatenate([g_st, sum_a, sum_b, sum_skip], 0)
    theirs_g = swap_core(mine_g)
    later = jnp.where(core == 0, theirs_g[:modes], mine_g[:modes])
    mine_h, theirs_h = my_half(mine_g), my_half(theirs_g)
    early_h = jnp.where(core == 0, mine_h[:modes], theirs_h[:modes])
    total_g = early_h + decay_h * my_half(later)
    sent = jnp.concatenate([total_g, mine_h[modes:] + theirs_h[modes:]], 0).astype(BF16)
    got = of_plane(sent)
    got = got.astype(F32)
    plane_h = jnp.sum(weights(place >= 0, place)[0] * got[:, :modes], 0)
    plane_sums = jnp.sum(got[:, modes:], 0)
    plane_g = jnp.concatenate([plane_h, plane_sums], 0).astype(BF16)
    h_half = jnp.sum(weights(place > zz, place - zz - 1)[0] * got[:, :modes], 0)
    y_h, sums_half = 0.0, plane_sums
    for k in range(1, ny):
        came = shift_y(plane_g, -k).astype(F32)
        w = jnp.exp(-rate_h * float(per_plane * (k - 1)))
        y_h = y_h + jnp.where(yy + k < ny, w * came[:modes], 0.0)
        sums_half = sums_half + came[modes:]
    h_half = h_half + jnp.exp(-rate_h * (per_pair * (nz - 1 - zz)).astype(F32)) * y_h
    final = both_halves(jnp.concatenate([h_half, sums_half], 0))
    h_pair = final[:modes]
    h_in = jnp.where(core == 0, later + fall_block * h_pair, h_pair)
    tot_a, tot_b = final[modes : 2 * modes], final[2 * modes : 3 * modes]
    grad_skip = final[3 * modes]
    grad_residues = norm * tot_a
    grad_decay = rate * residues * (jnp.exp(-2.0 * rate) / norm * tot_a - norm * tot_b)
    corr_in = corr_local + jnp.sum((gain * h_in)[:, None, :] * rise, 0)
    grad_mixed = corr_in + skip_gain[None, :] * gc
    grad_inner = (grad_mixed * value_f).astype(BF16)
    grad_values = (grad_mixed * inner_f).astype(BF16)

    over_z = lax.all_to_all(summed_y, "ctx", 0, 0, tiled=True, axis_index_groups=z_groups)
    grad_weight = jnp.sum(over_z.astype(F32), 0)
    return (
        mixed,
        grad_outer,
        grad_inner,
        grad_values,
        grad_weight,
        grad_skip,
        grad_residues,
        grad_decay,
    )


def solution(mesh):
    placed = (
        P("ctx", "tp"),
        P("ctx", "tp"),
        P("ctx", "tp"),
        P(None, "tp"),
        P(None, "tp"),
        P("tp"),
        P("tp", None),
        P("ctx", "tp"),
    )

    return jax.shard_map(
        body,
        mesh=mesh,
        in_specs=placed,
        out_specs=(
            P("ctx", "tp"),
            P("ctx", "tp"),
            P("ctx", "tp"),
            P("ctx", "tp"),
            P("tp", "ctx"),
            P("tp"),
            P(None, "tp"),
            P(None, "tp"),
        ),
        check_vma=False,
    )
```

```python
import jax
import jax.numpy as jnp
import numpy as np
from jax import lax
from jax.experimental import pallas as pl
from jax.experimental.layout import Layout, with_layout_constraint
from jax.experimental.pallas import tpu as pltpu
from jax.sharding import PartitionSpec as P

F32 = jnp.float32
BF16 = jnp.bfloat16
FINE = lax.Precision.HIGH


def dft_tables(block):
    size = 2 * block
    freqs = np.arange(block + 1)
    rows = np.arange(block)
    angles = 2.0 * np.pi * (freqs[:, None] * rows[None, :] % size) / size
    forward = np.concatenate([np.cos(angles), -np.sin(angles)], axis=0)
    weight = np.where((freqs == 0) | (freqs == block), 1.0, 2.0)[:, None] / size
    inverse = np.concatenate([weight * np.cos(angles), -weight * np.sin(angles)], axis=0).T
    return jnp.asarray(forward, F32), jnp.asarray(inverse, F32)


def spectrum(forward, rows):
    both = jnp.dot(forward, rows, precision=FINE, preferred_element_type=F32)
    half = both.shape[0] // 2
    return both[:half], both[half:]


def back(inverse, real_part, imag_part):
    return jnp.dot(
        inverse, jnp.concatenate([real_part, imag_part], 0), precision=FINE, preferred_element_type=F32
    )


def row_major(a):
    return with_layout_constraint(a, Layout(major_to_minor=tuple(range(a.ndim))))


def in_vmem(count):
    return [pl.BlockSpec(memory_space=pltpu.VMEM)] * count


def weight_part(step, turns, result, result_other, blocks, taken, width):
    count = len(blocks)
    tokens, chans = result.shape
    tiles = blocks[0].shape[1] // (2 * width)

    def kernel(turns_ref, mine_ref, other_ref, *refs):
        block_refs, taken_refs = refs[:count], refs[count : 2 * count]
        out_ref, rows_ref, sem = refs[2 * count :]
        core = turns_ref[0]
        chosen = (turns_ref[1] - step + count) % count
        for k in range(count):

            @pl.when(chosen == k)
            def _():
                for i in range(tiles):
                    at = pl.multiple_of((2 * i + core) * width, width)
                    for half, source in enumerate((block_refs[k], taken_refs[k])):
                        pltpu.make_async_copy(
                            source.at[:, pl.ds(at, width)],
                            rows_ref.at[pl.ds(half * tokens, tokens), pl.ds(i * width, width)],
                            sem,
                        ).start()

        left = jnp.concatenate([mine_ref[...], other_ref[...]], 0).T
        pltpu.make_async_copy(rows_ref, rows_ref, sem).wait()
        part = jnp.dot(left, rows_ref[...], preferred_element_type=F32).astype(BF16)
        for i in range(tiles):
            out_ref[i] = part[:, i * width : (i + 1) * width]

    return pl.pallas_call(
        kernel,
        out_shape=jax.ShapeDtypeStruct((tiles, chans, width), BF16),
        in_specs=[pl.BlockSpec(memory_space=pltpu.SMEM)]
        + in_vmem(2)
        + [pl.BlockSpec(memory_space=pl.ANY)] * (2 * count),
        out_specs=in_vmem(1)[0],
        scratch_shapes=[
            pltpu.VMEM((2 * tokens, tiles * width), BF16),
            pltpu.SemaphoreType.DMA,
        ],
        compiler_params=pltpu.CompilerParams(vmem_limit_bytes=6 * 2**20),
    )(turns, result, result_other, *blocks, *taken)


def projections(turns, result, blocks, weight):
    count = len(blocks)
    tokens, feats = blocks[0].shape
    chans = result.shape[1]

    def kernel(turns_ref, result_ref, *refs):
        block_refs, weight_ref = refs[:count], refs[count]
        grad_ref, piece_refs = refs[count + 1], refs[count + 2 :]
        grad = None
        for j in range(count):
            at = pl.multiple_of((turns_ref[2] + j) % count * feats, feats)
            w = weight_ref[:, pl.ds(at, feats)]
            piece_refs[j][...] = jnp.dot(result_ref[...], w, preferred_element_type=F32).astype(
                BF16
            )
            term = lax.dot_general(
                block_refs[-j % count][...],
                w,
                (((1,), (1,)), ((), ())),
                preferred_element_type=F32,
            )
            grad = term if j == 0 else grad + term
        grad_ref[...] = grad

    return pl.pallas_call(
        kernel,
        out_shape=[jax.ShapeDtypeStruct((tokens, chans), F32)]
        + [jax.ShapeDtypeStruct((tokens, feats), BF16)] * count,
        in_specs=[pl.BlockSpec(memory_space=pltpu.SMEM)] + in_vmem(2 + count),
        out_specs=in_vmem(1 + count),
        compiler_params=pltpu.CompilerParams(vmem_limit_bytes=6 * 2**20),
    )(turns, result, *blocks, weight)


def body(outer_gate, inner_gate, values, residues, log_decay, skip_gain, out_weight, out_grad):
    ctx = lax.axis_size("ctx")
    tps = lax.axis_size("tp")
    dev = lax.axis_index("ctx")
    tp = lax.axis_index("tp")
    block, chans = outer_gate.shape
    modes = residues.shape[0]
    feats = out_grad.shape[1]
    ny = tps
    nz = ctx // (2 * ny)
    core = dev % 2
    pair = dev // 2
    zz = pair % nz
    pairs = ctx // 2
    yy = dev // (2 * nz)
    width = feats // (2 * nz)

    def swap_core(a):
        return lax.ppermute(a, "ctx", [(i, i ^ 1) for i in range(ctx)])

    def shift_tp(a, k):
        return lax.ppermute(a, "tp", [(i, (i + k) % tps) for i in range(tps)])

    def shift_y(a, k):
        per = 2 * nz
        return lax.ppermute(a, "ctx", [(i, (i // per + k) % ny * per + i % per) for i in range(ctx)])

    z_groups = [[i * 2 * nz + j * 2 + k for j in range(nz)] for i in range(ny) for k in range(2)]

    def of_plane(a):
        copies = jnp.broadcast_to(a[None], (nz, *a.shape))
        return lax.all_to_all(copies, "ctx", 0, 0, tiled=True, axis_index_groups=z_groups)

    def of_pairs(a):
        copies = jnp.broadcast_to(a[None], (pairs, *a.shape))
        groups = [[2 * i + j for i in range(pairs)] for j in range(2)]
        return lax.all_to_all(copies, "ctx", 0, 0, tiled=True, axis_index_groups=groups)

    og = [out_grad] + [row_major(shift_tp(out_grad, k)) for k in range(1, tps)]

    u = inner_gate.astype(F32) * values.astype(F32)
    rate = jnp.exp(log_decay)
    rows = jnp.arange(block, dtype=F32)[None, :, None]
    rate3 = rate[:, None, :]
    rise = jnp.exp(-rate3 * (block - rows))
    fall_block = jnp.exp(-rate * block)

    lead = rise * u[None]
    st = jnp.sum(lead, 1)
    st_lag = jnp.sum(lead * (block - rows), 1)
    mine = jnp.concatenate([st, st_lag], 0)
    theirs = swap_core(mine)
    first = jnp.where(core == 0, mine, theirs)
    second = jnp.where(core == 0, theirs, mine)
    half = chans // 2

    def my_half(a):
        return lax.dynamic_slice_in_dim(a, core * half, half, a.ndim - 1)

    def both_halves(a):
        other = swap_core(a)
        return jnp.concatenate(
            [jnp.where(core == 0, a, other), jnp.where(core == 0, other, a)], a.ndim - 1
        )

    rate_h = my_half(rate)
    decay_h = jnp.exp(-rate_h * block)
    f_h, s_h = my_half(first), my_half(second)
    total = decay_h * f_h[:modes] + s_h[:modes]
    total_lag = decay_h * (block * f_h[:modes] + f_h[modes:]) + s_h[modes:]
    to_send = jnp.concatenate([total, total_lag], 0).astype(BF16)
    gathered = of_pairs(to_send).astype(F32)
    place = jnp.arange(nz, dtype=jnp.int32)
    every = jnp.arange(pairs, dtype=jnp.int32)
    per_pair = 2 * block
    per_plane = per_pair * nz

    def weights(which, gap):
        gap = jnp.where(which, gap, 0).astype(F32)[:, None, None] * per_pair
        return jnp.where(which[:, None, None], jnp.exp(-rate_h[None] * gap), 0.0), gap

    w, gap = weights(every < pair, pair - 1 - every)
    base = gathered[:, :modes]
    in_h = jnp.sum(w * base, 0)
    in_lag_h = jnp.sum(w * (gap * base + gathered[:, modes:]), 0)
    incoming = both_halves(jnp.concatenate([in_h, in_lag_h], 0))
    in_pair, in_pair_lag = incoming[:modes], incoming[modes:]
    x_in = jnp.where(core == 0, in_pair, fall_block * in_pair + first[:modes])
    x_lag = jnp.where(
        core == 0, in_pair_lag, fall_block * (in_pair_lag + block * in_pair) + first[modes:]
    )

    outer_gate, inner_gate, values, residues, log_decay, x_in, x_lag = lax.optimization_barrier(
        (outer_gate, inner_gate, values, residues, log_decay, x_in, x_lag)
    )
    rate = jnp.exp(log_decay)
    gain = residues * jnp.sqrt(-jnp.expm1(-2.0 * rate))
    fall = jnp.exp(-rate[:, None, :] * rows)
    outer_f = outer_gate.astype(F32)
    u = inner_gate.astype(F32) * values.astype(F32)

    forward, inverse = dft_tables(block)
    response = jnp.sum(gain[:, None, :] * fall, 0)
    h_re, h_im = spectrum(forward, response)
    u_re, u_im = spectrum(forward, u)
    conv_local = back(inverse, h_re * u_re - h_im * u_im, h_re * u_im + h_im * u_re)
    conv_out = conv_local + jnp.sum((gain * x_in)[:, None, :] * fall, 0)
    gated = conv_out + skip_gain[None, :] * u
    result = row_major((outer_f * gated).astype(BF16))

    turns = jnp.stack([core, (tp - yy) % tps, tp]).astype(jnp.int32)
    taken = [row_major(swap_core(a)) for a in og]
    result_other = swap_core(result)
    y_parts, over_y = [None] * ny, [None] * ny
    for s in (2, 1, 3, 0):
        y_parts[s] = weight_part(s, turns, result, result_other, og, taken, width)
        over_y[s] = shift_y(y_parts[s], s) if s else y_parts[s]
    summed_y = sum(a.astype(F32) for a in over_y).astype(BF16)

    late = lax.optimization_barrier((result, gated, *y_parts))
    result, gated = late[:2]
    grad_gated, *pieces = projections(turns, result, og, out_weight)
    mixed = pieces[0].astype(F32)
    for k in range(1, tps):
        piece = shift_tp(pieces[k], k)
        mixed = mixed + piece.astype(F32)
    mixed = mixed.astype(BF16)

    late = lax.optimization_barrier(
        (outer_gate, inner_gate, values, residues, log_decay, grad_gated, *y_parts)
    )
    outer_gate, inner_gate, values, residues, log_decay, grad_gated = late[:6]
    outer_f = outer_gate.astype(F32)
    inner_f = inner_gate.astype(F32)
    value_f = values.astype(F32)
    u = inner_f * value_f
    rate = jnp.exp(log_decay)
    norm = jnp.sqrt(-jnp.expm1(-2.0 * rate))
    gain = residues * norm
    fall = jnp.exp(-rate[:, None, :] * rows)
    rise = jnp.exp(-rate[:, None, :] * (block - rows))
    fall_block = jnp.exp(-rate * block)
    gc = grad_gated * outer_f
    grad_outer = (grad_gated * gated).astype(BF16)

    g_re, g_im = spectrum(forward, gc)
    corr_local = back(inverse, h_re * g_re + h_im * g_im, h_re * g_im - h_im * g_re)
    lags = back(inverse, u_re * g_re + u_im * g_im, u_re * g_im - u_im * g_re)
    fg = fall * gc[None]
    g_st = jnp.sum(fg, 1)
    g_lag = jnp.sum(fg * rows, 1)
    fl = fall * lags[None]
    sum_a = g_st * x_in + jnp.sum(fl, 1)
    sum_b = g_lag * x_in + g_st * x_lag + jnp.sum(fl * rows, 1)
    sum_skip = jnp.sum(gc * u, 0, keepdims=True)
    mine_g = jnp.concatenate([g_st, sum_a, sum_b, sum_skip], 0)
    theirs_g = swap_core(mine_g)
    later = jnp.where(core == 0, theirs_g[:modes], mine_g[:modes])
    mine_h, theirs_h = my_half(mine_g), my_half(theirs_g)
    early_h = jnp.where(core == 0, mine_h[:modes], theirs_h[:modes])
    total_g = early_h + decay_h * my_half(later)
    sent = jnp.concatenate([total_g, mine_h[modes:] + theirs_h[modes:]], 0).astype(BF16)
    got = of_plane(sent)
    got = got.astype(F32)
    plane_h = jnp.sum(weights(place >= 0, place)[0] * got[:, :modes], 0)
    plane_sums = jnp.sum(got[:, modes:], 0)
    plane_g = jnp.concatenate([plane_h, plane_sums], 0).astype(BF16)
    h_half = jnp.sum(weights(place > zz, place - zz - 1)[0] * got[:, :modes], 0)
    y_h, sums_half = 0.0, plane_sums
    for k in range(1, ny):
        came = shift_y(plane_g, -k).astype(F32)
        w = jnp.exp(-rate_h * float(per_plane * (k - 1)))
        y_h = y_h + jnp.where(yy + k < ny, w * came[:modes], 0.0)
        sums_half = sums_half + came[modes:]
    h_half = h_half + jnp.exp(-rate_h * (per_pair * (nz - 1 - zz)).astype(F32)) * y_h
    final = both_halves(jnp.concatenate([h_half, sums_half], 0))
    h_pair = final[:modes]
    h_in = jnp.where(core == 0, later + fall_block * h_pair, h_pair)
    tot_a, tot_b = final[modes : 2 * modes], final[2 * modes : 3 * modes]
    grad_skip = final[3 * modes]
    grad_residues = norm * tot_a
    grad_decay = rate * residues * (jnp.exp(-2.0 * rate) / norm * tot_a - norm * tot_b)
    corr_in = corr_local + jnp.sum((gain * h_in)[:, None, :] * rise, 0)
    grad_mixed = corr_in + skip_gain[None, :] * gc
    grad_inner = (grad_mixed * value_f).astype(BF16)
    grad_values = (grad_mixed * inner_f).astype(BF16)

    over_z = lax.all_to_all(summed_y, "ctx", 0, 0, tiled=True, axis_index_groups=z_groups)
    grad_weight = jnp.sum(over_z.astype(F32), 0)
    return (
        mixed,
        grad_outer,
        grad_inner,
        grad_values,
        grad_weight,
        grad_skip,
        grad_residues,
        grad_decay,
    )


def solution(mesh):
    placed = (
        P("ctx", "tp"),
        P("ctx", "tp"),
        P("ctx", "tp"),
        P(None, "tp"),
        P(None, "tp"),
        P("tp"),
        P("tp", None),
        P("ctx", "tp"),
    )

    return jax.shard_map(
        body,
        mesh=mesh,
        in_specs=placed,
        out_specs=(
            P("ctx", "tp"),
            P("ctx", "tp"),
            P("ctx", "tp"),
            P("ctx", "tp"),
            P("tp", "ctx"),
            P("tp"),
            P(None, "tp"),
            P(None, "tp"),
        ),
        check_vma=False,
    )
```

```python
import jax
import jax.numpy as jnp
import numpy as np
from jax import lax
from jax.experimental import pallas as pl
from jax.experimental.layout import Layout, with_layout_constraint
from jax.experimental.pallas import tpu as pltpu
from jax.sharding import PartitionSpec as P

F32 = jnp.float32
BF16 = jnp.bfloat16
FINE = lax.Precision.HIGH


def dft_tables(block):
    size = 2 * block
    freqs = np.arange(block + 1)
    rows = np.arange(block)
    angles = 2.0 * np.pi * (freqs[:, None] * rows[None, :] % size) / size
    forward = np.concatenate([np.cos(angles), -np.sin(angles)], axis=0)
    weight = np.where((freqs == 0) | (freqs == block), 1.0, 2.0)[:, None] / size
    inverse = np.concatenate([weight * np.cos(angles), -weight * np.sin(angles)], axis=0).T
    return jnp.asarray(forward, F32), jnp.asarray(inverse, F32)


def spectrum(forward, rows):
    both = jnp.dot(forward, rows, precision=FINE, preferred_element_type=F32)
    half = both.shape[0] // 2
    return both[:half], both[half:]


def back(inverse, real_part, imag_part):
    return jnp.dot(
        inverse, jnp.concatenate([real_part, imag_part], 0), precision=FINE, preferred_element_type=F32
    )


def row_major(a):
    return with_layout_constraint(a, Layout(major_to_minor=tuple(range(a.ndim))))


def in_vmem(count):
    return [pl.BlockSpec(memory_space=pltpu.VMEM)] * count


def weight_parts(turns, result, result_other, blocks, taken, width):
    count = len(blocks)
    tokens, chans = result.shape
    tiles = blocks[0].shape[1] // (2 * width)

    def kernel(turns_ref, *refs):
        mine_ref, other_ref = refs[:2]
        block_refs, taken_refs = refs[2 : 2 + count], refs[2 + count : 2 + 2 * count]
        out_refs = refs[2 + 2 * count : 2 + 3 * count]
        all_ref, part_ref, in_sems, out_sems = refs[2 + 3 * count :]
        core = turns_ref[0]
        for k in range(count):
            for i in range(tiles):
                at = pl.multiple_of((2 * i + core) * width, width)
                lanes = pl.ds(i * width, width)
                for half, source in enumerate((block_refs[k], taken_refs[k])):
                    pltpu.make_async_copy(
                        source.at[:, pl.ds(at, width)],
                        all_ref.at[k, pl.ds(half * tokens, tokens), lanes],
                        in_sems.at[k],
                    ).start()
        left = jnp.concatenate([mine_ref[...], other_ref[...]], 0).T
        for k in range(count):
            pltpu.make_async_copy(all_ref.at[k], all_ref.at[k], in_sems.at[k]).wait()
        for s in range(count):
            part = jnp.dot(
                left, all_ref[(turns_ref[1] - s + count) % count], preferred_element_type=F32
            ).astype(BF16)
            for i in range(tiles):
                part_ref[s, i] = part[:, i * width : (i + 1) * width]
            pltpu.make_async_copy(part_ref.at[s], out_refs[s], out_sems.at[s]).start()
        for s in range(count):
            pltpu.make_async_copy(part_ref.at[s], out_refs[s], out_sems.at[s]).wait()

    return pl.pallas_call(
        kernel,
        out_shape=[jax.ShapeDtypeStruct((tiles, chans, width), BF16)] * count,
        in_specs=[pl.BlockSpec(memory_space=pltpu.SMEM)]
        + in_vmem(2)
        + [pl.BlockSpec(memory_space=pl.ANY)] * (2 * count),
        out_specs=[pl.BlockSpec(memory_space=pl.ANY)] * count,
        scratch_shapes=[
            pltpu.VMEM((count, 2 * tokens, tiles * width), BF16),
            pltpu.VMEM((count, tiles, chans, width), BF16),
            pltpu.SemaphoreType.DMA((count,)),
            pltpu.SemaphoreType.DMA((count,)),
        ],
        compiler_params=pltpu.CompilerParams(vmem_limit_bytes=6 * 2**20),
    )(turns, result, result_other, *blocks, *taken)


def projections(turns, result, blocks, weight):
    count = len(blocks)
    tokens, feats = blocks[0].shape
    chans = result.shape[1]

    def kernel(turns_ref, result_ref, *refs):
        block_refs, weight_ref = refs[:count], refs[count]
        grad_ref, piece_refs = refs[count + 1], refs[count + 2 :]
        grad = None
        for j in range(count):
            at = pl.multiple_of((turns_ref[2] + j) % count * feats, feats)
            w = weight_ref[:, pl.ds(at, feats)]
            piece_refs[j][...] = jnp.dot(result_ref[...], w, preferred_element_type=F32).astype(
                BF16
            )
            term = lax.dot_general(
                block_refs[-j % count][...],
                w,
                (((1,), (1,)), ((), ())),
                preferred_element_type=F32,
            )
            grad = term if j == 0 else grad + term
        grad_ref[...] = grad

    return pl.pallas_call(
        kernel,
        out_shape=[jax.ShapeDtypeStruct((tokens, chans), F32)]
        + [jax.ShapeDtypeStruct((tokens, feats), BF16)] * count,
        in_specs=[pl.BlockSpec(memory_space=pltpu.SMEM)] + in_vmem(2 + count),
        out_specs=in_vmem(1 + count),
        compiler_params=pltpu.CompilerParams(vmem_limit_bytes=6 * 2**20),
    )(turns, result, *blocks, weight)


def first_states(inner_gate, values, log_decay):
    block, chans = inner_gate.shape
    modes = log_decay.shape[0]
    sub = 8

    def kernel(inner_ref, values_ref, decay_ref, out_ref):
        u = inner_ref[...].astype(F32) * values_ref[...].astype(F32)
        row = lax.broadcasted_iota(jnp.int32, (sub, 1), 0).astype(F32)
        groups = block // sub
        for n in range(modes):
            rate = jnp.exp(decay_ref[n : n + 1, :])
            near = jnp.exp(-rate * (sub - row))
            step = jnp.exp(-rate * float(sub))
            base = jnp.zeros((sub, chans), F32)
            lagged = jnp.zeros((sub, chans), F32)
            for b in range(groups):
                base_old = base
                base = u[b * sub : (b + 1) * sub] + step * base_old
                lagged = step * (lagged + float(sub) * base_old)
            st = jnp.sum(near * base, 0, keepdims=True)
            lag = jnp.sum(near * ((sub - row) * base + lagged), 0, keepdims=True)
            out_ref[n : n + 1, :] = st
            out_ref[modes + n : modes + n + 1, :] = lag

    return pl.pallas_call(
        kernel,
        out_shape=jax.ShapeDtypeStruct((2 * modes, chans), F32),
        in_specs=in_vmem(3),
        out_specs=in_vmem(1)[0],
        compiler_params=pltpu.CompilerParams(vmem_limit_bytes=4 * 2**20),
    )(inner_gate, values, log_decay)


def body(outer_gate, inner_gate, values, residues, log_decay, skip_gain, out_weight, out_grad):
    ctx = lax.axis_size("ctx")
    tps = lax.axis_size("tp")
    dev = lax.axis_index("ctx")
    tp = lax.axis_index("tp")
    block, chans = outer_gate.shape
    modes = residues.shape[0]
    feats = out_grad.shape[1]
    ny = tps
    nz = ctx // (2 * ny)
    core = dev % 2
    pair = dev // 2
    zz = pair % nz
    pairs = ctx // 2
    yy = dev // (2 * nz)
    width = feats // (2 * nz)

    def swap_core(a):
        return lax.ppermute(a, "ctx", [(i, i ^ 1) for i in range(ctx)])

    def shift_tp(a, k):
        return lax.ppermute(a, "tp", [(i, (i + k) % tps) for i in range(tps)])

    def shift_y(a, k):
        per = 2 * nz
        return lax.ppermute(a, "ctx", [(i, (i // per + k) % ny * per + i % per) for i in range(ctx)])

    z_groups = [[i * 2 * nz + j * 2 + k for j in range(nz)] for i in range(ny) for k in range(2)]

    def of_plane(a):
        copies = jnp.broadcast_to(a[None], (nz, *a.shape))
        return lax.all_to_all(copies, "ctx", 0, 0, tiled=True, axis_index_groups=z_groups)

    def of_pairs(a):
        copies = jnp.broadcast_to(a[None], (pairs, *a.shape))
        groups = [[2 * i + j for i in range(pairs)] for j in range(2)]
        return lax.all_to_all(copies, "ctx", 0, 0, tiled=True, axis_index_groups=groups)

    og = [out_grad] + [row_major(shift_tp(out_grad, k)) for k in range(1, tps)]

    u = inner_gate.astype(F32) * values.astype(F32)
    rate = jnp.exp(log_decay)
    rows = jnp.arange(block, dtype=F32)[None, :, None]
    rate3 = rate[:, None, :]
    rise = jnp.exp(-rate3 * (block - rows))
    fall_block = jnp.exp(-rate * block)

    mine = first_states(inner_gate, values, log_decay)
    theirs = swap_core(mine)
    first = jnp.where(core == 0, mine, theirs)
    second = jnp.where(core == 0, theirs, mine)
    half = chans // 2

    def my_half(a):
        return lax.dynamic_slice_in_dim(a, core * half, half, a.ndim - 1)

    def both_halves(a):
        other = swap_core(a)
        return jnp.concatenate(
            [jnp.where(core == 0, a, other), jnp.where(core == 0, other, a)], a.ndim - 1
        )

    rate_h = my_half(rate)
    decay_h = jnp.exp(-rate_h * block)
    f_h, s_h = my_half(first), my_half(second)
    total = decay_h * f_h[:modes] + s_h[:modes]
    total_lag = decay_h * (block * f_h[:modes] + f_h[modes:]) + s_h[modes:]
    to_send = jnp.concatenate([total, total_lag], 0).astype(BF16)
    gathered = of_pairs(to_send).astype(F32)
    place = jnp.arange(nz, dtype=jnp.int32)
    every = jnp.arange(pairs, dtype=jnp.int32)
    per_pair = 2 * block
    per_plane = per_pair * nz

    def weights(which, gap):
        gap = jnp.where(which, gap, 0).astype(F32)[:, None, None] * per_pair
        return jnp.where(which[:, None, None], jnp.exp(-rate_h[None] * gap), 0.0), gap

    w, gap = weights(every < pair, pair - 1 - every)
    base = gathered[:, :modes]
    in_h = jnp.sum(w * base, 0)
    in_lag_h = jnp.sum(w * (gap * base + gathered[:, modes:]), 0)
    incoming = both_halves(jnp.concatenate([in_h, in_lag_h], 0))
    in_pair, in_pair_lag = incoming[:modes], incoming[modes:]
    x_in = jnp.where(core == 0, in_pair, fall_block * in_pair + first[:modes])
    x_lag = jnp.where(
        core == 0, in_pair_lag, fall_block * (in_pair_lag + block * in_pair) + first[modes:]
    )

    outer_gate, inner_gate, values, residues, log_decay, x_in, x_lag = lax.optimization_barrier(
        (outer_gate, inner_gate, values, residues, log_decay, x_in, x_lag)
    )
    rate = jnp.exp(log_decay)
    gain = residues * jnp.sqrt(-jnp.expm1(-2.0 * rate))
    fall = jnp.exp(-rate[:, None, :] * rows)
    outer_f = outer_gate.astype(F32)
    u = inner_gate.astype(F32) * values.astype(F32)

    forward, inverse = dft_tables(block)
    response = jnp.sum(gain[:, None, :] * fall, 0)
    h_re, h_im = spectrum(forward, response)
    u_re, u_im = spectrum(forward, u)
    conv_local = back(inverse, h_re * u_re - h_im * u_im, h_re * u_im + h_im * u_re)
    conv_out = conv_local + jnp.sum((gain * x_in)[:, None, :] * fall, 0)
    gated = conv_out + skip_gain[None, :] * u
    result = row_major((outer_f * gated).astype(BF16))

    turns = jnp.stack([core, (tp - yy) % tps, tp]).astype(jnp.int32)
    taken = [row_major(swap_core(a)) for a in og]
    result_other = swap_core(result)
    y_parts = weight_parts(turns, result, result_other, og, taken, width)
    over_y = [y_parts[0]] + [shift_y(y_parts[s], s) for s in range(1, ny)]
    summed_y = sum(a.astype(F32) for a in over_y).astype(BF16)

    late = lax.optimization_barrier((result, gated, *y_parts))
    result, gated = late[:2]
    grad_gated, *pieces = projections(turns, result, og, out_weight)
    mixed = pieces[0].astype(F32)
    for k in range(1, tps):
        piece = shift_tp(pieces[k], k)
        mixed = mixed + piece.astype(F32)
    mixed = mixed.astype(BF16)

    late = lax.optimization_barrier(
        (outer_gate, inner_gate, values, residues, log_decay, grad_gated, *y_parts)
    )
    outer_gate, inner_gate, values, residues, log_decay, grad_gated = late[:6]
    outer_f = outer_gate.astype(F32)
    inner_f = inner_gate.astype(F32)
    value_f = values.astype(F32)
    u = inner_f * value_f
    rate = jnp.exp(log_decay)
    norm = jnp.sqrt(-jnp.expm1(-2.0 * rate))
    gain = residues * norm
    fall = jnp.exp(-rate[:, None, :] * rows)
    rise = jnp.exp(-rate[:, None, :] * (block - rows))
    fall_block = jnp.exp(-rate * block)
    gc = grad_gated * outer_f
    grad_outer = (grad_gated * gated).astype(BF16)

    g_re, g_im = spectrum(forward, gc)
    corr_local = back(inverse, h_re * g_re + h_im * g_im, h_re * g_im - h_im * g_re)
    lags = back(inverse, u_re * g_re + u_im * g_im, u_re * g_im - u_im * g_re)
    fg = fall * gc[None]
    g_st = jnp.sum(fg, 1)
    g_lag = jnp.sum(fg * rows, 1)
    fl = fall * lags[None]
    sum_a = g_st * x_in + jnp.sum(fl, 1)
    sum_b = g_lag * x_in + g_st * x_lag + jnp.sum(fl * rows, 1)
    sum_skip = jnp.sum(gc * u, 0, keepdims=True)
    mine_g = jnp.concatenate([g_st, sum_a, sum_b, sum_skip], 0)
    theirs_g = swap_core(mine_g)
    later = jnp.where(core == 0, theirs_g[:modes], mine_g[:modes])
    mine_h, theirs_h = my_half(mine_g), my_half(theirs_g)
    early_h = jnp.where(core == 0, mine_h[:modes], theirs_h[:modes])
    total_g = early_h + decay_h * my_half(later)
    sent = jnp.concatenate([total_g, mine_h[modes:] + theirs_h[modes:]], 0).astype(BF16)
    got = of_plane(sent)
    got = got.astype(F32)
    plane_h = jnp.sum(weights(place >= 0, place)[0] * got[:, :modes], 0)
    plane_sums = jnp.sum(got[:, modes:], 0)
    plane_g = jnp.concatenate([plane_h, plane_sums], 0).astype(BF16)
    h_half = jnp.sum(weights(place > zz, place - zz - 1)[0] * got[:, :modes], 0)
    y_h, sums_half = 0.0, plane_sums
    for k in range(1, ny):
        came = shift_y(plane_g, -k).astype(F32)
        w = jnp.exp(-rate_h * float(per_plane * (k - 1)))
        y_h = y_h + jnp.where(yy + k < ny, w * came[:modes], 0.0)
        sums_half = sums_half + came[modes:]
    h_half = h_half + jnp.exp(-rate_h * (per_pair * (nz - 1 - zz)).astype(F32)) * y_h
    final = both_halves(jnp.concatenate([h_half, sums_half], 0))
    h_pair = final[:modes]
    h_in = jnp.where(core == 0, later + fall_block * h_pair, h_pair)
    tot_a, tot_b = final[modes : 2 * modes], final[2 * modes : 3 * modes]
    grad_skip = final[3 * modes]
    grad_residues = norm * tot_a
    grad_decay = rate * residues * (jnp.exp(-2.0 * rate) / norm * tot_a - norm * tot_b)
    corr_in = corr_local + jnp.sum((gain * h_in)[:, None, :] * rise, 0)
    grad_mixed = corr_in + skip_gain[None, :] * gc
    grad_inner = (grad_mixed * value_f).astype(BF16)
    grad_values = (grad_mixed * inner_f).astype(BF16)

    over_z = lax.all_to_all(summed_y, "ctx", 0, 0, tiled=True, axis_index_groups=z_groups)
    grad_weight = jnp.sum(over_z.astype(F32), 0)
    return (
        mixed,
        grad_outer,
        grad_inner,
        grad_values,
        grad_weight,
        grad_skip,
        grad_residues,
        grad_decay,
    )


def solution(mesh):
    placed = (
        P("ctx", "tp"),
        P("ctx", "tp"),
        P("ctx", "tp"),
        P(None, "tp"),
        P(None, "tp"),
        P("tp"),
        P("tp", None),
        P("ctx", "tp"),
    )

    return jax.shard_map(
        body,
        mesh=mesh,
        in_specs=placed,
        out_specs=(
            P("ctx", "tp"),
            P("ctx", "tp"),
            P("ctx", "tp"),
            P("ctx", "tp"),
            P("tp", "ctx"),
            P("tp"),
            P(None, "tp"),
            P(None, "tp"),
        ),
        check_vma=False,
    )
```

```python
import jax
import jax.numpy as jnp
import numpy as np
from jax import lax
from jax.experimental import pallas as pl
from jax.experimental.layout import Layout, with_layout_constraint
from jax.experimental.pallas import tpu as pltpu
from jax.sharding import PartitionSpec as P

F32 = jnp.float32
BF16 = jnp.bfloat16
FINE = lax.Precision.HIGH


def dft_tables(block):
    size = 2 * block
    freqs = np.arange(block + 1)
    rows = np.arange(block)
    angles = 2.0 * np.pi * (freqs[:, None] * rows[None, :] % size) / size
    forward = np.concatenate([np.cos(angles), -np.sin(angles)], axis=0)
    weight = np.where((freqs == 0) | (freqs == block), 1.0, 2.0)[:, None] / size
    inverse = np.concatenate([weight * np.cos(angles), -weight * np.sin(angles)], axis=0).T
    return jnp.asarray(forward, F32), jnp.asarray(inverse, F32)


def spectrum(forward, rows):
    both = jnp.dot(forward, rows, precision=FINE, preferred_element_type=F32)
    half = both.shape[0] // 2
    return both[:half], both[half:]


def back(inverse, real_part, imag_part):
    return jnp.dot(
        inverse, jnp.concatenate([real_part, imag_part], 0), precision=FINE, preferred_element_type=F32
    )


def row_major(a):
    return with_layout_constraint(a, Layout(major_to_minor=tuple(range(a.ndim))))


def in_vmem(count):
    return [pl.BlockSpec(memory_space=pltpu.VMEM)] * count


def weight_parts(turns, result, result_other, blocks, taken, width):
    count = len(blocks)
    tokens, chans = result.shape
    tiles = blocks[0].shape[1] // (2 * width)

    def kernel(turns_ref, *refs):
        mine_ref, other_ref = refs[:2]
        block_refs, taken_refs = refs[2 : 2 + count], refs[2 + count : 2 + 2 * count]
        out_refs = refs[2 + 2 * count : 2 + 3 * count]
        all_ref, part_ref, in_sems, out_sems = refs[2 + 3 * count :]
        core = turns_ref[0]
        for k in range(count):
            for i in range(tiles):
                at = pl.multiple_of((2 * i + core) * width, width)
                lanes = pl.ds(i * width, width)
                for half, source in enumerate((block_refs[k], taken_refs[k])):
                    pltpu.make_async_copy(
                        source.at[:, pl.ds(at, width)],
                        all_ref.at[k, pl.ds(half * tokens, tokens), lanes],
                        in_sems.at[k],
                    ).start()
        left = jnp.concatenate([mine_ref[...], other_ref[...]], 0).T
        for k in range(count):
            pltpu.make_async_copy(all_ref.at[k], all_ref.at[k], in_sems.at[k]).wait()
        for s in range(count):
            part = jnp.dot(
                left, all_ref[(turns_ref[1] - s + count) % count], preferred_element_type=F32
            ).astype(BF16)
            for i in range(tiles):
                part_ref[s, i] = part[:, i * width : (i + 1) * width]
            pltpu.make_async_copy(part_ref.at[s], out_refs[s], out_sems.at[s]).start()
        for s in range(count):
            pltpu.make_async_copy(part_ref.at[s], out_refs[s], out_sems.at[s]).wait()

    return pl.pallas_call(
        kernel,
        out_shape=[jax.ShapeDtypeStruct((tiles, chans, width), BF16)] * count,
        in_specs=[pl.BlockSpec(memory_space=pltpu.SMEM)]
        + in_vmem(2)
        + [pl.BlockSpec(memory_space=pl.ANY)] * (2 * count),
        out_specs=[pl.BlockSpec(memory_space=pl.ANY)] * count,
        scratch_shapes=[
            pltpu.VMEM((count, 2 * tokens, tiles * width), BF16),
            pltpu.VMEM((count, tiles, chans, width), BF16),
            pltpu.SemaphoreType.DMA((count,)),
            pltpu.SemaphoreType.DMA((count,)),
        ],
        compiler_params=pltpu.CompilerParams(vmem_limit_bytes=6 * 2**20),
    )(turns, result, result_other, *blocks, *taken)


def projections(turns, result, blocks, weight):
    count = len(blocks)
    tokens, feats = blocks[0].shape
    chans = result.shape[1]

    def kernel(turns_ref, result_ref, *refs):
        block_refs, weight_ref = refs[:count], refs[count]
        grad_ref, piece_refs = refs[count + 1], refs[count + 2 :]
        grad = None
        for j in range(count):
            at = pl.multiple_of((turns_ref[2] + j) % count * feats, feats)
            w = weight_ref[:, pl.ds(at, feats)]
            piece_refs[j][...] = jnp.dot(result_ref[...], w, preferred_element_type=F32).astype(
                BF16
            )
            term = lax.dot_general(
                block_refs[-j % count][...],
                w,
                (((1,), (1,)), ((), ())),
                preferred_element_type=F32,
            )
            grad = term if j == 0 else grad + term
        grad_ref[...] = grad

    return pl.pallas_call(
        kernel,
        out_shape=[jax.ShapeDtypeStruct((tokens, chans), F32)]
        + [jax.ShapeDtypeStruct((tokens, feats), BF16)] * count,
        in_specs=[pl.BlockSpec(memory_space=pltpu.SMEM)] + in_vmem(2 + count),
        out_specs=in_vmem(1 + count),
        compiler_params=pltpu.CompilerParams(vmem_limit_bytes=6 * 2**20),
    )(turns, result, *blocks, weight)


def first_states(inner_gate, values, log_decay):
    block, chans = inner_gate.shape
    modes = log_decay.shape[0]
    sub = 8

    def kernel(inner_ref, values_ref, decay_ref, out_ref):
        u = inner_ref[...].astype(F32) * values_ref[...].astype(F32)
        row = lax.broadcasted_iota(jnp.int32, (sub, 1), 0).astype(F32)
        groups = block // sub
        for n in range(modes):
            rate = jnp.exp(decay_ref[n : n + 1, :])
            near = jnp.exp(-rate * (sub - row))
            step = jnp.exp(-rate * float(sub))
            base = jnp.zeros((sub, chans), F32)
            lagged = jnp.zeros((sub, chans), F32)
            for b in range(groups):
                base_old = base
                base = u[b * sub : (b + 1) * sub] + step * base_old
                lagged = step * (lagged + float(sub) * base_old)
            st = jnp.sum(near * base, 0, keepdims=True)
            lag = jnp.sum(near * ((sub - row) * base + lagged), 0, keepdims=True)
            out_ref[n : n + 1, :] = st
            out_ref[modes + n : modes + n + 1, :] = lag

    def whole(shape):
        return pl.BlockSpec(shape, lambda i: (0, 0))

    return pl.pallas_call(
        kernel,
        out_shape=jax.ShapeDtypeStruct((2 * modes, chans), F32),
        grid=(1,),
        in_specs=[whole((block, chans)), whole((block, chans)), whole((modes, chans))],
        out_specs=whole((2 * modes, chans)),
        compiler_params=pltpu.CompilerParams(vmem_limit_bytes=60 * 2**20),
    )(inner_gate, values, log_decay)


def body(outer_gate, inner_gate, values, residues, log_decay, skip_gain, out_weight, out_grad):
    ctx = lax.axis_size("ctx")
    tps = lax.axis_size("tp")
    dev = lax.axis_index("ctx")
    tp = lax.axis_index("tp")
    block, chans = outer_gate.shape
    modes = residues.shape[0]
    feats = out_grad.shape[1]
    ny = tps
    nz = ctx // (2 * ny)
    core = dev % 2
    pair = dev // 2
    zz = pair % nz
    pairs = ctx // 2
    yy = dev // (2 * nz)
    width = feats // (2 * nz)

    def swap_core(a):
        return lax.ppermute(a, "ctx", [(i, i ^ 1) for i in range(ctx)])

    def shift_tp(a, k):
        return lax.ppermute(a, "tp", [(i, (i + k) % tps) for i in range(tps)])

    def shift_y(a, k):
        per = 2 * nz
        return lax.ppermute(a, "ctx", [(i, (i // per + k) % ny * per + i % per) for i in range(ctx)])

    z_groups = [[i * 2 * nz + j * 2 + k for j in range(nz)] for i in range(ny) for k in range(2)]

    def of_plane(a):
        copies = jnp.broadcast_to(a[None], (nz, *a.shape))
        return lax.all_to_all(copies, "ctx", 0, 0, tiled=True, axis_index_groups=z_groups)

    def of_pairs(a):
        copies = jnp.broadcast_to(a[None], (pairs, *a.shape))
        groups = [[2 * i + j for i in range(pairs)] for j in range(2)]
        return lax.all_to_all(copies, "ctx", 0, 0, tiled=True, axis_index_groups=groups)

    og = [out_grad] + [row_major(shift_tp(out_grad, k)) for k in range(1, tps)]

    u = inner_gate.astype(F32) * values.astype(F32)
    rate = jnp.exp(log_decay)
    rows = jnp.arange(block, dtype=F32)[None, :, None]
    rate3 = rate[:, None, :]
    rise = jnp.exp(-rate3 * (block - rows))
    fall_block = jnp.exp(-rate * block)

    mine = first_states(inner_gate, values, log_decay)
    theirs = swap_core(mine)
    first = jnp.where(core == 0, mine, theirs)
    second = jnp.where(core == 0, theirs, mine)
    half = chans // 2

    def my_half(a):
        return lax.dynamic_slice_in_dim(a, core * half, half, a.ndim - 1)

    def both_halves(a):
        other = swap_core(a)
        return jnp.concatenate(
            [jnp.where(core == 0, a, other), jnp.where(core == 0, other, a)], a.ndim - 1
        )

    rate_h = my_half(rate)
    decay_h = jnp.exp(-rate_h * block)
    f_h, s_h = my_half(first), my_half(second)
    total = decay_h * f_h[:modes] + s_h[:modes]
    total_lag = decay_h * (block * f_h[:modes] + f_h[modes:]) + s_h[modes:]
    to_send = jnp.concatenate([total, total_lag], 0).astype(BF16)
    gathered = of_pairs(to_send).astype(F32)
    place = jnp.arange(nz, dtype=jnp.int32)
    every = jnp.arange(pairs, dtype=jnp.int32)
    per_pair = 2 * block
    per_plane = per_pair * nz

    def weights(which, gap):
        gap = jnp.where(which, gap, 0).astype(F32)[:, None, None] * per_pair
        return jnp.where(which[:, None, None], jnp.exp(-rate_h[None] * gap), 0.0), gap

    w, gap = weights(every < pair, pair - 1 - every)
    base = gathered[:, :modes]
    in_h = jnp.sum(w * base, 0)
    in_lag_h = jnp.sum(w * (gap * base + gathered[:, modes:]), 0)
    incoming = both_halves(jnp.concatenate([in_h, in_lag_h], 0))
    in_pair, in_pair_lag = incoming[:modes], incoming[modes:]
    x_in = jnp.where(core == 0, in_pair, fall_block * in_pair + first[:modes])
    x_lag = jnp.where(
        core == 0, in_pair_lag, fall_block * (in_pair_lag + block * in_pair) + first[modes:]
    )

    outer_gate, inner_gate, values, residues, log_decay, x_in, x_lag = lax.optimization_barrier(
        (outer_gate, inner_gate, values, residues, log_decay, x_in, x_lag)
    )
    rate = jnp.exp(log_decay)
    gain = residues * jnp.sqrt(-jnp.expm1(-2.0 * rate))
    fall = jnp.exp(-rate[:, None, :] * rows)
    outer_f = outer_gate.astype(F32)
    u = inner_gate.astype(F32) * values.astype(F32)

    forward, inverse = dft_tables(block)
    response = jnp.sum(gain[:, None, :] * fall, 0)
    h_re, h_im = spectrum(forward, response)
    u_re, u_im = spectrum(forward, u)
    conv_local = back(inverse, h_re * u_re - h_im * u_im, h_re * u_im + h_im * u_re)
    conv_out = conv_local + jnp.sum((gain * x_in)[:, None, :] * fall, 0)
    gated = conv_out + skip_gain[None, :] * u
    result = row_major((outer_f * gated).astype(BF16))

    turns = jnp.stack([core, (tp - yy) % tps, tp]).astype(jnp.int32)
    taken = [row_major(swap_core(a)) for a in og]
    result_other = swap_core(result)
    y_parts = weight_parts(turns, result, result_other, og, taken, width)
    over_y = [y_parts[0]] + [shift_y(y_parts[s], s) for s in range(1, ny)]
    summed_y = sum(a.astype(F32) for a in over_y).astype(BF16)

    late = lax.optimization_barrier((result, gated, *y_parts))
    result, gated = late[:2]
    grad_gated, *pieces = projections(turns, result, og, out_weight)
    mixed = pieces[0].astype(F32)
    for k in range(1, tps):
        piece = shift_tp(pieces[k], k)
        mixed = mixed + piece.astype(F32)
    mixed = mixed.astype(BF16)

    late = lax.optimization_barrier(
        (outer_gate, inner_gate, values, residues, log_decay, grad_gated, *y_parts)
    )
    outer_gate, inner_gate, values, residues, log_decay, grad_gated = late[:6]
    outer_f = outer_gate.astype(F32)
    inner_f = inner_gate.astype(F32)
    value_f = values.astype(F32)
    u = inner_f * value_f
    rate = jnp.exp(log_decay)
    norm = jnp.sqrt(-jnp.expm1(-2.0 * rate))
    gain = residues * norm
    fall = jnp.exp(-rate[:, None, :] * rows)
    rise = jnp.exp(-rate[:, None, :] * (block - rows))
    fall_block = jnp.exp(-rate * block)
    gc = grad_gated * outer_f
    grad_outer = (grad_gated * gated).astype(BF16)

    g_re, g_im = spectrum(forward, gc)
    corr_local = back(inverse, h_re * g_re + h_im * g_im, h_re * g_im - h_im * g_re)
    lags = back(inverse, u_re * g_re + u_im * g_im, u_re * g_im - u_im * g_re)
    fg = fall * gc[None]
    g_st = jnp.sum(fg, 1)
    g_lag = jnp.sum(fg * rows, 1)
    fl = fall * lags[None]
    sum_a = g_st * x_in + jnp.sum(fl, 1)
    sum_b = g_lag * x_in + g_st * x_lag + jnp.sum(fl * rows, 1)
    sum_skip = jnp.sum(gc * u, 0, keepdims=True)
    mine_g = jnp.concatenate([g_st, sum_a, sum_b, sum_skip], 0)
    theirs_g = swap_core(mine_g)
    later = jnp.where(core == 0, theirs_g[:modes], mine_g[:modes])
    mine_h, theirs_h = my_half(mine_g), my_half(theirs_g)
    early_h = jnp.where(core == 0, mine_h[:modes], theirs_h[:modes])
    total_g = early_h + decay_h * my_half(later)
    sent = jnp.concatenate([total_g, mine_h[modes:] + theirs_h[modes:]], 0).astype(BF16)
    got = of_plane(sent)
    got = got.astype(F32)
    plane_h = jnp.sum(weights(place >= 0, place)[0] * got[:, :modes], 0)
    plane_sums = jnp.sum(got[:, modes:], 0)
    plane_g = jnp.concatenate([plane_h, plane_sums], 0).astype(BF16)
    h_half = jnp.sum(weights(place > zz, place - zz - 1)[0] * got[:, :modes], 0)
    y_h, sums_half = 0.0, plane_sums
    for k in range(1, ny):
        came = shift_y(plane_g, -k).astype(F32)
        w = jnp.exp(-rate_h * float(per_plane * (k - 1)))
        y_h = y_h + jnp.where(yy + k < ny, w * came[:modes], 0.0)
        sums_half = sums_half + came[modes:]
    h_half = h_half + jnp.exp(-rate_h * (per_pair * (nz - 1 - zz)).astype(F32)) * y_h
    final = both_halves(jnp.concatenate([h_half, sums_half], 0))
    h_pair = final[:modes]
    h_in = jnp.where(core == 0, later + fall_block * h_pair, h_pair)
    tot_a, tot_b = final[modes : 2 * modes], final[2 * modes : 3 * modes]
    grad_skip = final[3 * modes]
    grad_residues = norm * tot_a
    grad_decay = rate * residues * (jnp.exp(-2.0 * rate) / norm * tot_a - norm * tot_b)
    corr_in = corr_local + jnp.sum((gain * h_in)[:, None, :] * rise, 0)
    grad_mixed = corr_in + skip_gain[None, :] * gc
    grad_inner = (grad_mixed * value_f).astype(BF16)
    grad_values = (grad_mixed * inner_f).astype(BF16)

    over_z = lax.all_to_all(summed_y, "ctx", 0, 0, tiled=True, axis_index_groups=z_groups)
    grad_weight = jnp.sum(over_z.astype(F32), 0)
    return (
        mixed,
        grad_outer,
        grad_inner,
        grad_values,
        grad_weight,
        grad_skip,
        grad_residues,
        grad_decay,
    )


def solution(mesh):
    placed = (
        P("ctx", "tp"),
        P("ctx", "tp"),
        P("ctx", "tp"),
        P(None, "tp"),
        P(None, "tp"),
        P("tp"),
        P("tp", None),
        P("ctx", "tp"),
    )

    return jax.shard_map(
        body,
        mesh=mesh,
        in_specs=placed,
        out_specs=(
            P("ctx", "tp"),
            P("ctx", "tp"),
            P("ctx", "tp"),
            P("ctx", "tp"),
            P("tp", "ctx"),
            P("tp"),
            P(None, "tp"),
            P(None, "tp"),
        ),
        check_vma=False,
    )
```
